32 devices in a mesh: fsdp: 8 (over z, x), replica: 4 (over y, core).
Axes of the slice: x: 2, y: 2, z: 4, core: 2. Of those that a mesh axis runs over, the one named last changes fastest.
Arguments:
- layer_input: bfloat16 [32, 1024, 768], P(('fsdp', 'replica')), may hold values from -6 to 6
- cotangent: bfloat16 [32, 1024, 768], P(('fsdp', 'replica')), may hold values from -6 to 6
- segment_ids: int32 [32, 1024], P(('fsdp', 'replica')), may hold values from 0 to 4, as said below
- pad_mask: int32 [32, 1024], P(('fsdp', 'replica')), may hold values from 0 to 1, as said below
- ln1_gain: bfloat16 [768], P('fsdp'), may hold values from 0.5 to 1.5
- ln1_bias: bfloat16 [768], P('fsdp'), may hold values from -1.1953125 to 1.1953125
- w_qkv: bfloat16 [768, 2304], P('fsdp'), may hold values from -0.21875 to 0.21875
- b_qkv: bfloat16 [2304], P('fsdp'), may hold values from -1.1953125 to 1.1953125
- w_out: bfloat16 [768, 768], P('fsdp'), may hold values from -1.25 to 1.25
- b_out: bfloat16 [768], P('fsdp'), may hold values from -1.1953125 to 1.1953125
- ln2_gain: bfloat16 [768], P('fsdp'), may hold values from 0.5 to 1.5
- ln2_bias: bfloat16 [768], P('fsdp'), may hold values from -1.1953125 to 1.1953125
- w_up: bfloat16 [768, 3072], P('fsdp'), may hold values from -0.21875 to 0.21875
- b_up: bfloat16 [3072], P('fsdp'), may hold values from -1.1953125 to 1.1953125
- w_down: bfloat16 [3072, 768], P('fsdp'), may hold values from -0.109375 to 0.109375
- b_down: bfloat16 [768], P('fsdp'), may hold values from -1.1953125 to 1.1953125
Outputs:
- layer_out: bfloat16 [32, 1024, 768], P(('fsdp', 'replica'))
- input_grad: bfloat16 [32, 1024, 768], P(('fsdp', 'replica'))
- grad_ln1_gain: float32 [768], P('fsdp')
- grad_ln1_bias: float32 [768], P('fsdp')
- grad_w_qkv: float32 [768, 2304], P('fsdp')
- grad_b_qkv: float32 [2304], P('fsdp')
- grad_w_out: float32 [768, 768], P('fsdp')
- grad_b_out: float32 [768], P('fsdp')
- grad_ln2_gain: float32 [768], P('fsdp')
- grad_ln2_bias: float32 [768], P('fsdp')
- grad_w_up: float32 [768, 3072], P('fsdp')
- grad_b_up: float32 [3072], P('fsdp')
- grad_w_down: float32 [3072, 768], P('fsdp')
- grad_b_down: float32 [768], P('fsdp')
The draws below stay inside these ranges and needn't reach their ends.
Inputs may be any that keep to these rules, and one draw needn't show every extreme that they name: `segment_ids`: each row packs 4 genes numbered 0 to 3 in order from its start, each of 128 to 256 codons, never falling along a row, and 4 on the padded tail; in every row one gene has exactly 256 codons and another exactly 128. `pad_mask`: 1 exactly where segment_ids is under 4; every row ends in at least 128 padded codons.
All inputs are finite; a program needn't handle non-finite values.
Results may differ from the reference program's by a relative error of at most 0.014.
Values may be sent and summed in bfloat16 or wider, within the bound.
No kernel may reach another device: no remote copies, remote signals or barrier semaphores. Data moves between devices by JAX's collectives and lax.ppermute only.
A program may use at most 320 MiB of HBM per device.

```python
import math
import jax
import jax.numpy as jnp
from jax import lax

D = 768
HEADS = 12
HEAD_DIM = 64
FF = 3072
ROW_LEN = 1024
GENES = 4
ROWS = 32


def gene_plan(key):
    base_key = jax.random.fold_in(key, 11)
    length_key, first_key, second_key = jax.random.split(base_key, 3)
    shortest = ROW_LEN // 8
    longest = ROW_LEN // 4
    lengths = jax.random.randint(length_key, (ROWS, GENES), shortest, longest + 1, dtype=jnp.int32)
    first_slot = jax.random.randint(first_key, (ROWS, 1), 0, GENES, dtype=jnp.int32)
    second_slot = (first_slot + jax.random.randint(second_key, (ROWS, 1), 1, GENES, dtype=jnp.int32)) % GENES
    slot_ids = jnp.arange(GENES, dtype=jnp.int32)[None, :]
    lengths = jnp.where(slot_ids == first_slot, longest, lengths)
    lengths = jnp.where(slot_ids == second_slot, shortest, lengths)
    return lengths.astype(jnp.int32)


def gene_limits(key):
    return jnp.cumsum(gene_plan(key), -1).astype(jnp.int32)


def draw_segment_ids(key, part):
    gene_end = gene_limits(key)
    codon_ids = jnp.arange(ROW_LEN, dtype=jnp.int32)
    passed = (codon_ids[None, :, None] >= gene_end[:, None, :]).astype(jnp.int32)
    return jnp.sum(passed, -1).astype(jnp.int32)


def draw_pad_mask(key, part):
    gene_end = gene_limits(key)
    codon_ids = jnp.arange(ROW_LEN, dtype=jnp.int32)
    return (codon_ids[None, :] < gene_end[:, -1:]).astype(jnp.int32)


def levels(rng, shape, pieces, low, largest):
    loudness = 1.0
    for dim, shards_of in pieces:
        heights = jax.random.uniform(jax.random.fold_in(jax.random.fold_in(rng, 6), dim), (shards_of,), jnp.float32, low / len(pieces), largest / len(pieces))
        loudness = loudness * jnp.repeat(jnp.exp(heights), shape[dim] // shards_of).reshape((-1,) + (1,) * (len(shape) - 1 - dim))
    return loudness


def scatter_about(stream_key, dims, scale, reach, cuts=(), kind=jnp.bfloat16):
    level = levels(stream_key, dims, cuts, -0.22, 0.18) if cuts else 1.0
    drawn = jax.random.normal(stream_key, dims, jnp.float32) * scale * level
    return jnp.minimum(jnp.maximum(drawn, -reach), reach).astype(kind)


def setup_inputs(seed: int = 0) -> dict:
    splits = jax.random.split(jax.random.key(seed), 17)
    layer_input = scatter_about(splits[0], (ROWS, ROW_LEN, D), 1.0, 6.0, ((0, 32),))
    cotangent = scatter_about(splits[1], (ROWS, ROW_LEN, D), 1.0, 6.0, ((0, 32),))
    segment_ids = draw_segment_ids(jax.random.fold_in(splits[16], 71), 0)
    pad_mask = draw_pad_mask(jax.random.fold_in(splits[16], 71), 0)
    ln1_gain = jnp.clip(1.0 + 0.1 * jax.random.normal(splits[4], (D,), jnp.float32), 0.5, 1.5).astype(jnp.bfloat16)
    ln1_bias = scatter_about(splits[5], (D,), 0.2, 1.1953125, ((0, 8),))
    w_qkv = scatter_about(splits[6], (D, 3 * D), D ** -0.5, 0.21875, ((0, 8),))
    b_qkv = scatter_about(splits[7], (3 * D,), 0.2, 1.1953125, ((0, 8),))
    w_out = scatter_about(splits[8], (D, D), (D // 32) ** -0.5, 1.25, ((0, 8),))
    b_out = scatter_about(splits[9], (D,), 0.2, 1.1953125, ((0, 8),))
    ln2_gain = jnp.clip(1.0 + 0.1 * jax.random.normal(splits[10], (D,), jnp.float32), 0.5, 1.5).astype(jnp.bfloat16)
    ln2_bias = scatter_about(splits[11], (D,), 0.2, 1.1953125, ((0, 8),))
    w_up = scatter_about(splits[12], (D, FF), D ** -0.5, 0.21875, ((0, 8),))
    b_up = scatter_about(splits[13], (FF,), 0.2, 1.1953125, ((0, 8),))
    w_down = scatter_about(splits[14], (FF, D), FF ** -0.5, 0.109375, ((0, 8),))
    b_down = scatter_about(splits[15], (D,), 0.2, 1.1953125, ((0, 8),))
    return dict(layer_input=layer_input, cotangent=cotangent, segment_ids=segment_ids, pad_mask=pad_mask, ln1_gain=ln1_gain, ln1_bias=ln1_bias, w_qkv=w_qkv, b_qkv=b_qkv, w_out=w_out, b_out=b_out, ln2_gain=ln2_gain, ln2_bias=ln2_bias, w_up=w_up, b_up=b_up, w_down=w_down, b_down=b_down)


EPSILON = 1e-05
NEG_FILL = -1000000000.0
HIGHEST = lax.Precision.HIGHEST

@jax.custom_vjp
def low(v):
    return lax.optimization_barrier(v.astype(jnp.bfloat16)).astype(jnp.float32)

@jax.custom_vjp
def low_back(v):
    return v

def low_keep(v):
    return (low(v), None)

def low_pass(kept, grad):
    return (grad,)

def back_keep(v):
    return (v, None)

def back_low(kept, grad):
    return (low(grad),)
low.defvjp(low_keep, low_pass)
low_back.defvjp(back_keep, back_low)

def layer_norm(inputs, gain_vector, bias_vector):
    centered = inputs - lax.optimization_barrier(jnp.mean(inputs, -1, keepdims=True))
    variance = lax.optimization_barrier(jnp.mean(centered * centered, -1, keepdims=True))
    return centered * lax.rsqrt(variance + EPSILON) * gain_vector + bias_vector

def rotate(tensor, cosine_table, sine_table):
    half_dim = tensor.shape[-1] // 2
    first_half = tensor[..., :half_dim]
    second_half = tensor[..., half_dim:]
    return jnp.concatenate([first_half * cosine_table - second_half * sine_table, second_half * cosine_table + first_half * sine_table], -1)

def exact_gelu(inputs):
    return jax.nn.gelu(inputs, approximate=False)

def rotary_tables(positions):
    frequency = jnp.power(10000.0, jnp.arange(HEAD_DIM // 2, dtype=jnp.float32) * (-2.0 / HEAD_DIM))
    angles = positions.astype(jnp.float32)[..., None] * frequency
    return (jnp.cos(angles)[..., None, :], jnp.sin(angles)[..., None, :])

def gene_positions(segments):
    slot_ids = jnp.arange(GENES + 1, dtype=jnp.int32)
    slot_hits = segments[..., :, None] == slot_ids
    counts = lax.optimization_barrier(jnp.sum(slot_hits.astype(jnp.int32), -2)).astype(jnp.int32)
    starts = (jnp.cumsum(counts, -1) - counts).astype(jnp.int32)
    gene_start = lax.optimization_barrier(jnp.sum(jnp.where(slot_hits, starts[..., None, :], 0), -1)).astype(jnp.int32)
    return (jnp.arange(segments.shape[-1], dtype=jnp.int32) - gene_start).astype(jnp.int32)

def allowed_pairs(segments, valid_codons):
    same_gene = (segments[..., :, None] == segments[..., None, :]) & (valid_codons[..., :, None] > 0) & (valid_codons[..., None, :] > 0)
    codon_ids = jnp.arange(segments.shape[-1], dtype=jnp.int32)
    return same_gene | (codon_ids[:, None] == codon_ids[None, :])

def forward(inputs, params, allowed, cosine_table, sine_table):
    ln1_gain, ln1_bias, w_qkv, b_qkv, w_out, b_out, ln2_gain, ln2_bias, w_up, b_up, w_down, b_down = params
    row_count, length, model_width = inputs.shape
    score_scale = 1.0 / math.sqrt(HEAD_DIM)
    normed = low(layer_norm(inputs, ln1_gain, ln1_bias))
    projected = low_back(jnp.einsum('rtd,de->rte', normed, w_qkv, precision=HIGHEST) + b_qkv)
    head_shape = (row_count, length, HEADS, HEAD_DIM)
    queries = low(rotate(projected[..., :model_width].reshape(head_shape), cosine_table, sine_table))
    key_rows = low(rotate(projected[..., model_width:2 * model_width].reshape(head_shape), cosine_table, sine_table))
    value_rows = low(projected[..., 2 * model_width:].reshape(head_shape))

    def head_attention(head_items):
        head_queries, head_keys, head_values = head_items
        scores = low_back(score_scale * jnp.einsum('rqd,rkd->rqk', head_queries, head_keys, precision=HIGHEST))
        scores = jnp.where(allowed, scores, NEG_FILL)
        shifted = jnp.exp(scores - lax.optimization_barrier(jnp.max(scores, -1, keepdims=True)))
        weights = shifted / lax.optimization_barrier(jnp.sum(shifted, -1, keepdims=True))
        return jnp.einsum('rqk,rkd->rqd', low(weights), head_values, precision=HIGHEST)
    heads_first = (queries.transpose(2, 0, 1, 3), key_rows.transpose(2, 0, 1, 3), value_rows.transpose(2, 0, 1, 3))
    attended = lax.map(jax.checkpoint(head_attention), heads_first)
    attended = attended.transpose(1, 2, 0, 3).reshape(row_count, length, model_width)
    attended = low(low_back(attended))
    branch = low_back(jnp.einsum('rtd,de->rte', attended, w_out, precision=HIGHEST) + b_out)
    middle = inputs + branch
    normed_two = low(layer_norm(middle, ln2_gain, ln2_bias))
    hidden = low_back(jnp.einsum('rtd,df->rtf', normed_two, w_up, precision=HIGHEST) + b_up)
    activated = low(exact_gelu(hidden))
    return middle + low_back(jnp.einsum('rtf,fd->rtd', activated, w_down, precision=HIGHEST) + b_down)

def reference(layer_input, cotangent, segment_ids, pad_mask, ln1_gain, ln1_bias, w_qkv, b_qkv, w_out, b_out, ln2_gain, ln2_bias, w_up, b_up, w_down, b_down):
    params = tuple((parameter.astype(jnp.float32) for parameter in (ln1_gain, ln1_bias, w_qkv, b_qkv, w_out, b_out, ln2_gain, ln2_bias, w_up, b_up, w_down, b_down)))
    positions = gene_positions(segment_ids)
    cosine_table, sine_table = rotary_tables(positions)
    group_rows = math.gcd(ROWS, max(1, 2048 // ROW_LEN))
    group_count = ROWS // group_rows

    def regroup(array):
        return array.reshape((group_count, group_rows) + array.shape[1:])

    def one_group(totals, group_items):
        group_inputs, group_cotangent, group_segments, group_mask, group_cosine, group_sine = group_items
        allowed = allowed_pairs(group_segments, group_mask)

        def layer_only(inputs, parameters):
            return forward(inputs, parameters, allowed, group_cosine, group_sine)
        outputs, pull_back = jax.vjp(layer_only, group_inputs.astype(jnp.float32), params)
        input_grads, param_grads = pull_back(group_cotangent.astype(jnp.float32))
        totals = jax.tree.map(jnp.add, totals, param_grads)
        return (totals, (outputs.astype(jnp.bfloat16), input_grads.astype(jnp.bfloat16)))
    zero_grads = jax.tree.map(jnp.zeros_like, params)
    scanned = (regroup(layer_input), regroup(cotangent), regroup(segment_ids), regroup(pad_mask), regroup(cosine_table), regroup(sine_table))
    totals, (outputs, input_grads) = lax.scan(one_group, zero_grads, scanned)
    return (outputs.reshape(ROWS, ROW_LEN, D), input_grads.reshape(ROWS, ROW_LEN, D), totals[0], totals[1], totals[2], totals[3], totals[4], totals[5], totals[6], totals[7], totals[8], totals[9], totals[10], totals[11])
```

```python
import functools
import math

import jax
import jax.numpy as jnp
from jax import lax
from jax.experimental import pallas as pl
from jax.experimental.pallas import tpu as pltpu
from jax.sharding import PartitionSpec as P

HEADS = 12
HEAD_DIM = 64
GENES = 4
LANES = 128
EPSILON = 1e-05
NEG_FILL = -1000000000.0
F32 = jnp.float32
BF16 = jnp.bfloat16
MIB = 1 << 20


def nn(left, right):
    return lax.dot_general(left, right, (((1,), (0,)), ((), ())), preferred_element_type=F32)


def nt(left, right):
    return lax.dot_general(left, right, (((1,), (1,)), ((), ())), preferred_element_type=F32)


def tn(left, right):
    return lax.dot_general(left, right, (((0,), (0,)), ((), ())), preferred_element_type=F32)


def iota(shape, axis):
    return lax.broadcasted_iota(jnp.int32, shape, axis)


def full(shape):
    return pl.BlockSpec(shape, lambda *ids: (0,) * len(shape))


def rows_of(shape):
    return pl.BlockSpec(shape, lambda g, *ids: (g,) + (0,) * (len(shape) - 1))


def call(kernel, grid, in_specs, out_specs, out_shape, scratch=(), vmem=60, prefetch=1, name=None, cost=None):
    return pl.pallas_call(
        kernel,
        grid_spec=pltpu.PrefetchScalarGridSpec(
            num_scalar_prefetch=prefetch,
            grid=grid,
            in_specs=in_specs,
            out_specs=out_specs,
            scratch_shapes=list(scratch),
        ),
        out_shape=out_shape,
        compiler_params=pltpu.CompilerParams(
            dimension_semantics=("arbitrary",) * len(grid), vmem_limit_bytes=vmem * MIB
        ),
        name=name,
        cost_estimate=cost and pl.CostEstimate(flops=int(cost[0]), bytes_accessed=int(cost[1]), transcendentals=0),
    )


def shape_of(shape, dtype):
    return jax.ShapeDtypeStruct(shape, dtype)


def slot_plan(segments):
    lengths = [jnp.sum((segments == g).astype(jnp.int32)) for g in range(GENES)]
    span = segments.shape[0] // GENES
    starts, before, start, free = [], [], 0, 0
    for g in range(GENES):
        starts.append(start)
        before.append(free)
        start = start + lengths[g]
        free = free + span - lengths[g]
    return jnp.stack(
        [jnp.asarray(v, jnp.int32) for v in lengths + starts + before + [start]]
    )


def source_of_slots(plan, gene, slots):
    length = plan[gene]
    return jnp.where(
        slots < length,
        plan[GENES + gene] + slots,
        plan[3 * GENES] + plan[2 * GENES + gene] + slots - length,
    )


def reorder_kernel(plan, x_ref, c_ref, xp_ref, cp_ref):
    gene = pl.program_id(0)
    span = xp_ref.shape[0]
    length = x_ref.shape[0]
    source = source_of_slots(plan, gene, iota((span, 1), 0))
    pick = jnp.where(iota((span, length), 1) == source, 1.0, 0.0).astype(BF16)
    xp_ref[...] = nn(pick, x_ref[...]).astype(BF16)
    cp_ref[...] = nn(pick, c_ref[...]).astype(BF16)


def reorder(plan, x, c):
    length, width = x.shape
    span = length // GENES
    return call(
        reorder_kernel,
        (GENES,),
        [full((length, width))] * 2,
        [rows_of((span, width))] * 2,
        [shape_of((length, width), BF16)] * 2,
        name="reorder",
        cost=(3.3e9, 8e6),
    )(plan, x, c)


def normalize(x):
    mean = jnp.mean(x, -1, keepdims=True)
    centered = x - mean
    scale = lax.rsqrt(jnp.mean(centered * centered, -1, keepdims=True) + EPSILON)
    return centered * scale, scale


def swap_halves(t):
    low = (iota(t.shape, 1) % HEAD_DIM) < HEAD_DIM // 2
    return jnp.where(
        low, pltpu.roll(t, LANES - HEAD_DIM // 2, 1), pltpu.roll(t, HEAD_DIM // 2, 1)
    )


def head_masks(rows):
    lane = iota((rows, LANES), 1)
    return [(lane < HEAD_DIM), (lane >= HEAD_DIM)]


def allowed_pairs(plan, gene, span):
    length = plan[gene]
    i, j = iota((span, span), 0), iota((span, span), 1)
    return ((i < length) & (j < length)) | (i == j)


def keep(mask, value):
    return jnp.where(mask, value, jnp.zeros_like(value))


Z_SIZE, HALF = 4, 2
COLUMNS = 384
AXES = ("fsdp", "replica")


def tuned_mesh(mesh):
    return mesh.shape["fsdp"] == 2 * Z_SIZE and mesh.shape["replica"] == 4


def pairs(move):
    out = []
    for z in range(Z_SIZE):
        for x in range(2):
            for y in range(2):
                for c in range(2):
                    tz, tx, ty, tc = move(z, x, y, c)
                    out.append((((z * 2 + x) * 2 + y) * 2 + c, (((tz % Z_SIZE) * 2 + tx) * 2 + ty) * 2 + tc))
    return out


ACROSS_X = pairs(lambda z, x, y, c: (z, 1 - x, y, c))
ACROSS_Y = pairs(lambda z, x, y, c: (z, x, 1 - y, c))
ACROSS_CORE = pairs(lambda z, x, y, c: (z, x, y, 1 - c))
ALONG_Z = [pairs(functools.partial(lambda d, z, x, y, c: (z + d, x, y, c), d)) for d in range(Z_SIZE)]


def move(array, table):
    return lax.ppermute(array, AXES, table)


def place():
    f, r = lax.axis_index("fsdp"), lax.axis_index("replica")
    return jnp.stack([f // 2, f % 2, r // 2, r % 2]).astype(jnp.int32)


def gather_small(at, vector):
    rows = jnp.stack([vector] + [move(vector, ALONG_Z[d]) for d in range(1, Z_SIZE)])
    rows = jnp.stack([rows, move(rows, ACROSS_X)], 1).reshape(2 * Z_SIZE, -1)
    picks = [
        lax.dynamic_slice(rows, (((at[0] - f // 2) % Z_SIZE) * 2 + (at[1] ^ (f % 2)), 0), (1, rows.shape[1]))
        for f in range(2 * Z_SIZE)
    ]
    return jnp.concatenate(picks, 0)


def gather_pieces(quarter):
    along = [quarter] + [move(quarter, ALONG_Z[d]) for d in range(1, Z_SIZE)]
    first = jnp.stack([q[0] for q in along])
    second = jnp.stack([q[1] for q in along])
    first = jnp.stack([first, move(first, ACROSS_Y)])
    second = jnp.stack([second, move(second, ACROSS_X)])
    mine = [first, move(first, ACROSS_X), second, move(second, ACROSS_Y)]
    return mine + [move(m, ACROSS_CORE) for m in mine]


def reduce_pieces(at, kept, sent):
    got = move(sent, ACROSS_CORE)
    near = lambda *i: kept[i].astype(F32) + got[i].astype(F32)
    a, s = slice(None), lambda v: v.astype(BF16)
    first = near(a, 0, a, 0) + move(s(near(a, 1, a, 0)), ACROSS_X).astype(F32)
    second = near(a, a, 0, 1) + move(s(near(a, a, 1, 1)), ACROSS_Y).astype(F32)
    first = first[:, 0] + move(s(first[:, 1]), ACROSS_Y).astype(F32)
    second = second[:, 0] + move(s(second[:, 1]), ACROSS_X).astype(F32)
    both = jnp.stack([first, second], 1)
    total = both[0]
    for d in range(1, Z_SIZE):
        total = total + move(s(both[d]), ALONG_Z[d]).astype(F32)
    total = s(total)
    other = move(total, ACROSS_Y)
    by_y = jnp.where(at[2] == 0, jnp.stack([total, other]), jnp.stack([other, total]))
    other = move(by_y, ACROSS_CORE)
    return jnp.where(at[3] == 0, jnp.stack([by_y, other]), jnp.stack([other, by_y]))


def spot(at, dz, dx, dy, dc):
    z = lax.rem(at[0] + (Z_SIZE - dz), Z_SIZE)
    return z * 2 + lax.bitwise_xor(at[1], dx), lax.bitwise_xor(at[2], dy), lax.bitwise_xor(at[3], dc)


def piece_of(refs, half, dx, dy, dc):
    refs = refs[4 * dc : 4 * dc + 4]
    if half == 0:
        return refs[dx].at[dy]
    return refs[2 + dy].at[dx]


EVERY = [(dx, dy, dc) for dx in range(2) for dy in range(2) for dc in range(2)]


def at_rows(start, size):
    return pl.ds(pl.multiple_of(start, 16), size)


def at_columns(start, size):
    return pl.ds(pl.multiple_of(start, LANES), size)


def quarters_kernel(at, wqkv_ref, wout_ref, wup_ref, wdown_ref, first_ref, second_ref, sem):
    y, c = at[2], at[3]
    rows = wqkv_ref.shape[0] // 2
    width = wdown_ref.shape[1]
    copies = []

    def copy(src, row, size, column, dst):
        part = src.at[at_rows(row, size), at_columns(column, COLUMNS)]
        copies.append(pltpu.make_async_copy(part, dst, sem))

    for b in range(3):
        copy(wqkv_ref, c * rows, rows, b * width + y * COLUMNS, first_ref.at[b // 2, pl.ds((b % 2) * rows, rows)])
    copy(wout_ref, c * rows, rows, y * COLUMNS, first_ref.at[1, pl.ds(rows, rows)])
    for b in range(4):
        copy(wup_ref, c * rows, rows, b * width + y * COLUMNS, second_ref.at[0, pl.ds(b * rows, rows)])
    copy(wdown_ref, c * 4 * rows, 4 * rows, y * COLUMNS, second_ref.at[1])
    for one in copies:
        one.start()
    for one in copies:
        one.wait()


ANY = pl.BlockSpec(memory_space=pl.ANY)


def quarters(at, wqkv, wout, wup, wdown):
    rows = wqkv.shape[0] // 2
    return call(
        quarters_kernel,
        (1,),
        [ANY] * 4,
        [ANY] * 2,
        [shape_of((2, 2 * rows, COLUMNS), BF16), shape_of((2, 4 * rows, COLUMNS), BF16)],
        [pltpu.SemaphoreType.DMA],
        name="quarters",
    )(at, wqkv, wout, wup, wdown)


def run(copies):
    for one in copies:
        one.start()
    for one in copies:
        one.wait()


def attend_kernel(plan, at, *refs, pieces):
    (xp_ref, cos_ref, sin_ref, g1_ref, b1_ref, bqkv_ref, bout_ref), refs = refs[:7], refs[7:]
    source, refs = (refs[:8], refs[8:]) if pieces else (refs[:2], refs[2:])
    (qkv_ref, o_ref, lse_ref, x1_ref), refs = refs[:4], refs[4:]
    if pieces:
        whole, refs = refs[:2], refs[2:]
    wqkv_ref, wout_ref, mask_ref, sem = refs
    gene = pl.program_id(0)
    span, width = xp_ref.shape

    def wait_both():
        pltpu.make_async_copy(wqkv_ref, wqkv_ref, sem.at[0]).wait()
        pltpu.make_async_copy(wout_ref, wout_ref, sem.at[1]).wait()

    @pl.when(gene == 0)
    def _():
        if pieces:
            rows = width // (4 * Z_SIZE)

            def one(dz, carry):
                for dx, dy, dc in EVERY:
                    f, y, c = spot(at, dz, dx, dy, dc)
                    down = at_rows(f * 2 * rows + c * rows, rows)
                    for b in range(4):
                        src = piece_of(source, b // 2, dx, dy, dc).at[dz, pl.ds((b % 2) * rows, rows)]
                        across = at_columns((b % 3) * width + y * COLUMNS, COLUMNS)
                        if b < 3:
                            dst = wqkv_ref.at[down, across]
                        else:
                            dst = wout_ref.at[down, across]
                        pltpu.make_async_copy(src, dst, sem.at[b // 3]).start()
                return carry

            lax.fori_loop(0, Z_SIZE, one, 0)
        else:
            pltpu.make_async_copy(source[0], wqkv_ref, sem.at[0]).start()
            pltpu.make_async_copy(source[1], wout_ref, sem.at[1]).start()
        wait_both()
        if pieces:
            pltpu.make_async_copy(wqkv_ref, whole[0], sem.at[0]).start()
            pltpu.make_async_copy(wout_ref, whole[1], sem.at[1]).start()

    x = xp_ref[...].astype(F32)
    xhat, _ = normalize(x)
    a1 = (xhat * g1_ref[...] + b1_ref[...]).astype(BF16)
    cos, sin = cos_ref[...], sin_ref[...]
    for part in range(3):
        base = part * width
        t = nn(a1, wqkv_ref[:, base : base + width]) + bqkv_ref[:, base : base + width]
        for p in range(width // LANES):
            piece = t[:, p * LANES : (p + 1) * LANES]
            if part < 2:
                piece = piece * cos + swap_halves(piece) * sin
            qkv_ref[:, base + p * LANES : base + (p + 1) * LANES] = piece.astype(BF16)
    mask_ref[...] = jnp.where(allowed_pairs(plan, gene, span), 1.0, 0.0)
    masks = head_masks(span)
    for p in range(width // LANES):
        here = slice(p * LANES, (p + 1) * LANES)
        q = qkv_ref[:, p * LANES : (p + 1) * LANES]
        k = qkv_ref[:, width + p * LANES : width + (p + 1) * LANES] * BF16(1.0 / math.sqrt(HEAD_DIM))
        v = qkv_ref[:, 2 * width + p * LANES : 2 * width + (p + 1) * LANES]
        o = jnp.zeros((span, LANES), F32)
        for h in range(2):
            s = nt(keep(masks[h], k), q)
            s = jnp.where(mask_ref[...] > 0.5, s, NEG_FILL)
            peak = jnp.max(s, 0, keepdims=True)
            e = jnp.exp(s - peak)
            total = jnp.sum(e, 0, keepdims=True)
            weights = (e * (1.0 / total)).astype(BF16)
            o = o + tn(weights, keep(masks[h], v))
            lse_ref[pl.ds(2 * p + h, 1), :] = peak + jnp.log(total)
        o_ref[:, here] = o.astype(BF16)
    x1_ref[...] = x + nn(o_ref[...], wout_ref[...]) + bout_ref[...]
    if pieces:

        @pl.when(gene == pl.num_programs(0) - 1)
        def _():
            wait_both()


def attend(plan, at, xp, cos, sin, g1, b1, bqkv, bout, source):
    length, width = xp.shape
    span = length // GENES
    pieces = len(source) == 8
    weights = [shape_of((width, 3 * width), BF16), shape_of((width, width), BF16)]
    got = call(
        functools.partial(attend_kernel, pieces=pieces),
        (GENES,),
        [
            rows_of((span, width)),
            rows_of((span, LANES)),
            rows_of((span, LANES)),
            full((1, width)),
            full((1, width)),
            full((1, 3 * width)),
            full((1, width)),
        ]
        + [ANY] * len(source),
        [
            rows_of((span, 3 * width)),
            rows_of((span, width)),
            pl.BlockSpec((16, span), lambda g, *ids: (0, g)),
            rows_of((span, width)),
        ]
        + [ANY] * (2 if pieces else 0),
        [
            shape_of((length, 3 * width), BF16),
            shape_of((length, width), BF16),
            shape_of((16, length), F32),
            shape_of((length, width), F32),
        ]
        + (weights if pieces else []),
        [
            pltpu.VMEM((width, 3 * width), BF16),
            pltpu.VMEM((width, width), BF16),
            pltpu.VMEM((span, span), F32),
            pltpu.SemaphoreType.DMA((2,)),
        ],
        prefetch=2,
        name="attend",
        cost=(11e9, 20e6),
    )(plan, at, xp, cos, sin, g1, b1, bqkv, bout, *source)
    return got[:4], (got[4:] if pieces else source)


def feed_kernel(at, *refs, block, pieces, steps):
    (x1_ref, c_ref, g2_ref, b2_ref, bup_ref, bdown_ref), refs = refs[:6], refs[6:]
    source, refs = (refs[:8], refs[8:]) if pieces else (refs[:2], refs[2:])
    (out_ref, dx1_ref, da_ref, gbup_ref, sums_ref, first_ref, second_ref), refs = refs[:7], refs[7:]
    a2_ref, acc_ref, dh_ref, gr_ref, du_ref, wups, wdowns, gups, gdowns, load_sem, store_sem = refs
    step = pl.program_id(0)
    length, width = x1_ref.shape
    chunk = bup_ref.shape[1]
    blocks = length // block
    slot = lax.rem(step, 2)
    rows = width // (4 * Z_SIZE)

    def load(j, to):
        if pieces:

            def one(dz, carry):
                for dx, dy, dc in EVERY:
                    f, y, c = spot(at, dz, dx, dy, dc)
                    src = piece_of(source, 0, dx, dy, dc).at[dz, at_rows(j * rows, rows)]
                    dst = wups.at[to, at_rows(f * 2 * rows + c * rows, rows), at_columns(y * COLUMNS, COLUMNS)]
                    pltpu.make_async_copy(src, dst, load_sem.at[0, to]).start()
                return carry

            lax.fori_loop(0, Z_SIZE, one, 0)
            back = lax.rem(at[0] + (Z_SIZE - j), Z_SIZE)
            for dx, dy, dc in EVERY:
                f, y, c = spot(at, back, dx, dy, dc)
                x = lax.bitwise_xor(at[1], dx)
                src = piece_of(source, 1, dx, dy, dc).at[back]
                dst = wdowns.at[to, at_rows((x * 2 + c) * 4 * rows, 4 * rows), at_columns(y * COLUMNS, COLUMNS)]
                pltpu.make_async_copy(src, dst, load_sem.at[1, to]).start()
        else:
            part = source[0].at[:, at_columns(j * chunk, chunk)]
            pltpu.make_async_copy(part, wups.at[to], load_sem.at[0, to]).start()
            part = source[1].at[at_rows(j * chunk, chunk), :]
            pltpu.make_async_copy(part, wdowns.at[to], load_sem.at[1, to]).start()

    def store(j, to):
        if pieces:

            def one(dz, carry):
                for dx, dy, dc in EVERY:
                    f, y, c = spot(at, Z_SIZE - dz, dx, dy, dc)
                    src = gups.at[to, at_rows(f * 2 * rows + c * rows, rows), at_columns(y * COLUMNS, COLUMNS)]
                    dst = (first_ref, second_ref)[dc].at[dz, dx, dy, 0, at_rows(j * rows, rows)]
                    pltpu.make_async_copy(src, dst, store_sem.at[0, to]).start()
                return carry

            lax.fori_loop(0, Z_SIZE, one, 0)
            ahead = lax.rem(j + Z_SIZE - at[0], Z_SIZE)
            for dx, dy, dc in EVERY:
                f, y, c = spot(at, 0, dx, dy, dc)
                x = lax.bitwise_xor(at[1], dx)
                src = gdowns.at[to, at_rows((x * 2 + c) * 4 * rows, 4 * rows), at_columns(y * COLUMNS, COLUMNS)]
                dst = (first_ref, second_ref)[dc].at[ahead, dx, dy, 1]
                pltpu.make_async_copy(src, dst, store_sem.at[1, to]).start()
        else:
            part = first_ref.at[:, at_columns(j * chunk, chunk)]
            pltpu.make_async_copy(gups.at[to], part, store_sem.at[0, to]).start()
            part = second_ref.at[at_rows(j * chunk, chunk), :]
            pltpu.make_async_copy(gdowns.at[to], part, store_sem.at[1, to]).start()

    def wait_load(to):
        pltpu.make_async_copy(wups.at[to], wups.at[to], load_sem.at[0, to]).wait()
        pltpu.make_async_copy(wdowns.at[to], wdowns.at[to], load_sem.at[1, to]).wait()

    def wait_store(to):
        pltpu.make_async_copy(gups.at[to], gups.at[to], store_sem.at[0, to]).wait()
        pltpu.make_async_copy(gdowns.at[to], gdowns.at[to], store_sem.at[1, to]).wait()

    @pl.when(step == 0)
    def _():
        load(0, 0)

        def one(i, carry):
            here = pl.ds(i * block, block)
            xhat, _ = normalize(x1_ref[here, :])
            a2_ref[here, :] = (xhat * g2_ref[...] + b2_ref[...]).astype(BF16)
            return carry

        lax.fori_loop(0, blocks, one, 0)

    wait_load(slot)

    @pl.when(step < steps - 1)
    def _():
        load(step + 1, 1 - slot)

    wup_ref, wdown_ref = wups.at[slot], wdowns.at[slot]

    def one(i, bias_sum):
        here = pl.ds(i * block, block)
        u = nn(a2_ref[here, :], wup_ref[...]) + bup_ref[...]
        phi = 0.5 + 0.5 * lax.erf(u * math.sqrt(0.5))
        slope = phi + u * (jnp.exp(-0.5 * u * u) * (1.0 / math.sqrt(2.0 * math.pi)))
        gr = (u * phi).astype(BF16)
        gr_ref[here, :] = gr
        du = (nt(c_ref[here, :], wdown_ref[...]) * slope).astype(BF16)
        du_ref[here, :] = du
        out = nn(gr, wdown_ref[...])
        dh = nt(du, wup_ref[...])

        @pl.when(step == 0)
        def _():
            acc_ref[here, :] = out
            dh_ref[here, :] = dh

        @pl.when(step > 0)
        def _():
            acc_ref[here, :] += out
            dh_ref[here, :] += dh

        return bias_sum + jnp.sum(du.astype(F32), 0, keepdims=True)

    gbup_ref[...] = lax.fori_loop(0, blocks, one, jnp.zeros((1, chunk), F32))

    @pl.when(step >= 2)
    def _():
        wait_store(slot)

    gdowns[slot] = tn(gr_ref[...], c_ref[...]).astype(BF16)
    gups[slot] = tn(a2_ref[...], du_ref[...]).astype(BF16)
    store(step, slot)

    @pl.when(step == steps - 1)
    def _():
        def one(i, sums):
            here = pl.ds(i * block, block)
            x1 = x1_ref[here, :]
            xhat, scale = normalize(x1)
            out_ref[here, :] = (x1 + acc_ref[here, :] + bdown_ref[...]).astype(BF16)
            dh = dh_ref[here, :]
            c = c_ref[here, :].astype(F32)
            e = dh * g2_ref[...]
            dx1 = c + scale * (
                e - jnp.mean(e, -1, keepdims=True) - xhat * jnp.mean(e * xhat, -1, keepdims=True)
            )
            dx1_ref[here, :] = dx1
            da = dx1.astype(BF16)
            da_ref[here, :] = da
            new = (
                jnp.sum(dh * xhat, 0, keepdims=True),
                jnp.sum(dh, 0, keepdims=True),
                jnp.sum(c, 0, keepdims=True),
                jnp.sum(da.astype(F32), 0, keepdims=True),
            )
            return tuple(a + b for a, b in zip(sums, new))

        sums = lax.fori_loop(0, blocks, one, (jnp.zeros((1, width), F32),) * 4)
        for i in range(4):
            sums_ref[i : i + 1, :] = sums[i]
        wait_store(1 - slot)
        wait_store(slot)


def feed(at, x1, c, g2, b2, bup, bdown, source):
    length, width = x1.shape
    hidden = bup.shape[1]
    steps = 4
    chunk = hidden // steps
    pieces = len(source) == 8
    if pieces:
        rows = width // Z_SIZE
        stored = [shape_of((Z_SIZE, 2, 2, 2, rows, COLUMNS), BF16)] * 2
    else:
        stored = [shape_of((width, hidden), BF16), shape_of((hidden, width), BF16)]
    return call(
        functools.partial(feed_kernel, block=length // 4, pieces=pieces, steps=steps),
        (steps,),
        [
            full((length, width)),
            full((length, width)),
            full((1, width)),
            full((1, width)),
            pl.BlockSpec((1, chunk), lambda j, *ids: (0, j)),
            full((1, width)),
        ]
        + [ANY] * len(source),
        [
            full((length, width)),
            full((length, width)),
            full((length, width)),
            pl.BlockSpec((1, chunk), lambda j, *ids: (0, j)),
            full((8, width)),
            ANY,
            ANY,
        ],
        [
            shape_of((length, width), BF16),
            shape_of((length, width), F32),
            shape_of((length, width), BF16),
            shape_of((1, hidden), F32),
            shape_of((8, width), F32),
        ]
        + stored,
        [
            pltpu.VMEM((length, width), BF16),
            pltpu.VMEM((length, width), F32),
            pltpu.VMEM((length, width), F32),
            pltpu.VMEM((length, chunk), BF16),
            pltpu.VMEM((length, chunk), BF16),
            pltpu.VMEM((2, width, chunk), BF16),
            pltpu.VMEM((2, chunk, width), BF16),
            pltpu.VMEM((2, width, chunk), BF16),
            pltpu.VMEM((2, chunk, width), BF16),
            pltpu.SemaphoreType.DMA((2, 2)),
            pltpu.SemaphoreType.DMA((2, 2)),
        ],
        name="feed",
        cost=(29e9, 40e6),
    )(at, x1, c, g2, b2, bup, bdown, *source)


def attend_back_kernel(
    plan, qkv_ref, da_ref, lse_ref, cos_ref, sin_ref, xp_ref, dx1_ref, g1_ref, wout_ref, wqkv_ref,
    dqkv_ref, dxp_ref, sums_ref, dout_ref, mask_ref
):
    gene = pl.program_id(0)
    span, width = da_ref.shape
    score_scale = 1.0 / math.sqrt(HEAD_DIM)
    dout_ref[...] = nt(da_ref[...], wout_ref[...]).astype(BF16)
    mask_ref[...] = jnp.where(allowed_pairs(plan, gene, span), 1.0, 0.0)
    cos, sin = cos_ref[...], sin_ref[...]
    masks = head_masks(span)

    def back(t):
        return (t * cos - swap_halves(t) * sin).astype(BF16)

    for p in range(width // LANES):
        here = slice(p * LANES, (p + 1) * LANES)
        q = qkv_ref[:, p * LANES : (p + 1) * LANES]
        k = qkv_ref[:, width + p * LANES : width + (p + 1) * LANES] * BF16(score_scale)
        v = qkv_ref[:, 2 * width + p * LANES : 2 * width + (p + 1) * LANES]
        dout = dout_ref[:, here]
        dq = jnp.zeros((span, LANES), F32)
        dk = jnp.zeros((span, LANES), F32)
        dv = jnp.zeros((span, LANES), F32)
        for h in range(2):
            kh = keep(masks[h], k)
            s = nt(kh, q)
            s = jnp.where(mask_ref[...] > 0.5, s, NEG_FILL)
            weights = jnp.exp(s - lse_ref[pl.ds(2 * p + h, 1), :])
            dw = nt(keep(masks[h], v), dout)
            dot = jnp.sum(weights * dw, 0, keepdims=True)
            ds = (weights * (dw - dot)).astype(BF16)
            dv = dv + nn(weights.astype(BF16), keep(masks[h], dout))
            dk = dk + nn(ds, keep(masks[h], q))
            dq = dq + tn(ds, kh)
        dqkv_ref[:, p * LANES : (p + 1) * LANES] = back(dq)
        dqkv_ref[:, width + p * LANES : width + (p + 1) * LANES] = back(dk * score_scale)
        dqkv_ref[:, 2 * width + p * LANES : 2 * width + (p + 1) * LANES] = dv.astype(BF16)

    dh = nt(dqkv_ref[...], wqkv_ref[...])
    xhat, scale = normalize(xp_ref[...].astype(F32))
    e = dh * g1_ref[...]
    dx = dx1_ref[...] + scale * (
        e - jnp.mean(e, -1, keepdims=True) - xhat * jnp.mean(e * xhat, -1, keepdims=True)
    )
    dxp_ref[...] = dx.astype(BF16)
    gain = jnp.sum(dh * xhat, 0, keepdims=True)
    bias = jnp.sum(dh, 0, keepdims=True)

    @pl.when(gene == 0)
    def _():
        sums_ref[0:1, :] = gain
        sums_ref[1:2, :] = bias

    @pl.when(gene > 0)
    def _():
        sums_ref[0:1, :] += gain
        sums_ref[1:2, :] += bias


def attend_back(plan, qkv, da, lse, cos, sin, xp, dx1, g1, wout, wqkv):
    length, width = da.shape
    span = length // GENES
    return call(
        attend_back_kernel,
        (GENES,),
        [
            rows_of((span, 3 * width)),
            rows_of((span, width)),
            pl.BlockSpec((16, span), lambda g, *ids: (0, g)),
            rows_of((span, LANES)),
            rows_of((span, LANES)),
            rows_of((span, width)),
            rows_of((span, width)),
            full((1, width)),
            full((width, width)),
            full((width, 3 * width)),
        ],
        [rows_of((span, 3 * width)), rows_of((span, width)), full((8, width))],
        [
            shape_of((length, 3 * width), BF16),
            shape_of((length, width), BF16),
            shape_of((8, width), F32),
        ],
        [pltpu.VMEM((span, width), BF16), pltpu.VMEM((span, span), F32)],
        name="attend_back",
        cost=(16e9, 25e6),
    )(plan, qkv, da, lse, cos, sin, xp, dx1, g1, wout, wqkv)


def grads_kernel(at, *refs, pieces):
    (xp_ref, g1_ref, b1_ref, o_ref, da_ref, dqkv_ref, small_ref), refs = refs[:7], refs[7:]
    first_ref, second_ref, a1_ref, grad_ref, sem, small_sem = refs
    step = pl.program_id(0)
    width = xp_ref.shape[1]
    slot = lax.rem(step, 2)
    rows = width // (4 * Z_SIZE)

    def wait(to):
        pltpu.make_async_copy(grad_ref.at[to], grad_ref.at[to], sem.at[to]).wait()

    def store(half, base, to):
        def one(dz, carry):
            for dx, dy, dc in EVERY:
                f, y, c = spot(at, Z_SIZE - dz, dx, dy, dc)
                src = grad_ref.at[to, at_rows(f * 2 * rows + c * rows, rows), at_columns(y * COLUMNS, COLUMNS)]
                dst = (first_ref, second_ref)[dc].at[dz, dx, dy, half, pl.ds(base * rows, rows)]
                pltpu.make_async_copy(src, dst, sem.at[to]).start()
            return carry

        lax.fori_loop(0, Z_SIZE, one, 0)

    def smalls(act):
        def one(dz, carry):
            for dx, dy, dc in EVERY:
                f, y, c = spot(at, Z_SIZE - dz, dx, dy, dc)
                src = small_ref.at[f, y, c]
                dst = (first_ref, second_ref)[dc].at[dz, dx, dy, :, pl.ds(2 * rows, 8)]
                act(pltpu.make_async_copy(src, dst, small_sem))
            return carry

        lax.fori_loop(0, Z_SIZE, one, 0)

    @pl.when(step >= 2)
    def _():
        wait(slot)

    for j in range(4):

        @pl.when(step == j)
        def _(j=j):
            if j == 0:
                if pieces:
                    smalls(lambda copy: copy.start())
                xhat, _ = normalize(xp_ref[...].astype(F32))
                a1_ref[...] = (xhat * g1_ref[...] + b1_ref[...]).astype(BF16)
            if j < 3:
                grad_ref[j % 2] = tn(a1_ref[...], dqkv_ref[...]).astype(BF16)
            else:
                grad_ref[j % 2] = tn(o_ref[...], da_ref[...]).astype(BF16)
            if pieces:
                store(j // 2, j % 2, j % 2)
            elif j < 3:
                dst = first_ref.at[:, pl.ds(j * width, width)]
                pltpu.make_async_copy(grad_ref.at[j % 2], dst, sem.at[j % 2]).start()
            else:
                pltpu.make_async_copy(grad_ref.at[j % 2], second_ref, sem.at[j % 2]).start()
            if j == 3:
                wait(0)
                wait(1)
                if pieces:
                    smalls(lambda copy: copy.wait())


def grads(at, xp, g1, b1, o, da, dqkv, small, pieces):
    length, width = xp.shape
    if pieces:
        rows = width // (2 * Z_SIZE) + 8
        stored = [shape_of((Z_SIZE, 2, 2, 2, rows, COLUMNS), BF16)] * 2
    else:
        stored = [shape_of((width, 3 * width), BF16), shape_of((width, width), BF16)]
    return call(
        functools.partial(grads_kernel, pieces=pieces),
        (4,),
        [
            full((length, width)),
            full((1, width)),
            full((1, width)),
            full((length, width)),
            full((length, width)),
            pl.BlockSpec((length, width), lambda j, *ids: (0, jnp.minimum(j, 2))),
            ANY,
        ],
        [ANY, ANY],
        stored,
        [
            pltpu.VMEM((length, width), BF16),
            pltpu.VMEM((2, width, width), BF16),
            pltpu.SemaphoreType.DMA((2,)),
            pltpu.SemaphoreType.DMA,
        ],
        name="grads",
        cost=(5e9, 12e6),
    )(at, xp, g1, b1, o, da, dqkv, small)


def restore_kernel(src_ref, outp_ref, dxp_ref, out_ref, dx_ref):
    span, width = out_ref.shape
    codon = iota((span, outp_ref.shape[0]), 0) + pl.program_id(0) * span
    pick = jnp.where(codon == src_ref[0:1, :], 1.0, 0.0).astype(BF16)
    out_ref[...] = nn(pick, outp_ref[...]).astype(BF16)
    dx_ref[...] = nn(pick, dxp_ref[...]).astype(BF16)


def restore(src, outp, dxp):
    length, width = outp.shape
    span = length // GENES
    return call(
        restore_kernel,
        (GENES,),
        [full((1, length)), full((length, width)), full((length, width))],
        [rows_of((span, width))] * 2,
        [shape_of((length, width), BF16)] * 2,
        prefetch=0,
        name="restore",
        cost=(3.3e9, 8e6),
    )(src, outp, dxp)


def gather(shard):
    return lax.all_gather(shard, "fsdp", axis=0, tiled=True)


def reduce_rows(grad):
    part = lax.psum_scatter(grad, "fsdp", scatter_dimension=0, tiled=True)
    return lax.psum(part.astype(BF16), "replica").astype(F32)


def rotary_tables(positions):
    frequency = jnp.power(10000.0, jnp.arange(HEAD_DIM // 2, dtype=F32) * (-2.0 / HEAD_DIM))
    angles = positions.astype(F32)[:, None] * jnp.tile(frequency, LANES // (HEAD_DIM // 2))[None]
    sign = jnp.where(jnp.arange(LANES) % HEAD_DIM < HEAD_DIM // 2, -1.0, 1.0).astype(F32)
    return jnp.cos(angles), jnp.sin(angles) * sign


def split_rows(packed, sizes):
    out, start = [], 0
    for size in sizes:
        out.append(packed[:, start : start + size])
        start += size
    return out


def body(
    layer_input, cotangent, segment_ids, pad_mask, ln1_gain, ln1_bias, w_qkv, b_qkv, w_out, b_out,
    ln2_gain, ln2_bias, w_up, b_up, w_down, b_down, *, tuned,
):
    length, width = layer_input.shape[1:]
    span = length // GENES
    small = (ln1_gain, ln1_bias, b_qkv, b_out, ln2_gain, ln2_bias, b_up, b_down)
    sizes = [v.shape[0] for v in small]
    packed = jnp.concatenate(small)
    if tuned:
        at = place()
        first, second = quarters(at, w_qkv, w_out, w_up, w_down)
        packed = gather_small(at, packed)
        attention = gather_pieces(first)
        forward = gather_pieces(second)
    else:
        at = jnp.zeros((4,), jnp.int32)
        packed = gather(packed[None])
        attention = gather(w_qkv), gather(w_out)
        forward = gather(w_up), gather(w_down)
    g1, b1, bqkv, bout, g2, b2, bup, bdown = (
        v.reshape(1, -1).astype(F32) for v in split_rows(packed, sizes)
    )
    plan = slot_plan(segment_ids[0])
    slots = jnp.arange(length, dtype=jnp.int32)
    gene, slot = slots // span, slots % span
    src = source_of_slots(plan, gene, slot)
    start = jnp.where(slot < plan[gene], plan[GENES + gene], plan[3 * GENES])
    cos, sin = rotary_tables(src - start)
    xp, cp = reorder(plan, layer_input[0], cotangent[0])
    (qkv, o, lse, x1), (wqkv, wout) = attend(plan, at, xp, cos, sin, g1, b1, bqkv, bout, attention)
    outp, dx1, da, gbup, sums2, *pieces_f = feed(at, x1, cp, g2, b2, bup, bdown, forward)
    dqkv, dxp, sums1 = attend_back(plan, qkv, da, lse, cos, sin, xp, dx1, g1, wout, wqkv)
    gbqkv = jnp.sum(dqkv.astype(F32), 0)
    small = [sums1[0], sums1[1], gbqkv, sums2[3], sums2[0], sums2[1], gbup[0], sums2[2]]
    count = width // (sizes[0])
    small = jnp.concatenate([v.reshape(count, -1) for v in small], 1)
    if tuned:
        room = 8 * COLUMNS
        small = jnp.pad(small, ((0, 0), (0, room - small.shape[1]))).astype(BF16)
        small = small.reshape(count, 2, 2, 2, 1, COLUMNS)
        small = jnp.pad(small, ((0, 0),) * 4 + ((0, 7), (0, 0)))
    pieces_a = grads(at, xp, g1, b1, o, da, dqkv, small, tuned)
    layer_out, input_grad = restore(src[None], outp, dxp)
    if tuned:
        f = reduce_pieces(at, *pieces_f)
        a = reduce_pieces(at, *pieces_a)
        rows = width // (4 * Z_SIZE)
        up = f[:, :, 0].reshape(2, 2, 4, rows, COLUMNS).transpose(0, 3, 2, 1, 4).reshape(2 * rows, -1)
        down = f[:, :, 1].transpose(0, 2, 1, 3).reshape(8 * rows, width)
        blocks = a[:, :, :, : 2 * rows].reshape(2, 2, 4, rows, COLUMNS).transpose(0, 3, 2, 1, 4)
        blocks = blocks.reshape(2 * rows, 4 * width)
        qkv_grad, out_grad = blocks[:, : 3 * width], blocks[:, 3 * width :]
        small = a[:, :, :, 2 * rows].transpose(1, 0, 2, 3).reshape(1, -1)[:, : sum(sizes)].astype(F32)
        up, down, qkv_grad, out_grad = (v.astype(F32) for v in (up, down, qkv_grad, out_grad))
    else:
        qkv_grad, out_grad = map(reduce_rows, pieces_a)
        up, down = map(reduce_rows, pieces_f)
        small = reduce_rows(small)
    dg1, db1, dbqkv, dbout, dg2, db2, dbup, dbdown = (v.reshape(-1) for v in split_rows(small, sizes))
    return (
        layer_out[None], input_grad[None], dg1, db1, qkv_grad, dbqkv, out_grad, dbout, dg2, db2,
        up, dbup, down, dbdown,
    )


def solution(mesh):
    rows = ("fsdp", "replica")
    by_row = P(rows, None, None)
    vector, matrix = P("fsdp"), P("fsdp", None)
    params = (
        vector, vector, matrix, vector, matrix, vector, vector, vector, matrix, vector, matrix, vector,
    )
    in_specs = (by_row, by_row, P(rows, None), P(rows, None)) + params
    out_specs = (by_row, by_row) + params
    return jax.shard_map(
        functools.partial(body, tuned=tuned_mesh(mesh)),
        mesh=mesh, in_specs=in_specs, out_specs=out_specs, check_vma=False,
    )
```

```python
import functools
import math

import jax
import jax.numpy as jnp
import numpy as np
from jax import lax
from jax.experimental import pallas as pl
from jax.experimental.pallas import tpu as pltpu
from jax.sharding import PartitionSpec as P

HEADS = 12
HEAD_DIM = 64
GENES = 4
LANES = 128
EPSILON = 1e-05
NEG_FILL = -1000000000.0
F32 = jnp.float32
BF16 = jnp.bfloat16
MIB = 1 << 20


def nn(left, right):
    return lax.dot_general(left, right, (((1,), (0,)), ((), ())), preferred_element_type=F32)


def nt(left, right):
    return lax.dot_general(left, right, (((1,), (1,)), ((), ())), preferred_element_type=F32)


def tn(left, right):
    return lax.dot_general(left, right, (((0,), (0,)), ((), ())), preferred_element_type=F32)


def iota(shape, axis):
    return lax.broadcasted_iota(jnp.int32, shape, axis)


def full(shape):
    return pl.BlockSpec(shape, lambda *ids: (0,) * len(shape))


def rows_of(shape):
    return pl.BlockSpec(shape, lambda g, *ids: (g,) + (0,) * (len(shape) - 1))


def call(kernel, grid, in_specs, out_specs, out_shape, scratch=(), vmem=60, prefetch=1, name=None, cost=None, aliases=None):
    return pl.pallas_call(
        kernel,
        grid_spec=pltpu.PrefetchScalarGridSpec(
            num_scalar_prefetch=prefetch,
            grid=grid,
            in_specs=in_specs,
            out_specs=out_specs,
            scratch_shapes=list(scratch),
        ),
        out_shape=out_shape,
        input_output_aliases=aliases or {},
        compiler_params=pltpu.CompilerParams(
            dimension_semantics=("arbitrary",) * len(grid), vmem_limit_bytes=vmem * MIB
        ),
        name=name,
        cost_estimate=cost and pl.CostEstimate(flops=int(cost[0]), bytes_accessed=int(cost[1]), transcendentals=0),
    )


def shape_of(shape, dtype):
    return jax.ShapeDtypeStruct(shape, dtype)


def normalize(x):
    mean = jnp.mean(x, -1, keepdims=True)
    centered = x - mean
    scale = lax.rsqrt(jnp.mean(centered * centered, -1, keepdims=True) + EPSILON)
    return centered * scale, scale


def swap_halves(t):
    low = (iota(t.shape, 1) % HEAD_DIM) < HEAD_DIM // 2
    return jnp.where(
        low, pltpu.roll(t, LANES - HEAD_DIM // 2, 1), pltpu.roll(t, HEAD_DIM // 2, 1)
    )


def head_masks(rows):
    lane = iota((rows, LANES), 1)
    return [(lane < HEAD_DIM), (lane >= HEAD_DIM)]


def allowed_pairs(plan, gene, span):
    length = plan[gene]
    i, j = iota((span, span), 0), iota((span, span), 1)
    return ((i < length) & (j < length)) | (i == j)


def keep(mask, value):
    return jnp.where(mask, value, jnp.zeros_like(value))


Z_SIZE = 4
COLUMNS = 384
AXES = ("fsdp", "replica")
ANY = pl.BlockSpec(memory_space=pl.ANY)
PIECES = 32
EVERY = [(dx, dy, dc) for dx in range(2) for dy in range(2) for dc in range(2)]
SLOTS = (0, 128, 256, 640, 768, 896, 1024, 1408)
PACKED = 1536


def tuned_mesh(mesh):
    return mesh.shape["fsdp"] == 2 * Z_SIZE and mesh.shape["replica"] == 4


def pairs(step):
    out = []
    for z in range(Z_SIZE):
        for x in range(2):
            for y in range(2):
                for c in range(2):
                    tz, tx, ty, tc = step(z, x, y, c)
                    out.append((((z * 2 + x) * 2 + y) * 2 + c, (((tz % Z_SIZE) * 2 + tx) * 2 + ty) * 2 + tc))
    return out


ACROSS_X = pairs(lambda z, x, y, c: (z, 1 - x, y, c))
ACROSS_Y = pairs(lambda z, x, y, c: (z, x, 1 - y, c))
ACROSS_CORE = pairs(lambda z, x, y, c: (z, x, y, 1 - c))
ALONG_Z = [pairs(functools.partial(lambda d, z, x, y, c: (z + d, x, y, c), d)) for d in range(Z_SIZE)]
tie = lax.optimization_barrier


def move(array, table):
    return lax.ppermute(array, AXES, table)


def place():
    f, r = lax.axis_index("fsdp"), lax.axis_index("replica")
    return jnp.stack([f // 2, f % 2, r // 2, r % 2]).astype(jnp.int32)


def spot(at, dz, dx, dy, dc):
    z = lax.rem(at[0] + (Z_SIZE - dz), Z_SIZE)
    return z * 2 + lax.bitwise_xor(at[1], dx), lax.bitwise_xor(at[2], dy), lax.bitwise_xor(at[3], dc)


def piece_index(half, dz, dx, dy):
    own = 24 + dx * 4 + dy * 2 + half
    if isinstance(dz, int) and dz == 0:
        return own
    far = (12 + dy * 6 + dx * 3 if half else dx * 6 + dy * 3) + dz - 1
    return far if isinstance(dz, int) else jnp.where(dz == 0, own, far)


def at_rows(start, size):
    return pl.ds(pl.multiple_of(start, 16), size)


def at_columns(start, size):
    return pl.ds(pl.multiple_of(start, LANES), size)


def quarters_kernel(at, *refs):
    wqkv, wout, wup, wdown = refs[:4]
    vectors, (near1, near2, side, packed) = refs[4:12], refs[12:]
    width = wout.shape[1]
    rows = wout.shape[0] // 2
    packed[...] = jnp.zeros_like(packed)
    for ref, start in zip(vectors, SLOTS):
        packed[:, start : start + ref.shape[0]] = ref[...].reshape(1, -1)
    tail = jnp.zeros((8, COLUMNS), BF16)
    for i in range(4):
        part = jnp.broadcast_to(packed[:, i * COLUMNS : (i + 1) * COLUMNS], (8, COLUMNS))
        tail = jnp.where(iota((8, COLUMNS), 0) == i, part, tail)
    mine = at_rows(at[3] * rows, rows)
    for y in range(2):
        for b in range(4):
            ref, base = (wqkv, b * width) if b < 3 else (wout, 0)
            start = base + y * COLUMNS
            side[y, b // 2, (b % 2) * rows : (b % 2 + 1) * rows, :] = ref[mine, start : start + COLUMNS]
            start = b * width + y * COLUMNS
            side[y, 0, (2 + b) * rows : (3 + b) * rows, :] = wup[mine, start : start + COLUMNS]
        here = slice(y * COLUMNS, (y + 1) * COLUMNS)
        side[y, 1, 2 * rows : 6 * rows, :] = wdown[at_rows(at[3] * 4 * rows, 4 * rows), here]
        for h in range(2):
            side[y, h, 6 * rows : 6 * rows + 8, :] = tail
    near1[:, 0 : 2 * rows, :] = side[at[2], :, 0 : 2 * rows, :]
    near2[...] = side[at[2], :, 2 * rows : 6 * rows, :]
    for h in range(2):
        near1[h, 2 * rows : 2 * rows + 8, :] = tail


def quarters(at, wqkv, wout, wup, wdown, vectors):
    rows = wqkv.shape[0] // 2
    shapes = [
        (2, 2 * rows + 8, COLUMNS),
        (2, 4 * rows, COLUMNS),
        (2, 2, 6 * rows + 8, COLUMNS),
    ]
    matrices = (wqkv, wout, wup, wdown)
    return call(
        quarters_kernel,
        (1,),
        [full(v.shape) for v in matrices + tuple(vectors)],
        [full(s) for s in shapes],
        [shape_of(s, BF16) for s in shapes],
        [pltpu.VMEM((1, PACKED), BF16)],
        name="quarters",
        cost=(0, 6e6),
    )(at, *matrices, *vectors)


def rel_mask(at, shards, columns, size, x_bit):
    z = (at[0] + Z_SIZE - iota((shards, columns), 0)) % Z_SIZE
    shard = z * 2 + lax.bitwise_xor(at[1], x_bit)
    return (iota((shards, columns), 1) // size == shard) & (iota((shards, columns), 0) < Z_SIZE)


def spread(size, columns):
    lanes = -(-size // LANES) * LANES
    lane, column = iota((lanes, columns), 0), iota((lanes, columns), 1)
    return jnp.where(column % size == lane, 1.0, 0.0).astype(BF16)


def unpack_kernel(at, near_ref, far_ref, *refs):
    out, row_ref = refs[:8], refs[8]
    row_ref[...] = jnp.zeros_like(row_ref)
    for x_bit, rows in enumerate((near_ref, far_ref)):
        for d in range(Z_SIZE):
            for i in range(4):
                row_ref[x_bit, d : d + 1, i * COLUMNS : (i + 1) * COLUMNS] = rows[d, i : i + 1, :].astype(F32)
    for ref, start in zip(out, SLOTS):
        columns = ref.shape[1]
        size = columns // (2 * Z_SIZE)
        table = spread(size, columns)
        lanes = slice(start, start + table.shape[0])
        total = jnp.zeros((1, columns), F32)
        for x_bit in range(2):
            got = nn(row_ref[x_bit, :, lanes].astype(BF16), table)
            mask = rel_mask(at, 8, columns, size, x_bit)
            total = total + jnp.sum(jnp.where(mask, got, 0.0), 0, keepdims=True)
        ref[...] = total


def unpack(at, near, far, sizes):
    shapes = [(1, n * 2 * Z_SIZE) for n in sizes]
    return call(
        unpack_kernel,
        (1,),
        [full(near.shape)] * 2,
        [full(s) for s in shapes],
        [shape_of(s, F32) for s in shapes],
        [pltpu.VMEM((2, 8, PACKED), F32)],
        name="unpack",
        cost=(1e8, 1e5),
    )(at, near, far)


def plan_of(segments):
    lengths = [jnp.sum(jnp.where(segments == g, 1.0, 0.0)).astype(jnp.int32) for g in range(GENES)]
    span = segments.size // GENES
    starts, before, start, free = [], [], 0, 0
    for g in range(GENES):
        starts.append(start)
        before.append(free)
        start = start + lengths[g]
        free = free + span - lengths[g]
    return [jnp.asarray(v, jnp.int32) for v in lengths + starts + before + [start]]


def source_of_slots(plan, gene, slots):
    length = plan[gene]
    return jnp.where(
        slots < length,
        plan[GENES + gene] + slots,
        plan[3 * GENES] + plan[2 * GENES + gene] + slots - length,
    )


def prepare_kernel(seg_ref, x_ref, c_ref, freq_ref, plan_ref, xp_ref, cp_ref, cos_ref, sin_ref):
    gene = pl.program_id(0)
    span = xp_ref.shape[0]
    length = x_ref.shape[0]

    @pl.when(gene == 0)
    def _():
        for i, v in enumerate(plan_of(seg_ref[...])):
            plan_ref[i] = v

    slots = iota((span, 1), 0)
    source = source_of_slots(plan_ref, gene, slots)
    pick = jnp.where(iota((span, length), 1) == source, 1.0, 0.0).astype(BF16)
    xp_ref[...] = nn(pick, x_ref[...]).astype(BF16)
    cp_ref[...] = nn(pick, c_ref[...]).astype(BF16)
    start = jnp.where(slots < plan_ref[gene], plan_ref[GENES + gene], plan_ref[3 * GENES])
    angle = (source - start).astype(F32) * freq_ref[...]
    low = iota((span, LANES), 1) % HEAD_DIM < HEAD_DIM // 2
    cos_ref[...] = jnp.cos(angle)
    sine = jnp.sin(angle)
    sin_ref[...] = jnp.where(low, -sine, sine)


def prepare(segments, x, c):
    length, width = x.shape
    span = length // GENES
    frequency = np.power(10000.0, np.arange(HEAD_DIM // 2) * (-2.0 / HEAD_DIM))
    frequency = jnp.asarray(np.tile(frequency, LANES // (HEAD_DIM // 2))[None], F32)
    return call(
        prepare_kernel,
        (GENES,),
        [full((1, length)), full((length, width)), full((length, width)), full((1, LANES))],
        [
            pl.BlockSpec(memory_space=pltpu.SMEM),
            rows_of((span, width)),
            rows_of((span, width)),
            rows_of((span, LANES)),
            rows_of((span, LANES)),
        ],
        [
            shape_of((16,), jnp.int32),
            shape_of((length, width), BF16),
            shape_of((length, width), BF16),
            shape_of((length, LANES), F32),
            shape_of((length, LANES), F32),
        ],
        prefetch=0,
        name="prepare",
        cost=(3.3e9, 8e6),
    )(segments, x, c, frequency)


def far_piece(refs, half, dz, dx, dy, dc):
    refs = refs[4 * dc : 4 * dc + 4]
    ref, at = (refs[dx], (dy, dz - 1)) if half == 0 else (refs[2 + dy], (dx, dz - 1))
    return ref.at[(half,) + at] if len(ref.shape) == 5 else ref.at[at]


def load_matrices(at, source, wqkv_ref, wout_ref, sem):
    width = wout_ref.shape[0]
    rows = width // (4 * Z_SIZE)
    own = at_rows((at[0] * 2 + at[1]) * 2 * rows, 2 * rows)
    pltpu.make_async_copy(source[0], wqkv_ref.at[own], sem.at[0]).start()
    pltpu.make_async_copy(source[1], wout_ref.at[own], sem.at[1]).start()

    def put(piece, f, y, c):
        down = at_rows((f * 2 + c) * rows, rows)
        for b in range(4):
            src = piece(b // 2).at[pl.ds((b % 2) * rows, rows)]
            across = at_columns((b % 3) * width + y * COLUMNS, COLUMNS)
            dst = wqkv_ref if b < 3 else wout_ref
            pltpu.make_async_copy(src, dst.at[down, across], sem.at[b // 3]).start()

    for dc in range(2):
        f, _, c = spot(at, 0, 1, 0, dc)
        for y in range(2):
            put(lambda half: source[2 + dc].at[y, half, pl.ds(0, 2 * rows)], f, y, c)

    def one(dz, carry):
        for dx, dy, dc in EVERY:
            put(lambda half: far_piece(source[4:], half, dz, dx, dy, dc), *spot(at, dz, dx, dy, dc))
        return carry

    lax.fori_loop(1, Z_SIZE, one, 0)


def attend_kernel(plan, at, *refs, pieces):
    (xp_ref, cos_ref, sin_ref, g1_ref, b1_ref, bqkv_ref, bout_ref), refs = refs[:7], refs[7:]
    source, refs = (refs[:12], refs[12:]) if pieces else (refs[:2], refs[2:])
    (qkv_ref, o_ref, lse_ref, x1_ref), refs = refs[:4], refs[4:]
    if pieces:
        whole, refs = refs[:2], refs[2:]
    wqkv_ref, wout_ref, mask_ref, sem = refs
    gene = pl.program_id(0)
    span, width = xp_ref.shape

    def wait_both():
        pltpu.make_async_copy(wqkv_ref, wqkv_ref, sem.at[0]).wait()
        pltpu.make_async_copy(wout_ref, wout_ref, sem.at[1]).wait()

    @pl.when(gene == 0)
    def _():
        if pieces:
            load_matrices(at, source, wqkv_ref, wout_ref, sem)
        else:
            pltpu.make_async_copy(source[0], wqkv_ref, sem.at[0]).start()
            pltpu.make_async_copy(source[1], wout_ref, sem.at[1]).start()
        wait_both()
        if pieces:
            pltpu.make_async_copy(wqkv_ref, whole[0], sem.at[0]).start()
            pltpu.make_async_copy(wout_ref, whole[1], sem.at[1]).start()

    x = xp_ref[...].astype(F32)
    xhat, _ = normalize(x)
    a1 = (xhat * g1_ref[...] + b1_ref[...]).astype(BF16)
    cos, sin = cos_ref[...], sin_ref[...]
    for part in range(3):
        base = part * width
        t = nn(a1, wqkv_ref[:, base : base + width]) + bqkv_ref[:, base : base + width]
        for p in range(width // LANES):
            piece = t[:, p * LANES : (p + 1) * LANES]
            if part < 2:
                piece = piece * cos + swap_halves(piece) * sin
            qkv_ref[:, base + p * LANES : base + (p + 1) * LANES] = piece.astype(BF16)
    mask_ref[...] = jnp.where(allowed_pairs(plan, gene, span), 1.0, 0.0)
    masks = head_masks(span)
    for p in range(width // LANES):
        here = slice(p * LANES, (p + 1) * LANES)
        q = qkv_ref[:, p * LANES : (p + 1) * LANES]
        k = qkv_ref[:, width + p * LANES : width + (p + 1) * LANES] * BF16(1.0 / math.sqrt(HEAD_DIM))
        v = qkv_ref[:, 2 * width + p * LANES : 2 * width + (p + 1) * LANES]
        o = jnp.zeros((span, LANES), F32)
        for h in range(2):
            s = nt(keep(masks[h], k), q)
            s = jnp.where(mask_ref[...] > 0.5, s, NEG_FILL)
            peak = jnp.max(s, 0, keepdims=True)
            e = jnp.exp(s - peak)
            total = jnp.sum(e, 0, keepdims=True)
            weights = (e * (1.0 / total)).astype(BF16)
            o = o + tn(weights, keep(masks[h], v))
            lse_ref[pl.ds(2 * p + h, 1), :] = peak + jnp.log(total)
        o_ref[:, here] = o.astype(BF16)
    x1_ref[...] = x + nn(o_ref[...], wout_ref[...]) + bout_ref[...]
    if pieces:

        @pl.when(gene == pl.num_programs(0) - 1)
        def _():
            wait_both()


def attend(plan, at, xp, cos, sin, g1, b1, bqkv, bout, source):
    length, width = xp.shape
    span = length // GENES
    pieces = len(source) == 12
    weights = [shape_of((width, 3 * width), BF16), shape_of((width, width), BF16)]
    got = call(
        functools.partial(attend_kernel, pieces=pieces),
        (GENES,),
        [
            rows_of((span, width)),
            rows_of((span, LANES)),
            rows_of((span, LANES)),
            full((1, width)),
            full((1, width)),
            full((1, 3 * width)),
            full((1, width)),
        ]
        + [ANY] * len(source),
        [
            rows_of((span, 3 * width)),
            rows_of((span, width)),
            pl.BlockSpec((16, span), lambda g, *ids: (0, g)),
            rows_of((span, width)),
        ]
        + [ANY] * (2 if pieces else 0),
        [
            shape_of((length, 3 * width), BF16),
            shape_of((length, width), BF16),
            shape_of((16, length), F32),
            shape_of((length, width), F32),
        ]
        + (weights if pieces else []),
        [
            pltpu.VMEM((width, 3 * width), BF16),
            pltpu.VMEM((width, width), BF16),
            pltpu.VMEM((span, span), F32),
            pltpu.SemaphoreType.DMA((2,)),
        ],
        prefetch=2,
        name="attend",
        cost=(11e9, 20e6),
    )(plan, at, xp, cos, sin, g1, b1, bqkv, bout, *source)
    return got[:4], (got[4:] if pieces else source)


def feed_kernel(at, *refs, block, pieces, steps):
    (x1_ref, c_ref, g2_ref, b2_ref, bup_ref, bdown_ref), refs = refs[:6], refs[6:]
    source, refs = (refs[:12], refs[12:]) if pieces else (refs[:2], refs[2:])
    (out_ref, dx1_ref, da_ref, gbup_ref, sums_ref, first_ref, second_ref), refs = refs[:7], refs[7:]
    a2_ref, acc_ref, dh_ref, gr_ref, du_ref, wups, wdowns, gups, gdowns, load_sem, store_sem = refs
    step = pl.program_id(0)
    length, width = x1_ref.shape
    chunk = bup_ref.shape[1]
    blocks = length // block
    slot = lax.rem(step, 2)
    rows = width // (4 * Z_SIZE)

    def load(j, to):
        if pieces:
            own = at_rows((at[0] * 2 + at[1]) * 2 * rows, 2 * rows)
            src = source[0].at[:, at_columns(j * chunk, chunk)]
            pltpu.make_async_copy(src, wups.at[to, own], load_sem.at[0, to]).start()

            def put_up(piece, f, y, c):
                dst = wups.at[to, at_rows((f * 2 + c) * rows, rows), at_columns(y * COLUMNS, COLUMNS)]
                pltpu.make_async_copy(piece.at[at_rows(j * rows, rows)], dst, load_sem.at[0, to]).start()

            def put_down(piece, x, y, c):
                dst = wdowns.at[to, at_rows((x * 2 + c) * 4 * rows, 4 * rows), at_columns(y * COLUMNS, COLUMNS)]
                pltpu.make_async_copy(piece, dst, load_sem.at[1, to]).start()

            for dc in range(2):
                f, _, c = spot(at, 0, 1, 0, dc)
                for y in range(2):
                    put_up(source[2 + dc].at[y, 0, pl.ds(2 * rows, 4 * rows)], f, y, c)

            def one(dz, carry):
                for dx, dy, dc in EVERY:
                    put_up(far_piece(source[4:], 0, dz, dx, dy, dc), *spot(at, dz, dx, dy, dc))
                return carry

            lax.fori_loop(1, Z_SIZE, one, 0)

            @pl.when(j == at[0])
            def _():
                here = at_rows(at[1] * 8 * rows, 8 * rows)
                pltpu.make_async_copy(source[1], wdowns.at[to, here], load_sem.at[1, to]).start()
                for dc in range(2):
                    _, _, c = spot(at, 0, 1, 0, dc)
                    for y in range(2):
                        put_down(source[2 + dc].at[y, 1, pl.ds(2 * rows, 4 * rows)], 1 - at[1], y, c)

            @pl.when(j != at[0])
            def _():
                back = lax.rem(at[0] + (Z_SIZE - j), Z_SIZE)
                for dx, dy, dc in EVERY:
                    _, y, c = spot(at, back, dx, dy, dc)
                    put_down(far_piece(source[4:], 1, back, dx, dy, dc), lax.bitwise_xor(at[1], dx), y, c)

        else:
            part = source[0].at[:, at_columns(j * chunk, chunk)]
            pltpu.make_async_copy(part, wups.at[to], load_sem.at[0, to]).start()
            part = source[1].at[at_rows(j * chunk, chunk), :]
            pltpu.make_async_copy(part, wdowns.at[to], load_sem.at[1, to]).start()

    def store(j, to):
        if pieces:

            def one(dz, carry):
                for dx, dy, dc in EVERY:
                    f, y, c = spot(at, Z_SIZE - dz, dx, dy, dc)
                    src = gups.at[to, at_rows(f * 2 * rows + c * rows, rows), at_columns(y * COLUMNS, COLUMNS)]
                    dst = (first_ref, second_ref)[dc].at[piece_index(0, dz, dx, dy), at_rows(j * rows, rows)]
                    pltpu.make_async_copy(src, dst, store_sem.at[0, to]).start()
                return carry

            lax.fori_loop(0, Z_SIZE, one, 0)
            ahead = lax.rem(j + Z_SIZE - at[0], Z_SIZE)
            for dx, dy, dc in EVERY:
                f, y, c = spot(at, 0, dx, dy, dc)
                x = lax.bitwise_xor(at[1], dx)
                src = gdowns.at[to, at_rows((x * 2 + c) * 4 * rows, 4 * rows), at_columns(y * COLUMNS, COLUMNS)]
                dst = (first_ref, second_ref)[dc].at[piece_index(1, ahead, dx, dy)]
                pltpu.make_async_copy(src, dst, store_sem.at[1, to]).start()
        else:
            part = first_ref.at[:, at_columns(j * chunk, chunk)]
            pltpu.make_async_copy(gups.at[to], part, store_sem.at[0, to]).start()
            part = second_ref.at[at_rows(j * chunk, chunk), :]
            pltpu.make_async_copy(gdowns.at[to], part, store_sem.at[1, to]).start()

    def wait_load(to):
        pltpu.make_async_copy(wups.at[to], wups.at[to], load_sem.at[0, to]).wait()
        pltpu.make_async_copy(wdowns.at[to], wdowns.at[to], load_sem.at[1, to]).wait()

    def wait_store(to):
        pltpu.make_async_copy(gups.at[to], gups.at[to], store_sem.at[0, to]).wait()
        pltpu.make_async_copy(gdowns.at[to], gdowns.at[to], store_sem.at[1, to]).wait()

    @pl.when(step == 0)
    def _():
        load(0, 0)

        def one(i, carry):
            here = pl.ds(i * block, block)
            xhat, _ = normalize(x1_ref[here, :])
            a2_ref[here, :] = (xhat * g2_ref[...] + b2_ref[...]).astype(BF16)
            return carry

        lax.fori_loop(0, blocks, one, 0)

    wait_load(slot)

    @pl.when(step < steps - 1)
    def _():
        load(step + 1, 1 - slot)

    wup_ref, wdown_ref = wups.at[slot], wdowns.at[slot]

    def one(i, bias_sum):
        here = pl.ds(i * block, block)
        u = nn(a2_ref[here, :], wup_ref[...]) + bup_ref[...]
        phi = 0.5 + 0.5 * lax.erf(u * math.sqrt(0.5))
        slope = phi + u * (jnp.exp(-0.5 * u * u) * (1.0 / math.sqrt(2.0 * math.pi)))
        gr = (u * phi).astype(BF16)
        gr_ref[here, :] = gr
        du = (nt(c_ref[here, :], wdown_ref[...]) * slope).astype(BF16)
        du_ref[here, :] = du
        out = nn(gr, wdown_ref[...])
        dh = nt(du, wup_ref[...])

        @pl.when(step == 0)
        def _():
            acc_ref[here, :] = out
            dh_ref[here, :] = dh

        @pl.when(step > 0)
        def _():
            acc_ref[here, :] += out
            dh_ref[here, :] += dh

        return bias_sum + jnp.sum(du.astype(F32), 0, keepdims=True)

    gbup_ref[...] = lax.fori_loop(0, blocks, one, jnp.zeros((1, chunk), F32))

    @pl.when(step >= 2)
    def _():
        wait_store(slot)

    gdowns[slot] = tn(gr_ref[...], c_ref[...]).astype(BF16)
    gups[slot] = tn(a2_ref[...], du_ref[...]).astype(BF16)
    store(step, slot)

    @pl.when(step == steps - 1)
    def _():
        def one(i, sums):
            here = pl.ds(i * block, block)
            x1 = x1_ref[here, :]
            xhat, scale = normalize(x1)
            out_ref[here, :] = (x1 + acc_ref[here, :] + bdown_ref[...]).astype(BF16)
            dh = dh_ref[here, :]
            c = c_ref[here, :].astype(F32)
            e = dh * g2_ref[...]
            dx1 = c + scale * (
                e - jnp.mean(e, -1, keepdims=True) - xhat * jnp.mean(e * xhat, -1, keepdims=True)
            )
            dx1_ref[here, :] = dx1
            da = dx1.astype(BF16)
            da_ref[here, :] = da
            new = (
                jnp.sum(dh * xhat, 0, keepdims=True),
                jnp.sum(dh, 0, keepdims=True),
                jnp.sum(c, 0, keepdims=True),
                jnp.sum(da.astype(F32), 0, keepdims=True),
            )
            return tuple(a + b for a, b in zip(sums, new))

        sums = lax.fori_loop(0, blocks, one, (jnp.zeros((1, width), F32),) * 4)
        for i in range(4):
            sums_ref[i : i + 1, :] = sums[i]
        wait_store(1 - slot)
        wait_store(slot)


def feed(at, x1, c, g2, b2, bup, bdown, source):
    length, width = x1.shape
    hidden = bup.shape[1]
    steps = 4
    chunk = hidden // steps
    pieces = len(source) == 12
    if pieces:
        rows = width // Z_SIZE
        stored = [shape_of((PIECES, rows, COLUMNS), BF16)] * 2
    else:
        stored = [shape_of((width, hidden), BF16), shape_of((hidden, width), BF16)]
    return call(
        functools.partial(feed_kernel, block=length // 4, pieces=pieces, steps=steps),
        (steps,),
        [
            full((length, width)),
            full((length, width)),
            full((1, width)),
            full((1, width)),
            pl.BlockSpec((1, chunk), lambda j, *ids: (0, j)),
            full((1, width)),
        ]
        + [ANY] * len(source),
        [
            full((length, width)),
            full((length, width)),
            full((length, width)),
            pl.BlockSpec((1, chunk), lambda j, *ids: (0, j)),
            full((8, width)),
            ANY,
            ANY,
        ],
        [
            shape_of((length, width), BF16),
            shape_of((length, width), F32),
            shape_of((length, width), BF16),
            shape_of((1, hidden), F32),
            shape_of((8, width), F32),
        ]
        + stored,
        [
            pltpu.VMEM((length, width), BF16),
            pltpu.VMEM((length, width), F32),
            pltpu.VMEM((length, width), F32),
            pltpu.VMEM((length, chunk), BF16),
            pltpu.VMEM((length, chunk), BF16),
            pltpu.VMEM((2, width, chunk), BF16),
            pltpu.VMEM((2, chunk, width), BF16),
            pltpu.VMEM((2, width, chunk), BF16),
            pltpu.VMEM((2, chunk, width), BF16),
            pltpu.SemaphoreType.DMA((2, 2)),
            pltpu.SemaphoreType.DMA((2, 2)),
        ],
        name="feed",
        cost=(29e9, 40e6),
    )(at, x1, c, g2, b2, bup, bdown, *source)


def attend_back_kernel(
    plan, qkv_ref, da_ref, lse_ref, cos_ref, sin_ref, xp_ref, dx1_ref, g1_ref, wout_ref, wqkv_ref,
    *refs, base,
):
    dqkv_ref, dxp_ref, sums_ref, bias_ref, dout_ref, mask_ref = refs[-6:]
    gene = pl.program_id(0) + base
    span, width = da_ref.shape
    score_scale = 1.0 / math.sqrt(HEAD_DIM)
    dout_ref[...] = nt(da_ref[...], wout_ref[...]).astype(BF16)
    mask_ref[...] = jnp.where(allowed_pairs(plan, gene, span), 1.0, 0.0)
    cos, sin = cos_ref[...], sin_ref[...]
    masks = head_masks(span)

    def back(t):
        return (t * cos - swap_halves(t) * sin).astype(BF16)

    for p in range(width // LANES):
        here = slice(p * LANES, (p + 1) * LANES)
        q = qkv_ref[:, p * LANES : (p + 1) * LANES]
        k = qkv_ref[:, width + p * LANES : width + (p + 1) * LANES] * BF16(score_scale)
        v = qkv_ref[:, 2 * width + p * LANES : 2 * width + (p + 1) * LANES]
        dout = dout_ref[:, here]
        dq = jnp.zeros((span, LANES), F32)
        dk = jnp.zeros((span, LANES), F32)
        dv = jnp.zeros((span, LANES), F32)
        for h in range(2):
            kh = keep(masks[h], k)
            s = nt(kh, q)
            s = jnp.where(mask_ref[...] > 0.5, s, NEG_FILL)
            weights = jnp.exp(s - lse_ref[pl.ds(2 * p + h, 1), :])
            dw = nt(keep(masks[h], v), dout)
            dot = jnp.sum(weights * dw, 0, keepdims=True)
            ds = (weights * (dw - dot)).astype(BF16)
            dv = dv + nn(weights.astype(BF16), keep(masks[h], dout))
            dk = dk + nn(ds, keep(masks[h], q))
            dq = dq + tn(ds, kh)
        dqkv_ref[:, p * LANES : (p + 1) * LANES] = back(dq)
        dqkv_ref[:, width + p * LANES : width + (p + 1) * LANES] = back(dk * score_scale)
        dqkv_ref[:, 2 * width + p * LANES : 2 * width + (p + 1) * LANES] = dv.astype(BF16)

    dh = nt(dqkv_ref[...], wqkv_ref[...])
    xhat, scale = normalize(xp_ref[...].astype(F32))
    e = dh * g1_ref[...]
    dx = dx1_ref[...] + scale * (
        e - jnp.mean(e, -1, keepdims=True) - xhat * jnp.mean(e * xhat, -1, keepdims=True)
    )
    dxp_ref[...] = dx.astype(BF16)
    gain = jnp.sum(dh * xhat, 0, keepdims=True)
    bias = jnp.sum(dh, 0, keepdims=True)

    bqkv = jnp.sum(dqkv_ref[...].astype(F32), 0, keepdims=True)

    @pl.when(gene == base)
    def _():
        sums_ref[0:1, :] = gain
        sums_ref[1:2, :] = bias
        bias_ref[0:1, :] = bqkv

    @pl.when(gene > base)
    def _():
        sums_ref[0:1, :] += gain
        sums_ref[1:2, :] += bias
        bias_ref[0:1, :] += bqkv


def attend_back(plan, qkv, da, lse, cos, sin, xp, dx1, g1, wout, wqkv, base, count, before=()):
    length, width = da.shape
    span = length // GENES
    rows = lambda shape: pl.BlockSpec(shape, lambda g, *ids: (g + base, 0))
    return call(
        functools.partial(attend_back_kernel, base=base),
        (count,),
        [
            rows((span, 3 * width)),
            rows((span, width)),
            pl.BlockSpec((16, span), lambda g, *ids: (0, g + base)),
            rows((span, LANES)),
            rows((span, LANES)),
            rows((span, width)),
            rows((span, width)),
            full((1, width)),
            full((width, width)),
            full((width, 3 * width)),
        ]
        + [ANY] * len(before),
        [rows((span, 3 * width)), rows((span, width)), full((8, width)), full((8, 3 * width))],
        [
            shape_of((length, 3 * width), BF16),
            shape_of((length, width), BF16),
            shape_of((8, width), F32),
            shape_of((8, 3 * width), F32),
        ],
        [pltpu.VMEM((span, width), BF16), pltpu.VMEM((span, span), F32)],
        name="attend_back",
        cost=(4e9 * count, 6e6 * count),
        aliases={11 + i: i for i in range(len(before))},
    )(plan, qkv, da, lse, cos, sin, xp, dx1, g1, wout, wqkv, *before)


def grads_kernel(at, *refs, pieces):
    (xp_ref, g1_ref, b1_ref, o_ref, da_ref, dqkv_ref), refs = refs[:6], refs[6:]
    if pieces:
        vectors, refs = refs[:8], refs[8:]
        first_ref, second_ref, a1_ref, grad_ref, sem, small_ref, small_sem = refs
    else:
        first_ref, second_ref, a1_ref, grad_ref, sem = refs
    step = pl.program_id(0)
    width = xp_ref.shape[1]
    slot = lax.rem(step, 2)
    rows = width // (4 * Z_SIZE)

    def wait(to):
        pltpu.make_async_copy(grad_ref.at[to], grad_ref.at[to], sem.at[to]).wait()

    def store(half, base, to):
        def one(dz, carry):
            for dx, dy, dc in EVERY:
                f, y, c = spot(at, Z_SIZE - dz, dx, dy, dc)
                src = grad_ref.at[to, at_rows(f * 2 * rows + c * rows, rows), at_columns(y * COLUMNS, COLUMNS)]
                dst = (first_ref, second_ref)[dc].at[piece_index(half, dz, dx, dy), pl.ds(base * rows, rows)]
                pltpu.make_async_copy(src, dst, sem.at[to]).start()
            return carry

        lax.fori_loop(0, Z_SIZE, one, 0)

    def pack():
        small_ref[...] = jnp.zeros_like(small_ref)
        shards = 2 * Z_SIZE
        columns = []
        for ref in vectors:
            size = ref.shape[1] // shards
            whole = jnp.broadcast_to(ref[...], (shards, ref.shape[1]))
            mask = iota(whole.shape, 1) // size == iota(whole.shape, 0)
            own = jnp.where(mask, whole, 0.0).astype(BF16)
            columns.append(nt(own, spread(size, ref.shape[1])).astype(BF16))
        rows = jnp.concatenate(columns, 1).astype(F32)
        for f in range(shards):
            for i in range(4):
                part = rows[f : f + 1, i * COLUMNS : (i + 1) * COLUMNS]
                small_ref[f, i // 2, i % 2, 0] = jnp.broadcast_to(part, (8, COLUMNS)).astype(BF16)

    def smalls(act):
        def one(dz, carry):
            for dx, dy, dc in EVERY:
                f, y, c = spot(at, Z_SIZE - dz, dx, dy, dc)
                for half in range(2):
                    src = small_ref.at[f, y, c, half]
                    dst = (first_ref, second_ref)[dc].at[piece_index(half, dz, dx, dy), pl.ds(2 * rows, 8)]
                    act(pltpu.make_async_copy(src, dst, small_sem))
            return carry

        lax.fori_loop(0, Z_SIZE, one, 0)

    @pl.when(step >= 2)
    def _():
        wait(slot)

    for j in range(4):

        @pl.when(step == j)
        def _(j=j):
            if j == 0:
                if pieces:
                    pack()
                    smalls(lambda copy: copy.start())
                xhat, _ = normalize(xp_ref[...].astype(F32))
                a1_ref[...] = (xhat * g1_ref[...] + b1_ref[...]).astype(BF16)
            if j < 3:
                grad_ref[j % 2] = tn(a1_ref[...], dqkv_ref[...]).astype(BF16)
            else:
                grad_ref[j % 2] = tn(o_ref[...], da_ref[...]).astype(BF16)
            if pieces:
                store(j // 2, j % 2, j % 2)
            elif j < 3:
                dst = first_ref.at[:, pl.ds(j * width, width)]
                pltpu.make_async_copy(grad_ref.at[j % 2], dst, sem.at[j % 2]).start()
            else:
                pltpu.make_async_copy(grad_ref.at[j % 2], second_ref, sem.at[j % 2]).start()
            if j == 3:
                wait(0)
                wait(1)
                if pieces:
                    smalls(lambda copy: copy.wait())


def grads(at, xp, g1, b1, o, da, dqkv, vectors):
    length, width = xp.shape
    pieces = bool(vectors)
    if pieces:
        rows = width // (2 * Z_SIZE) + 8
        stored = [shape_of((PIECES, rows, COLUMNS), BF16)] * 2
    else:
        stored = [shape_of((width, 3 * width), BF16), shape_of((width, width), BF16)]
    return call(
        functools.partial(grads_kernel, pieces=pieces),
        (4,),
        [
            full((length, width)),
            full((1, width)),
            full((1, width)),
            full((length, width)),
            full((length, width)),
            pl.BlockSpec((length, width), lambda j, *ids: (0, jnp.minimum(j, 2))),
        ]
        + [full(v.shape) for v in vectors],
        [ANY, ANY],
        stored,
        [
            pltpu.VMEM((length, width), BF16),
            pltpu.VMEM((2, width, width), BF16),
            pltpu.SemaphoreType.DMA((2,)),
        ]
        + (
            [pltpu.VMEM((2 * Z_SIZE, 2, 2, 2, 8, COLUMNS), BF16), pltpu.SemaphoreType.DMA]
            if pieces
            else []
        ),
        name="grads",
        cost=(5e9, 12e6),
    )(at, xp, g1, b1, o, da, dqkv, *vectors)


def restore_kernel(plan, outp_ref, dxp_ref, out_ref, dx_ref):
    span, width = out_ref.shape
    slots = iota((1, span), 1)
    source = jnp.concatenate([source_of_slots(plan, g, slots) for g in range(GENES)], 1)
    codon = iota((span, outp_ref.shape[0]), 0) + pl.program_id(0) * span
    pick = jnp.where(codon == source, 1.0, 0.0).astype(BF16)
    out_ref[...] = nn(pick, outp_ref[...]).astype(BF16)
    dx_ref[...] = nn(pick, dxp_ref[...]).astype(BF16)


def restore(plan, outp, dxp):
    length, width = outp.shape
    span = length // GENES
    return call(
        restore_kernel,
        (GENES,),
        [full((length, width)), full((length, width))],
        [rows_of((span, width))] * 2,
        [shape_of((length, width), BF16)] * 2,
        name="restore",
        cost=(3.3e9, 8e6),
    )(plan, outp, dxp)


def deliver_kernel(at, mine1, other1, mine2, other2, *out):
    wqkv, wout, wup, wdown = out[:4]
    vectors, row_ref = out[4:12], out[12]
    width = wout.shape[1]
    rows = wout.shape[0] // 2
    for dc, (one, two) in enumerate(((mine1, mine2), (other1, other2))):
        c = lax.bitwise_xor(at[3], dc)
        here = pl.ds(pl.multiple_of(c * rows, 8), rows)
        for y in range(2):
            for b in range(4):
                ref, base = (wqkv, b * width) if b < 3 else (wout, 0)
                start = base + y * COLUMNS
                piece = one[y, b // 2, (b % 2) * rows : (b % 2 + 1) * rows, :]
                ref[here, start : start + COLUMNS] = piece.astype(F32)
                start = b * width + y * COLUMNS
                wup[here, start : start + COLUMNS] = two[y, 0, b * rows : (b + 1) * rows, :].astype(F32)
            down = pl.ds(pl.multiple_of(c * 4 * rows, 8), 4 * rows)
            wdown[down, y * COLUMNS : (y + 1) * COLUMNS] = two[y, 1].astype(F32)
            start = at_columns((y * 2 + c) * COLUMNS, COLUMNS)
            row_ref[:, start] = one[y, 0, 2 * rows : 2 * rows + 8, :].astype(F32)
    for ref, start in zip(vectors, SLOTS):
        ref[...] = row_ref[0:1, start : start + ref.shape[0]].reshape(ref.shape[0])


def deliver(at, mine1, other1, mine2, other2, sizes):
    rows = mine2.shape[2] // 4
    width = 2 * COLUMNS
    shapes = [(2 * rows, 3 * width), (2 * rows, width), (2 * rows, 4 * width), (8 * rows, width)]
    shapes += [(n,) for n in sizes]
    return call(
        deliver_kernel,
        (1,),
        [full(v.shape) for v in (mine1, other1, mine2, other2)],
        [full(s) for s in shapes],
        [shape_of(s, F32) for s in shapes],
        [pltpu.VMEM((8, PACKED), F32)],
        name="deliver",
        cost=(0, 6e6),
    )(at, mine1, other1, mine2, other2)


def gather(shard):
    return lax.all_gather(shard, "fsdp", axis=0, tiled=True)


def reduce_rows(grad):
    part = lax.psum_scatter(grad, "fsdp", scatter_dimension=0, tiled=True)
    return lax.psum(part.astype(BF16), "replica").astype(F32)


def low(value):
    return value.astype(BF16)


def add(*values):
    total = values[0].astype(F32)
    for v in values[1:]:
        total = total + v.astype(F32)
    return total


def to_z(arrays):
    arrays = arrays if isinstance(arrays, list) else [arrays] * 3
    return [move(v, ALONG_Z[d]) for d, v in zip((1, 2, 3), arrays)]


def over_x(array):
    return move(array, ACROSS_X)


def over_y(array):
    return move(array, ACROSS_Y)


def over_core(array):
    return move(array, ACROSS_CORE)


def stack(arrays):
    return jnp.stack(list(arrays))


class Sum:
    def __init__(self, kept, got):
        self.kept, self.got, self.more = kept, got, {}

    def near(self, start, stop):
        return add(self.kept[start:stop], self.got[start:stop])

    def plane_one(self):
        return low(self.near(6, 12)), low(self.near(18, 24)), low(self.near(28, 32))

    def plane_two(self, by_x, by_y):
        self.first = add(self.near(0, 6), by_x)
        self.second = add(self.near(12, 18), by_y)
        return low(self.first[3:]), low(self.second[3:])

    def along_z(self, by_y, by_x):
        first, second = add(self.first[:3], by_y), add(self.second[:3], by_x)
        return [low(stack([first[d], second[d]])) for d in range(Z_SIZE - 1)]

    def across_y(self, by_z, side):
        own = add(self.near(24, 28), side)
        return low(stack([add(own[:2], *by_z), own[2:]]))


def settle(at, part, got):
    mine = low(add(part[0], got[1]))
    other = low(add(got[0], part[1]))
    return jnp.where(at[2] == 0, stack([mine, other]), stack([other, mine]))


def body(
    layer_input, cotangent, segment_ids, pad_mask, ln1_gain, ln1_bias, w_qkv, b_qkv, w_out, b_out,
    ln2_gain, ln2_bias, w_up, b_up, w_down, b_down, *, tuned,
):
    vectors = (ln1_gain, ln1_bias, b_qkv, b_out, ln2_gain, ln2_bias, b_up, b_down)
    sizes = [v.shape[0] for v in vectors]
    x, c = layer_input[0], cotangent[0]
    if tuned:
        at = place()
        near1, near2, side = quarters(at, w_qkv, w_out, w_up, w_down, vectors)
        near1, near2, side, x = tie((near1, near2, side, x))
        z1 = to_z(near1)
        far_side = over_x(side)
        z2_one = move(near2, ALONG_Z[1])
        prepared = prepare(segment_ids, x, c)
        z1, z2_one, prepared = tie((z1, z2_one, prepared))
        plan, xp, cp, cos, sin = prepared

        count = near1.shape[1] - 8
        first1, second1 = stack(q[0, :count] for q in z1), stack(q[1] for q in z1)
        rows = stack(q[0, count:] for q in [near1] + z1)
        first1, second1, near2 = tie((first1, second1, near2))
        first_y, second_x = over_y(first1), over_x(second1)
        z2_three = move(near2, ALONG_Z[3])
        first_y, second_x, z2_three, near2, far_side = tie((first_y, second_x, z2_three, near2, far_side))

        first1, second1 = stack([first1, first_y]), stack([second1, second_x])[:, :, :count]
        far_rows = jnp.concatenate([far_side[0, :1, 3 * count :], second_x[:, count:]])
        first1, second1, rows, far_rows, near2 = tie((first1, second1, rows, far_rows, near2))
        far_first1, far_second1 = over_x(first1), over_y(second1)
        z2 = [z2_one, move(near2, ALONG_Z[2]), z2_three]
        params = unpack(at, rows, far_rows, sizes)
        far_first1, far_second1, params, z2, far_side = tie((far_first1, far_second1, params, z2, far_side))

        first2, second2 = (stack(q[h] for q in z2) for h in range(2))
        near_core1 = stack([first1, second1])
        far_first1, far_second1, near_core1, first2, second2 = tie(
            (far_first1, far_second1, near_core1, first2, second2)
        )
        far_core1 = over_core(far_first1), over_core(far_second1)
        near_core1 = over_core(near_core1)
        first_y, second_x = over_y(first2), over_x(second2)
        core_side = over_core(far_side)
        first_y, second_x, far_core1, near_core1, core_side = tie(
            (first_y, second_x, far_core1, near_core1, core_side)
        )

        attention = (
            w_qkv, w_out, far_side, core_side, first1, far_first1, second1, far_second1,
            near_core1, far_core1[0], near_core1, far_core1[1],
        )
        first2, second2 = stack([first2, first_y]), stack([second2, second_x])
        first2, second2, attention, params, plan = tie((first2, second2, attention, params, plan))
        far_first2, far_second2 = over_x(first2), over_y(second2)
        core2 = [over_core(v) for v in (first2, second2)]
    else:
        at = jnp.zeros((4,), jnp.int32)
        plan, xp, cp, cos, sin = prepare(segment_ids, x, c)
        params = [gather(v[None]).reshape(1, -1).astype(F32) for v in vectors]
        attention = gather(w_qkv), gather(w_out)
        forward = gather(w_up), gather(w_down)
    g1, b1, bqkv, bout, g2, b2, bup, bdown = params
    (qkv, o, lse, x1), (wqkv, wout) = attend(plan, at, xp, cos, sin, g1, b1, bqkv, bout, attention)
    if tuned:
        far_first2, far_second2, core2, x1 = tie((far_first2, far_second2, core2, x1))
        far_core2 = over_core(far_first2), over_core(far_second2)
        forward = (
            w_up, w_down, far_side, core_side, first2, far_first2, second2, far_second2,
            core2[0], far_core2[0], core2[1], far_core2[1],
        )
    outp, dx1, da, gbup, sums2, *parts2 = feed(at, x1, cp, g2, b2, bup, bdown, forward)
    back = functools.partial(attend_back, plan, qkv, da, lse, cos, sin, xp, dx1, g1, wout, wqkv)
    half = GENES // 2
    if tuned:
        kept2, sent2 = parts2
        got2 = over_core(sent2)
        dqkv, dxp, *sums_low = back(0, half)
        got2, dqkv = tie((got2, dqkv))
        group2 = Sum(kept2, got2)
        to_x, to_y, side2, dqkv = tie(group2.plane_one() + (dqkv,))
        by_x, by_y = over_x(to_x), over_y(to_y)
        dqkv, dxp, *sums_high = back(half, half, (dqkv, dxp))
        by_x, by_y, dqkv = tie((by_x, by_y, dqkv))
        to_y, to_x = group2.plane_two(by_x, by_y)
        to_y, to_x, side2, dqkv = tie((to_y, to_x, side2, dqkv))
        by_y, by_x, by_side2 = over_y(to_y), over_x(to_x), over_x(side2)
    else:
        dqkv, dxp, *sums_low = back(0, half)
        dqkv, dxp, *sums_high = back(half, half, (dqkv, dxp))
    sums1, sumsb = (a + b for a, b in zip(sums_low, sums_high))
    row = lambda array, i: array[i : i + 1]
    small = [
        row(sums1, 0), row(sums1, 1), row(sumsb, 0), row(sums2, 3), row(sums2, 0), row(sums2, 1), gbup, row(sums2, 2),
    ]
    parts1 = grads(at, xp, g1, b1, o, da, dqkv, small if tuned else ())
    if tuned:
        by_y, by_x, by_side2, parts1 = tie((by_y, by_x, by_side2, parts1))
        kept1, sent1 = parts1
        to_z2 = group2.along_z(by_y, by_x)
        to_z2, sent1 = tie((to_z2, sent1))
        got1 = over_core(sent1)
        z2 = to_z(to_z2)
        got1 = tie(got1)
        group1 = Sum(kept1, got1)
        to_x, to_y, side1 = tie(group1.plane_one())
        by_x, by_y = over_x(to_x), over_y(to_y)
        by_x, by_y = tie((by_x, by_y))
        to_y, to_x = tie(group1.plane_two(by_x, by_y))
        by_y, by_x = over_y(to_y), over_x(to_x)
        by_y, by_x, z2 = tie((by_y, by_x, z2))
        to_z1 = group1.along_z(by_y, by_x)
        part2 = group2.across_y(z2, by_side2)
        to_z1, side1, part2, outp, dxp = tie((to_z1, side1, part2, outp, dxp))
        z1 = to_z(to_z1)
        by_side1, by_part2 = over_x(side1), over_y(part2)
        layer_out, input_grad = restore(plan, outp, dxp)
        z1, by_side1, by_part2, layer_out, input_grad = tie((z1, by_side1, by_part2, layer_out, input_grad))
        part1 = group1.across_y(z1, by_side1)
        final2 = settle(at, part2, by_part2)
        part1, final2 = tie((part1, final2))
        by_part1, other2 = over_y(part1), over_core(final2)
        final1 = settle(at, part1, by_part1)
        other1 = over_core(final1)
        wqkv, wout, wup, wdown, *small = deliver(at, final1, other1, final2, other2, sizes)
    else:
        layer_out, input_grad = restore(plan, outp, dxp)
        wqkv, wout = map(reduce_rows, parts1)
        wup, wdown = map(reduce_rows, parts2)
        small = [reduce_rows(v.reshape(-1)) for v in small]
    dg1, db1, dbqkv, dbout, dg2, db2, dbup, dbdown = small
    return (
        layer_out[None], input_grad[None], dg1, db1, wqkv, dbqkv, wout, dbout, dg2, db2,
        wup, dbup, wdown, dbdown,
    )


def solution(mesh):
    rows = ("fsdp", "replica")
    by_row = P(rows, None, None)
    vector, matrix = P("fsdp"), P("fsdp", None)
    params = (
        vector, vector, matrix, vector, matrix, vector, vector, vector, matrix, vector, matrix, vector,
    )
    in_specs = (by_row, by_row, P(rows, None), P(rows, None)) + params
    out_specs = (by_row, by_row) + params
    return jax.shard_map(
        functools.partial(body, tuned=tuned_mesh(mesh)),
        mesh=mesh, in_specs=in_specs, out_specs=out_specs, check_vma=False,
    )
```

```python
import functools
import math

import jax
import jax.numpy as jnp
import numpy as np
from jax import lax
from jax.experimental import pallas as pl
from jax.experimental.pallas import tpu as pltpu
from jax.sharding import PartitionSpec as P

HEADS = 12
HEAD_DIM = 64
GENES = 4
LANES = 128
EPSILON = 1e-05
NEG_FILL = -1000000000.0
F32 = jnp.float32
BF16 = jnp.bfloat16
MIB = 1 << 20
UNROLL_F = 6
UNROLL_B = 2


def nn(left, right):
    return lax.dot_general(left, right, (((1,), (0,)), ((), ())), preferred_element_type=F32)


def nt(left, right):
    return lax.dot_general(left, right, (((1,), (1,)), ((), ())), preferred_element_type=F32)


def tn(left, right):
    return lax.dot_general(left, right, (((0,), (0,)), ((), ())), preferred_element_type=F32)


def iota(shape, axis):
    return lax.broadcasted_iota(jnp.int32, shape, axis)


def full(shape):
    return pl.BlockSpec(shape, lambda *ids: (0,) * len(shape))


def rows_of(shape):
    return pl.BlockSpec(shape, lambda g, *ids: (g,) + (0,) * (len(shape) - 1))


def call(kernel, grid, in_specs, out_specs, out_shape, scratch=(), vmem=60, prefetch=1, name=None, cost=None, aliases=None):
    return pl.pallas_call(
        kernel,
        grid_spec=pltpu.PrefetchScalarGridSpec(
            num_scalar_prefetch=prefetch,
            grid=grid,
            in_specs=in_specs,
            out_specs=out_specs,
            scratch_shapes=list(scratch),
        ),
        out_shape=out_shape,
        input_output_aliases=aliases or {},
        compiler_params=pltpu.CompilerParams(
            dimension_semantics=("arbitrary",) * len(grid), vmem_limit_bytes=vmem * MIB
        ),
        name=name,
        cost_estimate=cost and pl.CostEstimate(flops=int(cost[0]), bytes_accessed=int(cost[1]), transcendentals=0),
    )


def shape_of(shape, dtype):
    return jax.ShapeDtypeStruct(shape, dtype)


def normalize(x):
    mean = jnp.mean(x, -1, keepdims=True)
    centered = x - mean
    scale = lax.rsqrt(jnp.mean(centered * centered, -1, keepdims=True) + EPSILON)
    return centered * scale, scale


def swap_halves(t):
    low = (iota(t.shape, 1) % HEAD_DIM) < HEAD_DIM // 2
    return jnp.where(
        low, pltpu.roll(t, LANES - HEAD_DIM // 2, 1), pltpu.roll(t, HEAD_DIM // 2, 1)
    )


def head_masks(rows):
    lane = iota((rows, LANES), 1)
    return [(lane < HEAD_DIM), (lane >= HEAD_DIM)]


def allowed_pairs(plan, gene, span):
    length = plan[gene]
    i, j = iota((span, span), 0), iota((span, span), 1)
    return ((i < length) & (j < length)) | (i == j)


def keep(mask, value):
    return jnp.where(mask, value, jnp.zeros_like(value))


Z_SIZE = 4
COLUMNS = 384
AXES = ("fsdp", "replica")
ANY = pl.BlockSpec(memory_space=pl.ANY)
PIECES = 32
EVERY = [(dx, dy, dc) for dx in range(2) for dy in range(2) for dc in range(2)]
SLOTS = (0, 128, 256, 640, 768, 896, 1024, 1408)
PACKED = 1536


def tuned_mesh(mesh):
    return mesh.shape["fsdp"] == 2 * Z_SIZE and mesh.shape["replica"] == 4


def pairs(step):
    out = []
    for z in range(Z_SIZE):
        for x in range(2):
            for y in range(2):
                for c in range(2):
                    tz, tx, ty, tc = step(z, x, y, c)
                    out.append((((z * 2 + x) * 2 + y) * 2 + c, (((tz % Z_SIZE) * 2 + tx) * 2 + ty) * 2 + tc))
    return out


ACROSS_X = pairs(lambda z, x, y, c: (z, 1 - x, y, c))
ACROSS_Y = pairs(lambda z, x, y, c: (z, x, 1 - y, c))
ACROSS_CORE = pairs(lambda z, x, y, c: (z, x, y, 1 - c))
ALONG_Z = [pairs(functools.partial(lambda d, z, x, y, c: (z + d, x, y, c), d)) for d in range(Z_SIZE)]
tie = lax.optimization_barrier


def move(array, table):
    return lax.ppermute(array, AXES, table)


def place():
    f, r = lax.axis_index("fsdp"), lax.axis_index("replica")
    return jnp.stack([f // 2, f % 2, r // 2, r % 2]).astype(jnp.int32)


def spot(at, dz, dx, dy, dc):
    z = lax.rem(at[0] + (Z_SIZE - dz), Z_SIZE)
    return z * 2 + lax.bitwise_xor(at[1], dx), lax.bitwise_xor(at[2], dy), lax.bitwise_xor(at[3], dc)


def piece_index(half, dz, dx, dy):
    return (16 + dy * 8 + dx * 4 if half else dx * 8 + dy * 4) + dz


def at_rows(start, size):
    return pl.ds(pl.multiple_of(start, 16), size)


def at_columns(start, size):
    return pl.ds(pl.multiple_of(start, LANES), size)


def quarters_kernel(at, *refs):
    wqkv, wout, wup, wdown = refs[:4]
    vectors, (near1, near2, side, packed) = refs[4:12], refs[12:]
    width = wout.shape[1]
    rows = wout.shape[0] // 2
    packed[...] = jnp.zeros_like(packed)
    for ref, start in zip(vectors, SLOTS):
        packed[:, start : start + ref.shape[0]] = ref[...].reshape(1, -1)
    tail = jnp.zeros((8, COLUMNS), BF16)
    for i in range(4):
        part = jnp.broadcast_to(packed[:, i * COLUMNS : (i + 1) * COLUMNS], (8, COLUMNS))
        tail = jnp.where(iota((8, COLUMNS), 0) == i, part, tail)
    mine = at_rows(at[3] * rows, rows)
    for y in range(2):
        for b in range(4):
            ref, base = (wqkv, b * width) if b < 3 else (wout, 0)
            start = base + y * COLUMNS
            side[y, b // 2, (b % 2) * rows : (b % 2 + 1) * rows, :] = ref[mine, start : start + COLUMNS]
            start = b * width + y * COLUMNS
            side[y, 0, (2 + b) * rows : (3 + b) * rows, :] = wup[mine, start : start + COLUMNS]
        here = slice(y * COLUMNS, (y + 1) * COLUMNS)
        side[y, 1, 2 * rows : 6 * rows, :] = wdown[at_rows(at[3] * 4 * rows, 4 * rows), here]
        for h in range(2):
            side[y, h, 6 * rows : 6 * rows + 8, :] = tail
    near1[:, 0 : 2 * rows, :] = side[at[2], :, 0 : 2 * rows, :]
    near2[...] = side[at[2], :, 2 * rows : 6 * rows, :]
    for h in range(2):
        near1[h, 2 * rows : 2 * rows + 8, :] = tail


def quarters(at, wqkv, wout, wup, wdown, vectors):
    rows = wqkv.shape[0] // 2
    shapes = [
        (2, 2 * rows + 8, COLUMNS),
        (2, 4 * rows, COLUMNS),
        (2, 2, 6 * rows + 8, COLUMNS),
    ]
    matrices = (wqkv, wout, wup, wdown)
    return call(
        quarters_kernel,
        (1,),
        [full(v.shape) for v in matrices + tuple(vectors)],
        [full(s) for s in shapes],
        [shape_of(s, BF16) for s in shapes],
        [pltpu.VMEM((1, PACKED), BF16)],
        name="quarters",
        cost=(0, 6e6),
    )(at, *matrices, *vectors)


def rel_mask(at, columns, size):
    row = iota((2 * Z_SIZE, columns), 0)
    z = (at[0] + Z_SIZE - row % Z_SIZE) % Z_SIZE
    shard = z * 2 + jnp.where(row < Z_SIZE, at[1], 1 - at[1])
    return iota((2 * Z_SIZE, columns), 1) // size == shard


def spread(size, columns):
    lanes = -(-size // LANES) * LANES
    lane, column = iota((lanes, columns), 0), iota((lanes, columns), 1)
    return jnp.where(column % size == lane, 1.0, 0.0).astype(BF16)


def unpack_kernel(at, near_ref, far_ref, *refs):
    out, row_ref = refs[:8], refs[8]
    for x_bit, rows in enumerate((near_ref, far_ref)):
        for d in range(Z_SIZE):
            here = x_bit * Z_SIZE + d
            for i in range(4):
                row_ref[here : here + 1, i * COLUMNS : (i + 1) * COLUMNS] = rows[d, i : i + 1, :].astype(F32)
    for ref, start in zip(out, SLOTS):
        columns = ref.shape[1]
        size = columns // (2 * Z_SIZE)
        table = spread(size, columns)
        got = nn(row_ref[:, start : start + table.shape[0]].astype(BF16), table)
        ref[...] = jnp.sum(jnp.where(rel_mask(at, columns, size), got, 0.0), 0, keepdims=True)


def unpack(at, near, far, sizes):
    shapes = [(1, n * 2 * Z_SIZE) for n in sizes]
    return call(
        unpack_kernel,
        (1,),
        [full(near.shape)] * 2,
        [full(s) for s in shapes],
        [shape_of(s, F32) for s in shapes],
        [pltpu.VMEM((2 * Z_SIZE, PACKED), F32)],
        name="unpack",
        cost=(1e8, 1e5),
    )(at, near, far)


def plan_of(segments):
    lengths = [jnp.sum(jnp.where(segments == g, 1.0, 0.0)).astype(jnp.int32) for g in range(GENES)]
    span = segments.size // GENES
    starts, before, start, free = [], [], 0, 0
    for g in range(GENES):
        starts.append(start)
        before.append(free)
        start = start + lengths[g]
        free = free + span - lengths[g]
    return [jnp.asarray(v, jnp.int32) for v in lengths + starts + before + [start]]


def source_of_slots(plan, gene, slots):
    length = plan[gene]
    return jnp.where(
        slots < length,
        plan[GENES + gene] + slots,
        plan[3 * GENES] + plan[2 * GENES + gene] + slots - length,
    )


def prepare_kernel(seg_ref, x_ref, c_ref, freq_ref, plan_ref, xp_ref, cp_ref, cos_ref, sin_ref):
    gene = pl.program_id(0)
    span = xp_ref.shape[0]
    length = x_ref.shape[0]

    @pl.when(gene == 0)
    def _():
        for i, v in enumerate(plan_of(seg_ref[...])):
            plan_ref[i] = v

    slots = iota((span, 1), 0)
    source = source_of_slots(plan_ref, gene, slots)
    pick = jnp.where(iota((span, length), 1) == source, 1.0, 0.0).astype(BF16)
    xp_ref[...] = nn(pick, x_ref[...]).astype(BF16)
    cp_ref[...] = nn(pick, c_ref[...]).astype(BF16)
    start = jnp.where(slots < plan_ref[gene], plan_ref[GENES + gene], plan_ref[3 * GENES])
    angle = (source - start).astype(F32) * freq_ref[...]
    low = iota((span, LANES), 1) % HEAD_DIM < HEAD_DIM // 2
    cos_ref[...] = jnp.cos(angle)
    sine = jnp.sin(angle)
    sin_ref[...] = jnp.where(low, -sine, sine)


def prepare(segments, x, c):
    length, width = x.shape
    span = length // GENES
    frequency = np.power(10000.0, np.arange(HEAD_DIM // 2) * (-2.0 / HEAD_DIM))
    frequency = jnp.asarray(np.tile(frequency, LANES // (HEAD_DIM // 2))[None], F32)
    return call(
        prepare_kernel,
        (GENES,),
        [full((1, length)), full((length, width)), full((length, width)), full((1, LANES))],
        [
            pl.BlockSpec(memory_space=pltpu.SMEM),
            rows_of((span, width)),
            rows_of((span, width)),
            rows_of((span, LANES)),
            rows_of((span, LANES)),
        ],
        [
            shape_of((16,), jnp.int32),
            shape_of((length, width), BF16),
            shape_of((length, width), BF16),
            shape_of((length, LANES), F32),
            shape_of((length, LANES), F32),
        ],
        prefetch=0,
        name="prepare",
        cost=(3.3e9, 8e6),
    )(segments, x, c, frequency)


def far_piece(refs, half, dz, dx, dy, dc):
    refs = refs[4 * dc : 4 * dc + 4]
    ref, at = (refs[dx], (dy, dz - 1)) if half == 0 else (refs[2 + dy], (dx, dz - 1))
    return ref.at[(half,) + at] if len(ref.shape) == 5 else ref.at[at]


def load_matrices(at, source, wqkv_ref, wout_ref, sem):
    width = wout_ref.shape[0]
    rows = width // (4 * Z_SIZE)
    own = at_rows((at[0] * 2 + at[1]) * 2 * rows, 2 * rows)
    pltpu.make_async_copy(source[0], wqkv_ref.at[own], sem.at[0]).start()
    pltpu.make_async_copy(source[1], wout_ref.at[own], sem.at[1]).start()

    def put(piece, f, y, c):
        down = at_rows((f * 2 + c) * rows, rows)
        for b in range(4):
            src = piece(b // 2).at[pl.ds((b % 2) * rows, rows)]
            across = at_columns((b % 3) * width + y * COLUMNS, COLUMNS)
            dst = wqkv_ref if b < 3 else wout_ref
            pltpu.make_async_copy(src, dst.at[down, across], sem.at[b // 3]).start()

    for dc in range(2):
        f, _, c = spot(at, 0, 1, 0, dc)
        for y in range(2):
            put(lambda half: source[2 + dc].at[y, half, pl.ds(0, 2 * rows)], f, y, c)

    def one(dz, carry):
        for dx, dy, dc in EVERY:
            put(lambda half: far_piece(source[4:], half, dz, dx, dy, dc), *spot(at, dz, dx, dy, dc))
        return carry

    lax.fori_loop(1, Z_SIZE, one, 0)


def attend_kernel(plan, at, *refs, pieces):
    (xp_ref, cos_ref, sin_ref, g1_ref, b1_ref, bqkv_ref, bout_ref), refs = refs[:7], refs[7:]
    source, refs = (refs[:12], refs[12:]) if pieces else (refs[:2], refs[2:])
    (qkv_ref, o_ref, lse_ref, x1_ref), refs = refs[:4], refs[4:]
    if pieces:
        whole, refs = refs[:2], refs[2:]
    wqkv_ref, wout_ref, mask_ref, sem = refs
    gene = pl.program_id(0)
    span, width = xp_ref.shape

    def wait_both():
        pltpu.make_async_copy(wqkv_ref, wqkv_ref, sem.at[0]).wait()
        pltpu.make_async_copy(wout_ref, wout_ref, sem.at[1]).wait()

    @pl.when(gene == 0)
    def _():
        if pieces:
            load_matrices(at, source, wqkv_ref, wout_ref, sem)
        else:
            pltpu.make_async_copy(source[0], wqkv_ref, sem.at[0]).start()
            pltpu.make_async_copy(source[1], wout_ref, sem.at[1]).start()
        wait_both()
        if pieces:
            pltpu.make_async_copy(wqkv_ref, whole[0], sem.at[0]).start()
            pltpu.make_async_copy(wout_ref, whole[1], sem.at[1]).start()

    x = xp_ref[...].astype(F32)
    xhat, _ = normalize(x)
    a1 = (xhat * g1_ref[...] + b1_ref[...]).astype(BF16)
    cos, sin = cos_ref[...], sin_ref[...]
    for part in range(3):
        base = part * width
        t = nn(a1, wqkv_ref[:, base : base + width]) + bqkv_ref[:, base : base + width]
        for p in range(width // LANES):
            piece = t[:, p * LANES : (p + 1) * LANES]
            if part < 2:
                piece = piece * cos + swap_halves(piece) * sin
            qkv_ref[:, base + p * LANES : base + (p + 1) * LANES] = piece.astype(BF16)
    mask_ref[...] = jnp.where(allowed_pairs(plan, gene, span), 1.0, 0.0)
    masks = head_masks(span)
    def pair(p, carry):
        part = lambda i: at_columns(i * width + p * LANES, LANES)
        q = qkv_ref[:, part(0)]
        k = qkv_ref[:, part(1)] * BF16(1.0 / math.sqrt(HEAD_DIM))
        v = qkv_ref[:, part(2)]
        o = jnp.zeros((span, LANES), F32)
        for h in range(2):
            s = nt(keep(masks[h], k), q)
            s = jnp.where(mask_ref[...] > 0.5, s, NEG_FILL)
            peak = jnp.max(s, 0, keepdims=True)
            e = jnp.exp(s - peak)
            total = jnp.sum(e, 0, keepdims=True)
            weights = (e * (1.0 / total)).astype(BF16)
            o = o + tn(weights, keep(masks[h], v))
            lse_ref[pl.ds(2 * p + h, 1), :] = peak + jnp.log(total)
        o_ref[:, part(0)] = o.astype(BF16)
        return carry

    lax.fori_loop(0, width // LANES, pair, 0, unroll=UNROLL_F)
    x1_ref[...] = x + nn(o_ref[...], wout_ref[...]) + bout_ref[...]
    if pieces:

        @pl.when(gene == pl.num_programs(0) - 1)
        def _():
            wait_both()


def attend(plan, at, xp, cos, sin, g1, b1, bqkv, bout, source):
    length, width = xp.shape
    span = length // GENES
    pieces = len(source) == 12
    weights = [shape_of((width, 3 * width), BF16), shape_of((width, width), BF16)]
    got = call(
        functools.partial(attend_kernel, pieces=pieces),
        (GENES,),
        [
            rows_of((span, width)),
            rows_of((span, LANES)),
            rows_of((span, LANES)),
            full((1, width)),
            full((1, width)),
            full((1, 3 * width)),
            full((1, width)),
        ]
        + [ANY] * len(source),
        [
            rows_of((span, 3 * width)),
            rows_of((span, width)),
            pl.BlockSpec((16, span), lambda g, *ids: (0, g)),
            rows_of((span, width)),
        ]
        + [ANY] * (2 if pieces else 0),
        [
            shape_of((length, 3 * width), BF16),
            shape_of((length, width), BF16),
            shape_of((16, length), F32),
            shape_of((length, width), F32),
        ]
        + (weights if pieces else []),
        [
            pltpu.VMEM((width, 3 * width), BF16),
            pltpu.VMEM((width, width), BF16),
            pltpu.VMEM((span, span), F32),
            pltpu.SemaphoreType.DMA((2,)),
        ],
        prefetch=2,
        name="attend",
        cost=(11e9, 20e6),
    )(plan, at, xp, cos, sin, g1, b1, bqkv, bout, *source)
    return got[:4], (got[4:] if pieces else source)


def feed_kernel(at, *refs, block, pieces, steps):
    (x1_hbm, c_hbm, g2_ref, b2_ref, bup_ref, bdown_ref), refs = refs[:6], refs[6:]
    source, refs = (refs[:12], refs[12:]) if pieces else (refs[:2], refs[2:])
    (out_hbm, dx1_hbm, da_hbm, gbup_ref, sums_ref, first_ref, second_ref), refs = refs[:7], refs[7:]
    x1_ref, c_ref, out_ref, da_ref, a2_ref, acc_ref, dh_ref, gr_ref, du_ref = refs[:9]
    wups, wdowns, gups, gdowns, load_sem, store_sem, in_sem, out_sem = refs[9:]
    step = pl.program_id(0)
    length, width = x1_ref.shape
    chunk = bup_ref.shape[1]
    blocks = length // block
    slot = lax.rem(step, 2)
    rows = width // (4 * Z_SIZE)

    def load(j, to):
        if pieces:
            own = at_rows((at[0] * 2 + at[1]) * 2 * rows, 2 * rows)
            src = source[0].at[:, at_columns(j * chunk, chunk)]
            pltpu.make_async_copy(src, wups.at[to, own], load_sem.at[0, to]).start()

            def put_up(piece, f, y, c):
                dst = wups.at[to, at_rows((f * 2 + c) * rows, rows), at_columns(y * COLUMNS, COLUMNS)]
                pltpu.make_async_copy(piece.at[at_rows(j * rows, rows)], dst, load_sem.at[0, to]).start()

            def put_down(piece, x, y, c):
                dst = wdowns.at[to, at_rows((x * 2 + c) * 4 * rows, 4 * rows), at_columns(y * COLUMNS, COLUMNS)]
                pltpu.make_async_copy(piece, dst, load_sem.at[1, to]).start()

            for dc in range(2):
                f, _, c = spot(at, 0, 1, 0, dc)
                for y in range(2):
                    put_up(source[2 + dc].at[y, 0, pl.ds(2 * rows, 4 * rows)], f, y, c)

            def one(dz, carry):
                for dx, dy, dc in EVERY:
                    put_up(far_piece(source[4:], 0, dz, dx, dy, dc), *spot(at, dz, dx, dy, dc))
                return carry

            lax.fori_loop(1, Z_SIZE, one, 0)

            @pl.when(j == at[0])
            def _():
                here = at_rows(at[1] * 8 * rows, 8 * rows)
                pltpu.make_async_copy(source[1], wdowns.at[to, here], load_sem.at[1, to]).start()
                for dc in range(2):
                    _, _, c = spot(at, 0, 1, 0, dc)
                    for y in range(2):
                        put_down(source[2 + dc].at[y, 1, pl.ds(2 * rows, 4 * rows)], 1 - at[1], y, c)

            @pl.when(j != at[0])
            def _():
                back = lax.rem(at[0] + (Z_SIZE - j), Z_SIZE)
                for dx, dy, dc in EVERY:
                    _, y, c = spot(at, back, dx, dy, dc)
                    put_down(far_piece(source[4:], 1, back, dx, dy, dc), lax.bitwise_xor(at[1], dx), y, c)

        else:
            part = source[0].at[:, at_columns(j * chunk, chunk)]
            pltpu.make_async_copy(part, wups.at[to], load_sem.at[0, to]).start()
            part = source[1].at[at_rows(j * chunk, chunk), :]
            pltpu.make_async_copy(part, wdowns.at[to], load_sem.at[1, to]).start()

    def store(j, to):
        if pieces:

            def one(dz, carry):
                for dx, dy, dc in EVERY:
                    f, y, c = spot(at, Z_SIZE - dz, dx, dy, dc)
                    src = gups.at[to, at_rows(f * 2 * rows + c * rows, rows), at_columns(y * COLUMNS, COLUMNS)]
                    dst = (first_ref, second_ref)[dc].at[piece_index(0, dz, dx, dy), at_rows(j * rows, rows)]
                    pltpu.make_async_copy(src, dst, store_sem.at[0, to]).start()
                return carry

            lax.fori_loop(0, Z_SIZE, one, 0)
            ahead = lax.rem(j + Z_SIZE - at[0], Z_SIZE)
            for dx, dy, dc in EVERY:
                f, y, c = spot(at, 0, dx, dy, dc)
                x = lax.bitwise_xor(at[1], dx)
                src = gdowns.at[to, at_rows((x * 2 + c) * 4 * rows, 4 * rows), at_columns(y * COLUMNS, COLUMNS)]
                dst = (first_ref, second_ref)[dc].at[piece_index(1, ahead, dx, dy)]
                pltpu.make_async_copy(src, dst, store_sem.at[1, to]).start()
        else:
            part = first_ref.at[:, at_columns(j * chunk, chunk)]
            pltpu.make_async_copy(gups.at[to], part, store_sem.at[0, to]).start()
            part = second_ref.at[at_rows(j * chunk, chunk), :]
            pltpu.make_async_copy(gdowns.at[to], part, store_sem.at[1, to]).start()

    def wait_load(to):
        pltpu.make_async_copy(wups.at[to], wups.at[to], load_sem.at[0, to]).wait()
        pltpu.make_async_copy(wdowns.at[to], wdowns.at[to], load_sem.at[1, to]).wait()

    def wait_store(to):
        pltpu.make_async_copy(gups.at[to], gups.at[to], store_sem.at[0, to]).wait()
        pltpu.make_async_copy(gdowns.at[to], gdowns.at[to], store_sem.at[1, to]).wait()

    def bring(i):
        here = at_rows(i * block, block)
        return [
            pltpu.make_async_copy(x1_hbm.at[here, :], x1_ref.at[here, :], in_sem.at[0, i]),
            pltpu.make_async_copy(c_hbm.at[here, :], c_ref.at[here, :], in_sem.at[1, i]),
        ]

    def give(i):
        here = at_rows(i * block, block)
        return [
            pltpu.make_async_copy(out_ref.at[here, :], out_hbm.at[here, :], out_sem.at[0, i]),
            pltpu.make_async_copy(x1_ref.at[here, :], dx1_hbm.at[here, :], out_sem.at[1, i]),
            pltpu.make_async_copy(da_ref.at[here, :], da_hbm.at[here, :], out_sem.at[2, i]),
        ]

    @pl.when(step == 0)
    def _():
        for i in range(blocks):
            bring(i)[0].start()
        load(0, 0)
        for i in range(blocks):
            bring(i)[1].start()

        def one(i, carry):
            here = pl.ds(i * block, block)
            bring(i)[0].wait()
            xhat, _ = normalize(x1_ref[here, :])
            a2_ref[here, :] = (xhat * g2_ref[...] + b2_ref[...]).astype(BF16)
            acc_ref[here, :] = jnp.zeros((block, width), F32)
            dh_ref[here, :] = jnp.zeros((block, width), F32)
            return carry

        lax.fori_loop(0, blocks, one, 0)
        for i in range(blocks):
            bring(i)[1].wait()

    wait_load(slot)

    @pl.when(step < steps - 1)
    def _():
        load(step + 1, 1 - slot)

    wup_ref, wdown_ref = wups.at[slot], wdowns.at[slot]

    def one(i, bias_sum):
        here = pl.ds(i * block, block)
        u = nn(a2_ref[here, :], wup_ref[...]) + bup_ref[...]
        phi = 0.5 + 0.5 * lax.erf(u * math.sqrt(0.5))
        slope = phi + u * (jnp.exp(-0.5 * u * u) * (1.0 / math.sqrt(2.0 * math.pi)))
        gr = (u * phi).astype(BF16)
        gr_ref[here, :] = gr
        du = (nt(c_ref[here, :], wdown_ref[...]) * slope).astype(BF16)
        du_ref[here, :] = du
        out = nn(gr, wdown_ref[...])
        dh = nt(du, wup_ref[...])

        acc_ref[here, :] += out
        dh_ref[here, :] += dh
        return bias_sum + jnp.sum(du.astype(F32), 0, keepdims=True)

    gbup_ref[...] = lax.fori_loop(0, blocks, one, jnp.zeros((1, chunk), F32))

    @pl.when(step >= 2)
    def _():
        wait_store(slot)

    gdowns[slot] = tn(gr_ref[...], c_ref[...]).astype(BF16)
    gups[slot] = tn(a2_ref[...], du_ref[...]).astype(BF16)
    store(step, slot)

    @pl.when(step == steps - 1)
    def _():
        def one(i, sums):
            here = pl.ds(i * block, block)
            x1 = x1_ref[here, :]
            xhat, scale = normalize(x1)
            out_ref[here, :] = (x1 + acc_ref[here, :] + bdown_ref[...]).astype(BF16)
            dh = dh_ref[here, :]
            c = c_ref[here, :].astype(F32)
            e = dh * g2_ref[...]
            dx1 = c + scale * (
                e - jnp.mean(e, -1, keepdims=True) - xhat * jnp.mean(e * xhat, -1, keepdims=True)
            )
            x1_ref[here, :] = dx1
            da = dx1.astype(BF16)
            da_ref[here, :] = da
            for copy in give(i):
                copy.start()
            new = (
                jnp.sum(dh * xhat, 0, keepdims=True),
                jnp.sum(dh, 0, keepdims=True),
                jnp.sum(c, 0, keepdims=True),
                jnp.sum(da.astype(F32), 0, keepdims=True),
            )
            return tuple(a + b for a, b in zip(sums, new))

        sums = lax.fori_loop(0, blocks, one, (jnp.zeros((1, width), F32),) * 4)
        for i in range(4):
            sums_ref[i : i + 1, :] = sums[i]
        for i in range(blocks):
            for copy in give(i):
                copy.wait()
        wait_store(1 - slot)
        wait_store(slot)


def feed(at, x1, c, g2, b2, bup, bdown, source):
    length, width = x1.shape
    hidden = bup.shape[1]
    steps = 4
    chunk = hidden // steps
    pieces = len(source) == 12
    if pieces:
        rows = width // Z_SIZE
        stored = [shape_of((PIECES, rows, COLUMNS), BF16)] * 2
    else:
        stored = [shape_of((width, hidden), BF16), shape_of((hidden, width), BF16)]
    return call(
        functools.partial(feed_kernel, block=length // 2, pieces=pieces, steps=steps),
        (steps,),
        [
            ANY,
            ANY,
            full((1, width)),
            full((1, width)),
            pl.BlockSpec((1, chunk), lambda j, *ids: (0, j)),
            full((1, width)),
        ]
        + [ANY] * len(source),
        [
            ANY,
            ANY,
            ANY,
            pl.BlockSpec((1, chunk), lambda j, *ids: (0, j)),
            full((8, width)),
            ANY,
            ANY,
        ],
        [
            shape_of((length, width), BF16),
            shape_of((length, width), F32),
            shape_of((length, width), BF16),
            shape_of((1, hidden), F32),
            shape_of((8, width), F32),
        ]
        + stored,
        [
            pltpu.VMEM((length, width), F32),
            pltpu.VMEM((length, width), BF16),
            pltpu.VMEM((length, width), BF16),
            pltpu.VMEM((length, width), BF16),
            pltpu.VMEM((length, width), BF16),
            pltpu.VMEM((length, width), F32),
            pltpu.VMEM((length, width), F32),
            pltpu.VMEM((length, chunk), BF16),
            pltpu.VMEM((length, chunk), BF16),
            pltpu.VMEM((2, width, chunk), BF16),
            pltpu.VMEM((2, chunk, width), BF16),
            pltpu.VMEM((2, width, chunk), BF16),
            pltpu.VMEM((2, chunk, width), BF16),
            pltpu.SemaphoreType.DMA((2, 2)),
            pltpu.SemaphoreType.DMA((2, 2)),
            pltpu.SemaphoreType.DMA((2, 4)),
            pltpu.SemaphoreType.DMA((3, 4)),
        ],
        name="feed",
        cost=(29e9, 40e6),
    )(at, x1, c, g2, b2, bup, bdown, *source)


def attend_back_kernel(
    plan, qkv_ref, da_ref, lse_ref, cos_ref, sin_ref, wout_ref, *refs, base,
):
    dqkv_ref, bias_ref, dout_ref, mask_ref = refs[-4:]
    gene = pl.program_id(0) + base
    span, width = da_ref.shape
    score_scale = 1.0 / math.sqrt(HEAD_DIM)
    dout_ref[...] = nt(da_ref[...], wout_ref[...]).astype(BF16)
    mask_ref[...] = jnp.where(allowed_pairs(plan, gene, span), 1.0, 0.0)
    cos, sin = cos_ref[...], sin_ref[...]
    masks = head_masks(span)

    def back(t):
        return (t * cos - swap_halves(t) * sin).astype(BF16)

    def pair(p, carry):
        part = lambda i: at_columns(i * width + p * LANES, LANES)
        q = qkv_ref[:, part(0)]
        k = qkv_ref[:, part(1)] * BF16(score_scale)
        v = qkv_ref[:, part(2)]
        dout = dout_ref[:, part(0)]
        dq = jnp.zeros((span, LANES), F32)
        dk = jnp.zeros((span, LANES), F32)
        dv = jnp.zeros((span, LANES), F32)
        for h in range(2):
            kh = keep(masks[h], k)
            s = nt(kh, q)
            s = jnp.where(mask_ref[...] > 0.5, s, NEG_FILL)
            weights = jnp.exp(s - lse_ref[pl.ds(2 * p + h, 1), :])
            dw = nt(keep(masks[h], v), dout)
            dot = jnp.sum(weights * dw, 0, keepdims=True)
            ds = (weights * (dw - dot)).astype(BF16)
            dv = dv + nn(weights.astype(BF16), keep(masks[h], dout))
            dk = dk + nn(ds, keep(masks[h], q))
            dq = dq + tn(ds, kh)
        dqkv_ref[:, part(0)] = back(dq)
        dqkv_ref[:, part(1)] = back(dk * score_scale)
        dqkv_ref[:, part(2)] = dv.astype(BF16)
        return carry

    lax.fori_loop(0, width // LANES, pair, 0, unroll=UNROLL_B)

    bqkv = jnp.sum(dqkv_ref[...].astype(F32), 0, keepdims=True)

    @pl.when(gene == base)
    def _():
        bias_ref[0:1, :] = bqkv

    @pl.when(gene > base)
    def _():
        bias_ref[0:1, :] += bqkv


def attend_back(plan, qkv, da, lse, cos, sin, wout, base, count, before=()):
    length, width = da.shape
    span = length // GENES
    rows = lambda shape: pl.BlockSpec(shape, lambda g, *ids: (g + base, 0))
    return call(
        functools.partial(attend_back_kernel, base=base),
        (count,),
        [
            rows((span, 3 * width)),
            rows((span, width)),
            pl.BlockSpec((16, span), lambda g, *ids: (0, g + base)),
            rows((span, LANES)),
            rows((span, LANES)),
            full((width, width)),
        ]
        + [ANY] * len(before),
        [rows((span, 3 * width)), full((8, 3 * width))],
        [shape_of((length, 3 * width), BF16), shape_of((8, 3 * width), F32)],
        [pltpu.VMEM((span, width), BF16), pltpu.VMEM((span, span), F32)],
        name="attend_back",
        cost=(4e9 * count, 6e6 * count),
        aliases={7 + i: i for i in range(len(before))},
    )(plan, qkv, da, lse, cos, sin, wout, *before)


def project_back_kernel(xp_ref, g1_ref, dx1_ref, dqkv_ref, wqkv_ref, dxp_ref, sums_ref):
    step = pl.program_id(0)
    dh = nt(dqkv_ref[...], wqkv_ref[...])
    xhat, scale = normalize(xp_ref[...].astype(F32))
    e = dh * g1_ref[...]
    dx = dx1_ref[...] + scale * (
        e - jnp.mean(e, -1, keepdims=True) - xhat * jnp.mean(e * xhat, -1, keepdims=True)
    )
    dxp_ref[...] = dx.astype(BF16)

    @pl.when(step == 0)
    def _():
        sums_ref[...] = jnp.zeros_like(sums_ref)

    sums_ref[0:1, :] += jnp.sum(dh * xhat, 0, keepdims=True)
    sums_ref[1:2, :] += jnp.sum(dh, 0, keepdims=True)


def project_back(xp, g1, dx1, dqkv, wqkv):
    length, width = xp.shape
    span = length // GENES
    return call(
        project_back_kernel,
        (GENES,),
        [
            rows_of((span, width)),
            full((1, width)),
            rows_of((span, width)),
            rows_of((span, 3 * width)),
            full((width, 3 * width)),
        ],
        [rows_of((span, width)), full((8, width))],
        [shape_of((length, width), BF16), shape_of((8, width), F32)],
        prefetch=0,
        name="project_back",
        cost=(0, 0),
    )(xp, g1, dx1, dqkv, wqkv)


def grads_kernel(at, *refs, pieces):
    (xp_hbm, o_hbm, da_hbm, dqkv_hbm, g1_ref, b1_ref), refs = refs[:6], refs[6:]
    sums, refs = (refs[:5], refs[5:]) if pieces else ((), refs)
    first_ref, second_ref, xp_ref, o_ref, da_ref, dqkv_ref, a1_ref, grad_ref, in_sem, sem, *rest = refs
    small_ref, small_sem = rest if pieces else (None, None)
    step = pl.program_id(0)
    width = xp_ref.shape[1]
    rows = width // (4 * Z_SIZE)
    slot = lax.rem(step, 2)

    def bring(j):
        part = dqkv_hbm.at[:, at_columns(j * width, width)]
        return pltpu.make_async_copy(part, dqkv_ref.at[lax.rem(j, 2)], in_sem.at[3 + lax.rem(j, 2)])

    whole = [
        pltpu.make_async_copy(src, dst, in_sem.at[i])
        for i, (src, dst) in enumerate(((o_hbm, o_ref), (da_hbm, da_ref), (xp_hbm, xp_ref)))
    ]

    def wait(to):
        pltpu.make_async_copy(grad_ref.at[to], grad_ref.at[to], sem.at[to]).wait()

    def store(half, base, to):
        def one(dz, carry):
            for dx, dy, dc in EVERY:
                f, y, c = spot(at, Z_SIZE - dz, dx, dy, dc)
                src = grad_ref.at[to, at_rows(f * 2 * rows + c * rows, rows), at_columns(y * COLUMNS, COLUMNS)]
                dst = (first_ref, second_ref)[dc].at[
                    jnp.where(half == 0, piece_index(0, dz, dx, dy), piece_index(1, dz, dx, dy)),
                    at_rows(base * rows, rows),
                ]
                pltpu.make_async_copy(src, dst, sem.at[to]).start()
            return carry

        lax.fori_loop(0, Z_SIZE, one, 0)

    def pack():
        sums1, low_ref, high_ref, sums2, gbup = sums
        line = lambda ref, i: ref[i : i + 1, :]
        vectors = [
            line(sums1, 0), line(sums1, 1), line(low_ref, 0) + line(high_ref, 0), line(sums2, 3),
            line(sums2, 0), line(sums2, 1), gbup[...], line(sums2, 2),
        ]
        shards = 2 * Z_SIZE
        columns = []
        for value in vectors:
            size = value.shape[1] // shards
            spread_out = jnp.broadcast_to(value, (shards, value.shape[1]))
            mask = iota(spread_out.shape, 1) // size == iota(spread_out.shape, 0)
            own = jnp.where(mask, spread_out, 0.0).astype(BF16)
            columns.append(nt(own, spread(size, value.shape[1])).astype(BF16))
        packed = jnp.concatenate(columns, 1).astype(F32)
        for f in range(shards):
            for i in range(4):
                part = packed[f : f + 1, i * COLUMNS : (i + 1) * COLUMNS]
                small_ref[f, i // 2, i % 2] = jnp.broadcast_to(part, (8, COLUMNS)).astype(BF16)

    def smalls(act):
        def one(dz, carry):
            for dx, dy, dc in EVERY:
                f, y, c = spot(at, Z_SIZE - dz, dx, dy, dc)
                for half in range(2):
                    src = small_ref.at[f, y, c]
                    dst = (first_ref, second_ref)[dc].at[piece_index(half, dz, dx, dy), pl.ds(2 * rows, 8)]
                    act(pltpu.make_async_copy(src, dst, small_sem))
            return carry

        lax.fori_loop(0, Z_SIZE, one, 0)

    @pl.when(step == 0)
    def _():
        for copy in whole:
            copy.start()
        bring(step).start()
        if pieces:
            pack()
            smalls(lambda copy: copy.start())
        whole[0].wait()
        whole[1].wait()
        grad_ref[0] = tn(o_ref[...], da_ref[...]).astype(BF16)
        if pieces:
            store(1, 1, 0)
        else:
            pltpu.make_async_copy(grad_ref.at[0], second_ref, sem.at[0]).start()
        whole[2].wait()
        xhat, _ = normalize(xp_ref[...].astype(F32))
        a1_ref[...] = (xhat * g1_ref[...] + b1_ref[...]).astype(BF16)

    @pl.when(step > 0)
    def _():
        bring(step - 1).wait()

        @pl.when(step < 3)
        def _():
            bring(step).start()

        @pl.when(step >= 2)
        def _():
            wait(slot)

        grad_ref[slot] = tn(a1_ref[...], dqkv_ref[lax.rem(step - 1, 2)]).astype(BF16)
        if pieces:
            store(lax.div(step - 1, 2), lax.rem(step - 1, 2), slot)
        else:
            dst = first_ref.at[:, at_columns((step - 1) * width, width)]
            pltpu.make_async_copy(grad_ref.at[slot], dst, sem.at[slot]).start()

    @pl.when(step == 3)
    def _():
        wait(0)
        wait(1)
        if pieces:
            smalls(lambda copy: copy.wait())


def grads(at, xp, g1, b1, o, da, dqkv, sums):
    pieces = bool(sums)
    length, width = xp.shape
    if pieces:
        rows = width // (2 * Z_SIZE) + 8
        stored = [shape_of((PIECES, rows, COLUMNS), BF16)] * 2
    else:
        stored = [shape_of((width, 3 * width), BF16), shape_of((width, width), BF16)]
    return call(
        functools.partial(grads_kernel, pieces=pieces),
        (4,),
        [ANY] * 4 + [full((1, width))] * 2 + [full(v.shape) for v in sums],
        [ANY, ANY],
        stored,
        [pltpu.VMEM((length, width), BF16)] * 3
        + [
            pltpu.VMEM((2, length, width), BF16),
            pltpu.VMEM((length, width), BF16),
            pltpu.VMEM((2, width, width), BF16),
            pltpu.SemaphoreType.DMA((5,)),
            pltpu.SemaphoreType.DMA((2,)),
        ]
        + ([pltpu.VMEM((2 * Z_SIZE, 2, 2, 8, COLUMNS), BF16), pltpu.SemaphoreType.DMA] if pieces else []),
        name="grads",
        cost=(5e9, 12e6),
    )(at, xp, o, da, dqkv, g1, b1, *sums)


def restore_kernel(plan, outp_ref, dxp_ref, out_ref, dx_ref):
    span, width = out_ref.shape
    slots = iota((1, span), 1)
    source = jnp.concatenate([source_of_slots(plan, g, slots) for g in range(GENES)], 1)
    codon = iota((span, outp_ref.shape[0]), 0) + pl.program_id(0) * span
    pick = jnp.where(codon == source, 1.0, 0.0).astype(BF16)
    out_ref[...] = nn(pick, outp_ref[...]).astype(BF16)
    dx_ref[...] = nn(pick, dxp_ref[...]).astype(BF16)


def restore(plan, outp, dxp):
    length, width = outp.shape
    span = length // GENES
    return call(
        restore_kernel,
        (GENES,),
        [full((length, width)), full((length, width))],
        [rows_of((span, width))] * 2,
        [shape_of((length, width), BF16)] * 2,
        name="restore",
        cost=(3.3e9, 8e6),
    )(plan, outp, dxp)


def deliver_first_kernel(at, mine, other, wqkv, wout, *rest):
    vectors, row_ref = rest[:8], rest[8]
    width = wout.shape[1]
    rows = wout.shape[0] // 2
    for dc, one in enumerate((mine, other)):
        c = lax.bitwise_xor(at[3], dc)
        here = pl.ds(pl.multiple_of(c * rows, 8), rows)
        for y in range(2):
            for b in range(4):
                ref, base = (wqkv, b * width) if b < 3 else (wout, 0)
                start = base + y * COLUMNS
                piece = one[y, b // 2, (b % 2) * rows : (b % 2 + 1) * rows, :]
                ref[here, start : start + COLUMNS] = piece.astype(F32)
            start = at_columns((y * 2 + c) * COLUMNS, COLUMNS)
            row_ref[:, start] = one[y, 0, 2 * rows : 2 * rows + 8, :].astype(F32)
    for ref, start in zip(vectors, SLOTS):
        ref[...] = row_ref[0:1, start : start + ref.shape[0]].reshape(ref.shape[0])


def deliver_first(at, mine, other, sizes):
    rows = (mine.shape[2] - 8) // 2
    width = 2 * COLUMNS
    shapes = [(2 * rows, 3 * width), (2 * rows, width)] + [(n,) for n in sizes]
    return call(
        deliver_first_kernel,
        (1,),
        [full(mine.shape)] * 2,
        [full(s) for s in shapes],
        [shape_of(s, F32) for s in shapes],
        [pltpu.VMEM((8, PACKED), F32)],
        name="deliver_first",
        cost=(0, 2e6),
    )(at, mine, other)


def deliver_second_kernel(at, mine, other, wup, wdown):
    width = wdown.shape[1]
    rows = wup.shape[0] // 2
    for dc, two in enumerate((mine, other)):
        c = lax.bitwise_xor(at[3], dc)
        here = pl.ds(pl.multiple_of(c * rows, 8), rows)
        down = pl.ds(pl.multiple_of(c * 4 * rows, 8), 4 * rows)
        for y in range(2):
            for b in range(4):
                start = b * width + y * COLUMNS
                wup[here, start : start + COLUMNS] = two[y, 0, b * rows : (b + 1) * rows, :].astype(F32)
            wdown[down, y * COLUMNS : (y + 1) * COLUMNS] = two[y, 1].astype(F32)


def deliver_second(at, mine, other):
    rows = mine.shape[2] // 4
    width = 2 * COLUMNS
    shapes = [(2 * rows, 4 * width), (8 * rows, width)]
    return call(
        deliver_second_kernel,
        (1,),
        [full(mine.shape)] * 2,
        [full(s) for s in shapes],
        [shape_of(s, F32) for s in shapes],
        name="deliver_second",
        cost=(0, 4e6),
    )(at, mine, other)


def gather(shard):
    return lax.all_gather(shard, "fsdp", axis=0, tiled=True)


def reduce_rows(grad):
    part = lax.psum_scatter(grad, "fsdp", scatter_dimension=0, tiled=True)
    return lax.psum(part.astype(BF16), "replica").astype(F32)


def low(value):
    return value.astype(BF16)


def add(*values):
    total = values[0].astype(F32)
    for v in values[1:]:
        total = total + v.astype(F32)
    return total


def to_z(arrays):
    arrays = arrays if isinstance(arrays, list) else [arrays] * 3
    return [move(v, ALONG_Z[d]) for d, v in zip((1, 2, 3), arrays)]


def over_x(array):
    return move(array, ACROSS_X)


def over_y(array):
    return move(array, ACROSS_Y)


def over_core(array):
    return move(array, ACROSS_CORE)


def stack(arrays):
    return jnp.stack(list(arrays))


class Sum:
    def __init__(self, kept, got):
        self.kept, self.got = kept, got

    def near(self, start, stop):
        return add(self.kept[start:stop], self.got[start:stop])

    def plane_one(self):
        return low(self.near(8, 16)), low(self.near(24, 32))

    def plane_two(self, by_x, by_y):
        self.first = add(self.near(0, 8), by_x)
        self.second = add(self.near(16, 24), by_y)
        return low(self.first[Z_SIZE:]), low(self.second[Z_SIZE:])

    def along_z(self, by_y, by_x):
        first, second = add(self.first[:Z_SIZE], by_y), add(self.second[:Z_SIZE], by_x)
        self.own = stack([first[0], second[0]])
        return [low(stack([first[d], second[d]])) for d in range(1, Z_SIZE)]

    def total(self, by_z):
        return low(add(self.own, *by_z))


def settle(bit, mine, other):
    return jnp.where(bit == 0, stack([mine, other]), stack([other, mine]))


def body(
    layer_input, cotangent, segment_ids, pad_mask, ln1_gain, ln1_bias, w_qkv, b_qkv, w_out, b_out,
    ln2_gain, ln2_bias, w_up, b_up, w_down, b_down, *, tuned,
):
    vectors = (ln1_gain, ln1_bias, b_qkv, b_out, ln2_gain, ln2_bias, b_up, b_down)
    sizes = [v.shape[0] for v in vectors]
    x, c = layer_input[0], cotangent[0]
    if tuned:
        at = place()
        near1, near2, side = quarters(at, w_qkv, w_out, w_up, w_down, vectors)
        near1, near2, side, x = tie((near1, near2, side, x))
        z1 = to_z(near1)
        far_side = over_x(side)
        z2_one = move(near2, ALONG_Z[1])
        prepared = prepare(segment_ids, x, c)
        z1, z2_one, prepared = tie((z1, z2_one, prepared))
        plan, xp, cp, cos, sin = prepared

        count = near1.shape[1] - 8
        first1, second1 = stack(q[0, :count] for q in z1), stack(q[1] for q in z1)
        rows = stack(q[0, count:] for q in [near1] + z1)
        first1, second1, near2 = tie((first1, second1, near2))
        first_y, second_x = over_y(first1), over_x(second1)
        z2_three = move(near2, ALONG_Z[3])
        first_y, second_x, z2_three, near2, far_side = tie((first_y, second_x, z2_three, near2, far_side))

        first1, second1 = stack([first1, first_y]), stack([second1, second_x])[:, :, :count]
        far_rows = jnp.concatenate([far_side[0, :1, 3 * count :], second_x[:, count:]])
        early = [stack(q[h] for q in (z2_one, z2_three)) for h in range(2)]
        first1, second1, rows, far_rows, near2, early = tie((first1, second1, rows, far_rows, near2, early))
        far_first1, far_second1 = over_x(first1), over_y(second1)
        z2_two = move(near2, ALONG_Z[2])
        early_far = [over_y(early[0]), over_x(early[1])]
        params = unpack(at, rows, far_rows, sizes)
        far_first1, far_second1, params, z2_two, early_far, far_side = tie(
            (far_first1, far_second1, params, z2_two, early_far, far_side)
        )

        late = [z2_two[h : h + 1] for h in range(2)]
        near_core1 = stack([first1, second1])
        far_first1, far_second1, near_core1, late = tie((far_first1, far_second1, near_core1, late))
        far_core1 = over_core(stack([far_first1, far_second1]))
        near_core1 = over_core(near_core1)
        late_far = [over_y(late[0]), over_x(late[1])]
        core_side = over_core(far_side)
        late_far, far_core1, near_core1, core_side = tie((late_far, far_core1, near_core1, core_side))

        attention = (
            w_qkv, w_out, far_side, core_side, first1, far_first1, second1, far_second1,
            near_core1, far_core1, near_core1, far_core1,
        )
        order = lambda e, l: jnp.concatenate([e[:1], l, e[1:]])
        first2, second2 = (
            stack([order(early[h], late[h]), order(early_far[h], late_far[h])]) for h in range(2)
        )
        first2, second2, attention, params, plan = tie((first2, second2, attention, params, plan))
        far_first2, far_second2 = over_x(first2), over_y(second2)
        core2 = [over_core(v) for v in (first2, second2)]
    else:
        at = jnp.zeros((4,), jnp.int32)
        plan, xp, cp, cos, sin = prepare(segment_ids, x, c)
        params = [gather(v[None]).reshape(1, -1).astype(F32) for v in vectors]
        attention = gather(w_qkv), gather(w_out)
        forward = gather(w_up), gather(w_down)
    g1, b1, bqkv, bout, g2, b2, bup, bdown = params
    (qkv, o, lse, x1), (wqkv, wout) = attend(plan, at, xp, cos, sin, g1, b1, bqkv, bout, attention)
    if tuned:
        far_first2, far_second2, core2, x1 = tie((far_first2, far_second2, core2, x1))
        far_core2 = over_core(far_first2), over_core(far_second2)
        forward = (
            w_up, w_down, far_side, core_side, first2, far_first2, second2, far_second2,
            core2[0], far_core2[0], core2[1], far_core2[1],
        )
    outp, dx1, da, gbup, sums2, *parts2 = feed(at, x1, cp, g2, b2, bup, bdown, forward)
    back = functools.partial(attend_back, plan, qkv, da, lse, cos, sin, wout)
    split = 1
    if tuned:
        kept2, sent2 = parts2
        got2 = over_core(sent2)
        dqkv, bias_low = back(0, split)
        got2, dqkv = tie((got2, dqkv))
        group2 = Sum(kept2, got2)
        to_x, to_y, dqkv = tie(group2.plane_one() + (dqkv,))
        by_x, by_y = over_x(to_x), over_y(to_y)
    else:
        dqkv, bias_low = back(0, split)
    dqkv, bias_high = back(split, GENES - split, (dqkv,))
    dxp, sums1 = project_back(xp, g1, dx1, dqkv, wqkv)
    sums = [sums1, bias_low, bias_high, sums2, gbup]
    if tuned:
        by_x, by_y, sums, dxp, dqkv = tie((by_x, by_y, sums, dxp, dqkv))
        to_y, to_x = group2.plane_two(by_x, by_y)
        to_y, to_x, dqkv = tie((to_y, to_x, dqkv))
        by_y, by_x = over_y(to_y), over_x(to_x)
        kept1, sent1 = grads(at, xp, g1, b1, o, da, dqkv, sums)
        by_y, by_x, kept1, sent1 = tie((by_y, by_x, kept1, sent1))
        got1 = over_core(sent1)
        got1, *to_z2 = tie([got1] + group2.along_z(by_y, by_x))
        group1 = Sum(kept1, got1)
        to_x, to_y, *to_z2 = tie([*group1.plane_one(), *to_z2])
        two = move(to_z2[1], ALONG_Z[2])
        by_x, by_y, two, *to_z2 = tie((over_x(to_x), over_y(to_y), two, to_z2[0], to_z2[2]))
        to_y, to_x, *to_z2 = tie([*group1.plane_two(by_x, by_y), *to_z2])
        one, three = move(to_z2[0], ALONG_Z[1]), move(to_z2[1], ALONG_Z[3])
        by_y, by_x, one, three = tie((over_y(to_y), over_x(to_x), one, three))
        z2 = one, two, three
        to_z1 = group1.along_z(by_y, by_x)
        total2 = group2.total(z2)
        to_z1, total2, outp, dxp = tie((to_z1, total2, outp, dxp))
        z1 = to_z(to_z1)
        by_y = over_y(total2)
        layer_out, input_grad = restore(plan, outp, dxp)
        z1, by_y, layer_out, input_grad = tie((z1, by_y, layer_out, input_grad))
        total1 = group1.total(z1)
        final2 = settle(at[2], total2, by_y)
        total1, final2 = tie((total1, final2))
        by_y, other2 = over_y(total1), over_core(final2)
        by_y, other2 = tie((by_y, other2))
        final1 = settle(at[2], total1, by_y)
        other1 = over_core(final1)
        wup, wdown = deliver_second(at, final2, other2)
        other1, wup, wdown = tie((other1, wup, wdown))
        wqkv, wout, *small = deliver_first(at, final1, other1, sizes)
    else:
        parts1 = grads(at, xp, g1, b1, o, da, dqkv, ())
        layer_out, input_grad = restore(plan, outp, dxp)
        wqkv, wout = map(reduce_rows, parts1)
        wup, wdown = map(reduce_rows, parts2)
        bias = bias_low + bias_high
        small = [sums1[0], sums1[1], bias[0], sums2[3], sums2[0], sums2[1], gbup[0], sums2[2]]
        small = [reduce_rows(v) for v in small]
    dg1, db1, dbqkv, dbout, dg2, db2, dbup, dbdown = small
    return (
        layer_out[None], input_grad[None], dg1, db1, wqkv, dbqkv, wout, dbout, dg2, db2,
        wup, dbup, wdown, dbdown,
    )


def solution(mesh):
    rows = ("fsdp", "replica")
    by_row = P(rows, None, None)
    vector, matrix = P("fsdp"), P("fsdp", None)
    params = (
        vector, vector, matrix, vector, matrix, vector, vector, vector, matrix, vector, matrix, vector,
    )
    in_specs = (by_row, by_row, P(rows, None), P(rows, None)) + params
    out_specs = (by_row, by_row) + params
    return jax.shard_map(
        functools.partial(body, tuned=tuned_mesh(mesh)),
        mesh=mesh, in_specs=in_specs, out_specs=out_specs, check_vma=False,
    )
```

```python
import functools
import math

import jax
import jax.numpy as jnp
import numpy as np
from jax import lax
from jax.experimental import pallas as pl
from jax.experimental.pallas import tpu as pltpu
from jax.sharding import PartitionSpec as P

HEADS = 12
HEAD_DIM = 64
GENES = 4
LANES = 128
EPSILON = 1e-05
NEG_FILL = -1000000000.0
F32 = jnp.float32
BF16 = jnp.bfloat16
MIB = 1 << 20


def nn(left, right):
    return lax.dot_general(left, right, (((1,), (0,)), ((), ())), preferred_element_type=F32)


def nt(left, right):
    return lax.dot_general(left, right, (((1,), (1,)), ((), ())), preferred_element_type=F32)


def tn(left, right):
    return lax.dot_general(left, right, (((0,), (0,)), ((), ())), preferred_element_type=F32)


def iota(shape, axis):
    return lax.broadcasted_iota(jnp.int32, shape, axis)


def full(shape):
    return pl.BlockSpec(shape, lambda *ids: (0,) * len(shape))


def rows_of(shape):
    return pl.BlockSpec(shape, lambda g, *ids: (g,) + (0,) * (len(shape) - 1))


def call(kernel, grid, in_specs, out_specs, out_shape, scratch=(), vmem=60, prefetch=1, name=None, cost=None, aliases=None):
    return pl.pallas_call(
        kernel,
        grid_spec=pltpu.PrefetchScalarGridSpec(
            num_scalar_prefetch=prefetch,
            grid=grid,
            in_specs=in_specs,
            out_specs=out_specs,
            scratch_shapes=list(scratch),
        ),
        out_shape=out_shape,
        input_output_aliases=aliases or {},
        compiler_params=pltpu.CompilerParams(
            dimension_semantics=("arbitrary",) * len(grid), vmem_limit_bytes=vmem * MIB
        ),
        name=name,
        cost_estimate=cost and pl.CostEstimate(flops=int(cost[0]), bytes_accessed=int(cost[1]), transcendentals=0),
    )


def shape_of(shape, dtype):
    return jax.ShapeDtypeStruct(shape, dtype)


def normalize(x):
    mean = jnp.mean(x, -1, keepdims=True)
    centered = x - mean
    scale = lax.rsqrt(jnp.mean(centered * centered, -1, keepdims=True) + EPSILON)
    return centered * scale, scale


def swap_halves(t):
    low = (iota(t.shape, 1) % HEAD_DIM) < HEAD_DIM // 2
    return jnp.where(
        low, pltpu.roll(t, LANES - HEAD_DIM // 2, 1), pltpu.roll(t, HEAD_DIM // 2, 1)
    )


def head_masks(rows):
    lane = iota((rows, LANES), 1)
    return [(lane < HEAD_DIM), (lane >= HEAD_DIM)]


def both(masks, value):
    return jnp.concatenate([keep(mask, value) for mask in masks], 0)


def beside(value):
    return jnp.concatenate([value[0], value[1]], 1)


def allowed_pairs(plan, gene, span):
    length = plan[gene]
    i, j = iota((span, span), 0), iota((span, span), 1)
    return ((i < length) & (j < length)) | (i == j)


def keep(mask, value):
    return jnp.where(mask, value, jnp.zeros_like(value))


Z_SIZE = 4
COLUMNS = 384
AXES = ("fsdp", "replica")
ANY = pl.BlockSpec(memory_space=pl.ANY)
PIECES = 32
EVERY = [(dx, dy, dc) for dx in range(2) for dy in range(2) for dc in range(2)]
SLOTS = (0, 128, 256, 640, 768, 896, 1024, 1408)
PACKED = 1536


def tuned_mesh(mesh):
    return mesh.shape["fsdp"] == 2 * Z_SIZE and mesh.shape["replica"] == 4


def pairs(step):
    out = []
    for z in range(Z_SIZE):
        for x in range(2):
            for y in range(2):
                for c in range(2):
                    tz, tx, ty, tc = step(z, x, y, c)
                    out.append((((z * 2 + x) * 2 + y) * 2 + c, (((tz % Z_SIZE) * 2 + tx) * 2 + ty) * 2 + tc))
    return out


ACROSS_X = pairs(lambda z, x, y, c: (z, 1 - x, y, c))
ACROSS_Y = pairs(lambda z, x, y, c: (z, x, 1 - y, c))
ACROSS_CORE = pairs(lambda z, x, y, c: (z, x, y, 1 - c))
ALONG_Z = [pairs(functools.partial(lambda d, z, x, y, c: (z + d, x, y, c), d)) for d in range(Z_SIZE)]
tie = lax.optimization_barrier


def move(array, table):
    return lax.ppermute(array, AXES, table)


def place():
    f, r = lax.axis_index("fsdp"), lax.axis_index("replica")
    return jnp.stack([f // 2, f % 2, r // 2, r % 2]).astype(jnp.int32)


def spot(at, dz, dx, dy, dc):
    z = lax.rem(at[0] + (Z_SIZE - dz), Z_SIZE)
    return z * 2 + lax.bitwise_xor(at[1], dx), lax.bitwise_xor(at[2], dy), lax.bitwise_xor(at[3], dc)


def piece_index(half, dz, dx, dy):
    return (16 + dy * 8 + dx * 4 if half else dx * 8 + dy * 4) + dz


def at_rows(start, size):
    return pl.ds(pl.multiple_of(start, 16), size)


def at_columns(start, size):
    return pl.ds(pl.multiple_of(start, LANES), size)


def quarters_kernel(at, *refs):
    wqkv, wout, wup, wdown = refs[:4]
    vectors, (near1, near2, side, packed) = refs[4:12], refs[12:]
    width = wout.shape[1]
    rows = wout.shape[0] // 2
    packed[...] = jnp.zeros_like(packed)
    for ref, start in zip(vectors, SLOTS):
        packed[:, start : start + ref.shape[0]] = ref[...].reshape(1, -1)
    tail = jnp.zeros((8, COLUMNS), BF16)
    for i in range(4):
        part = jnp.broadcast_to(packed[:, i * COLUMNS : (i + 1) * COLUMNS], (8, COLUMNS))
        tail = jnp.where(iota((8, COLUMNS), 0) == i, part, tail)
    mine = at_rows(at[3] * rows, rows)
    for y in range(2):
        for b in range(4):
            ref, base = (wqkv, b * width) if b < 3 else (wout, 0)
            start = base + y * COLUMNS
            side[y, b // 2, (b % 2) * rows : (b % 2 + 1) * rows, :] = ref[mine, start : start + COLUMNS]
            start = b * width + y * COLUMNS
            side[y, 0, (2 + b) * rows : (3 + b) * rows, :] = wup[mine, start : start + COLUMNS]
        here = slice(y * COLUMNS, (y + 1) * COLUMNS)
        side[y, 1, 2 * rows : 6 * rows, :] = wdown[at_rows(at[3] * 4 * rows, 4 * rows), here]
        for h in range(2):
            side[y, h, 6 * rows : 6 * rows + 8, :] = tail
    near1[:, 0 : 2 * rows, :] = side[at[2], :, 0 : 2 * rows, :]
    near2[...] = side[at[2], :, 2 * rows : 6 * rows, :]
    for h in range(2):
        near1[h, 2 * rows : 2 * rows + 8, :] = tail


def quarters(at, wqkv, wout, wup, wdown, vectors):
    rows = wqkv.shape[0] // 2
    shapes = [
        (2, 2 * rows + 8, COLUMNS),
        (2, 4 * rows, COLUMNS),
        (2, 2, 6 * rows + 8, COLUMNS),
    ]
    matrices = (wqkv, wout, wup, wdown)
    return call(
        quarters_kernel,
        (1,),
        [full(v.shape) for v in matrices + tuple(vectors)],
        [full(s) for s in shapes],
        [shape_of(s, BF16) for s in shapes],
        [pltpu.VMEM((1, PACKED), BF16)],
        name="quarters",
        cost=(0, 6e6),
    )(at, *matrices, *vectors)


def rel_mask(at, columns, size):
    row = iota((2 * Z_SIZE, columns), 0)
    z = (at[0] + Z_SIZE - row % Z_SIZE) % Z_SIZE
    shard = z * 2 + jnp.where(row < Z_SIZE, at[1], 1 - at[1])
    return iota((2 * Z_SIZE, columns), 1) // size == shard


def spread(size, columns):
    lanes = -(-size // LANES) * LANES
    lane, column = iota((lanes, columns), 0), iota((lanes, columns), 1)
    return jnp.where(column % size == lane, 1.0, 0.0).astype(BF16)


def unpack_kernel(at, near_ref, far_ref, *refs):
    out, row_ref = refs[:8], refs[8]
    for x_bit, rows in enumerate((near_ref, far_ref)):
        for d in range(Z_SIZE):
            here = x_bit * Z_SIZE + d
            for i in range(4):
                row_ref[here : here + 1, i * COLUMNS : (i + 1) * COLUMNS] = rows[d, i : i + 1, :].astype(F32)
    for ref, start in zip(out, SLOTS):
        columns = ref.shape[1]
        size = columns // (2 * Z_SIZE)
        table = spread(size, columns)
        got = nn(row_ref[:, start : start + table.shape[0]].astype(BF16), table)
        ref[...] = jnp.sum(jnp.where(rel_mask(at, columns, size), got, 0.0), 0, keepdims=True)


def unpack(at, near, far, sizes):
    shapes = [(1, n * 2 * Z_SIZE) for n in sizes]
    return call(
        unpack_kernel,
        (1,),
        [full(near.shape)] * 2,
        [full(s) for s in shapes],
        [shape_of(s, F32) for s in shapes],
        [pltpu.VMEM((2 * Z_SIZE, PACKED), F32)],
        name="unpack",
        cost=(1e8, 1e5),
    )(at, near, far)


def plan_of(segments):
    lengths = [jnp.sum(jnp.where(segments == g, 1.0, 0.0)).astype(jnp.int32) for g in range(GENES)]
    span = segments.size // GENES
    starts, before, start, free = [], [], 0, 0
    for g in range(GENES):
        starts.append(start)
        before.append(free)
        start = start + lengths[g]
        free = free + span - lengths[g]
    return [jnp.asarray(v, jnp.int32) for v in lengths + starts + before + [start]]


def source_of_slots(plan, gene, slots):
    length = plan[gene]
    return jnp.where(
        slots < length,
        plan[GENES + gene] + slots,
        plan[3 * GENES] + plan[2 * GENES + gene] + slots - length,
    )


def prepare_kernel(seg_ref, x_ref, c_ref, freq_ref, plan_ref, xp_ref, cp_ref, cos_ref, sin_ref):
    gene = pl.program_id(0)
    span = xp_ref.shape[0]
    length = x_ref.shape[0]

    @pl.when(gene == 0)
    def _():
        for i, v in enumerate(plan_of(seg_ref[...])):
            plan_ref[i] = v

    slots = iota((span, 1), 0)
    source = source_of_slots(plan_ref, gene, slots)
    pick = jnp.where(iota((span, length), 1) == source, 1.0, 0.0).astype(BF16)
    xp_ref[...] = nn(pick, x_ref[...]).astype(BF16)
    cp_ref[...] = nn(pick, c_ref[...]).astype(BF16)
    start = jnp.where(slots < plan_ref[gene], plan_ref[GENES + gene], plan_ref[3 * GENES])
    angle = (source - start).astype(F32) * freq_ref[...]
    low = iota((span, LANES), 1) % HEAD_DIM < HEAD_DIM // 2
    cos_ref[...] = jnp.cos(angle)
    sine = jnp.sin(angle)
    sin_ref[...] = jnp.where(low, -sine, sine)


def prepare(segments, x, c):
    length, width = x.shape
    span = length // GENES
    frequency = np.power(10000.0, np.arange(HEAD_DIM // 2) * (-2.0 / HEAD_DIM))
    frequency = jnp.asarray(np.tile(frequency, LANES // (HEAD_DIM // 2))[None], F32)
    return call(
        prepare_kernel,
        (GENES,),
        [full((1, length)), full((length, width)), full((length, width)), full((1, LANES))],
        [
            pl.BlockSpec(memory_space=pltpu.SMEM),
            rows_of((span, width)),
            rows_of((span, width)),
            rows_of((span, LANES)),
            rows_of((span, LANES)),
        ],
        [
            shape_of((16,), jnp.int32),
            shape_of((length, width), BF16),
            shape_of((length, width), BF16),
            shape_of((length, LANES), F32),
            shape_of((length, LANES), F32),
        ],
        prefetch=0,
        name="prepare",
        cost=(3.3e9, 8e6),
    )(segments, x, c, frequency)


def far_piece(refs, half, dz, dx, dy, dc):
    refs = refs[4 * dc : 4 * dc + 4]
    ref, at = (refs[dx], (dy, dz - 1)) if half == 0 else (refs[2 + dy], (dx, dz - 1))
    return ref.at[(half,) + at] if len(ref.shape) == 5 else ref.at[at]


def load_matrices(at, source, wqkv_ref, wout_ref, sem):
    width = wout_ref.shape[0]
    rows = width // (4 * Z_SIZE)
    own = at_rows((at[0] * 2 + at[1]) * 2 * rows, 2 * rows)
    pltpu.make_async_copy(source[0], wqkv_ref.at[own], sem.at[0]).start()
    pltpu.make_async_copy(source[1], wout_ref.at[own], sem.at[1]).start()

    def put(piece, f, y, c):
        down = at_rows((f * 2 + c) * rows, rows)
        for b in range(4):
            src = piece(b // 2).at[pl.ds((b % 2) * rows, rows)]
            across = at_columns((b % 3) * width + y * COLUMNS, COLUMNS)
            dst = wqkv_ref if b < 3 else wout_ref
            pltpu.make_async_copy(src, dst.at[down, across], sem.at[b // 3]).start()

    for dc in range(2):
        f, _, c = spot(at, 0, 1, 0, dc)
        for y in range(2):
            put(lambda half: source[2 + dc].at[y, half, pl.ds(0, 2 * rows)], f, y, c)

    def one(dz, carry):
        for dx, dy, dc in EVERY:
            put(lambda half: far_piece(source[4:], half, dz, dx, dy, dc), *spot(at, dz, dx, dy, dc))
        return carry

    lax.fori_loop(1, Z_SIZE, one, 0)


def attend_kernel(plan, at, *refs, pieces):
    (xp_ref, cos_ref, sin_ref, g1_ref, b1_ref, bqkv_ref, bout_ref), refs = refs[:7], refs[7:]
    source, refs = (refs[:12], refs[12:]) if pieces else (refs[:2], refs[2:])
    (qkv_ref, o_ref, lse_ref, x1_ref), refs = refs[:4], refs[4:]
    if pieces:
        whole, refs = refs[:2], refs[2:]
    wqkv_ref, wout_ref, mask_ref, a1_ref, sem = refs
    step = pl.program_id(0)
    gene = jnp.maximum(step - 1, 0)
    span = cos_ref.shape[0]
    width = xp_ref.shape[1]

    def wait_both():
        pltpu.make_async_copy(wqkv_ref, wqkv_ref, sem.at[0]).wait()
        pltpu.make_async_copy(wout_ref, wout_ref, sem.at[1]).wait()

    @pl.when(step == 0)
    def _():
        if pieces:
            load_matrices(at, source, wqkv_ref, wout_ref, sem)
        else:
            pltpu.make_async_copy(source[0], wqkv_ref, sem.at[0]).start()
            pltpu.make_async_copy(source[1], wout_ref, sem.at[1]).start()

        def norm(i, carry):
            here = pl.ds(i * span, span)
            xhat, _ = normalize(xp_ref[here, :].astype(F32))
            a1_ref[here, :] = (xhat * g1_ref[...] + b1_ref[...]).astype(BF16)
            return carry

        lax.fori_loop(0, GENES, norm, 0)
        wait_both()
        if pieces:
            pltpu.make_async_copy(wqkv_ref, whole[0], sem.at[0]).start()
            pltpu.make_async_copy(wout_ref, whole[1], sem.at[1]).start()

    @pl.when(step > 0)
    def _():
        attend_gene(
            plan, gene, xp_ref, a1_ref, cos_ref, sin_ref, bqkv_ref, bout_ref, wqkv_ref, wout_ref, mask_ref,
            qkv_ref, o_ref, lse_ref, x1_ref,
        )

    if pieces:

        @pl.when(step == pl.num_programs(0) - 1)
        def _():
            wait_both()


def attend_gene(
    plan, gene, xp_ref, a1_ref, cos_ref, sin_ref, bqkv_ref, bout_ref, wqkv_ref, wout_ref, mask_ref,
    qkv_ref, o_ref, lse_ref, x1_ref,
):
    span, width = o_ref.shape
    here = pl.ds(gene * span, span)
    x = xp_ref[here, :].astype(F32)
    a1 = a1_ref[here, :]
    cos, sin = cos_ref[...], sin_ref[...]
    for part in range(3):
        base = part * width
        t = nn(a1, wqkv_ref[:, base : base + width]) + bqkv_ref[:, base : base + width]
        for p in range(width // LANES):
            piece = t[:, p * LANES : (p + 1) * LANES]
            if part < 2:
                piece = piece * cos + swap_halves(piece) * sin
            qkv_ref[:, base + p * LANES : base + (p + 1) * LANES] = piece.astype(BF16)
    mask_ref[...] = jnp.where(allowed_pairs(plan, gene, span), 1.0, 0.0)
    masks = head_masks(span)
    def pair(p, carry):
        part = lambda i: at_columns(i * width + p * LANES, LANES)
        q = qkv_ref[:, part(0)]
        k = qkv_ref[:, part(1)] * BF16(1.0 / math.sqrt(HEAD_DIM))
        v = qkv_ref[:, part(2)]
        s = nt(both(masks, k), q).reshape(2, span, span)
        s = jnp.where((mask_ref[...] > 0.5)[None], s, NEG_FILL)
        peak = jnp.max(s, 1, keepdims=True)
        e = jnp.exp(s - peak)
        total = jnp.sum(e, 1, keepdims=True)
        weights = (e * (1.0 / total)).astype(BF16).reshape(2 * span, span)
        lse = peak + jnp.log(total)
        for h in range(2):
            lse_ref[pl.ds(2 * p + h, 1), :] = lse[h]
        o_ref[:, part(0)] = tn(weights, both(masks, v)).astype(BF16)
        return carry

    lax.fori_loop(0, width // LANES, pair, 0, unroll=True)
    x1_ref[...] = x + nn(o_ref[...], wout_ref[...]) + bout_ref[...]


def attend(plan, at, xp, cos, sin, g1, b1, bqkv, bout, source):
    length, width = xp.shape
    span = length // GENES
    pieces = len(source) == 12
    behind = lambda shape: pl.BlockSpec(shape, lambda g, *ids: (jnp.maximum(g - 1, 0), 0))
    weights = [shape_of((width, 3 * width), BF16), shape_of((width, width), BF16)]
    got = call(
        functools.partial(attend_kernel, pieces=pieces),
        (GENES + 1,),
        [
            full((length, width)),
            behind((span, LANES)),
            behind((span, LANES)),
            full((1, width)),
            full((1, width)),
            full((1, 3 * width)),
            full((1, width)),
        ]
        + [ANY] * len(source),
        [
            behind((span, 3 * width)),
            behind((span, width)),
            pl.BlockSpec((16, span), lambda g, *ids: (0, jnp.maximum(g - 1, 0))),
            behind((span, width)),
        ]
        + [ANY] * (2 if pieces else 0),
        [
            shape_of((length, 3 * width), BF16),
            shape_of((length, width), BF16),
            shape_of((16, length), F32),
            shape_of((length, width), F32),
        ]
        + (weights if pieces else []),
        [
            pltpu.VMEM((width, 3 * width), BF16),
            pltpu.VMEM((width, width), BF16),
            pltpu.VMEM((span, span), F32),
            pltpu.VMEM((length, width), BF16),
            pltpu.SemaphoreType.DMA((2,)),
        ],
        prefetch=2,
        name="attend",
        cost=(11e9, 20e6),
    )(plan, at, xp, cos, sin, g1, b1, bqkv, bout, *source)
    return got[:4], (got[4:] if pieces else source)


def feed_kernel(at, *refs, block, pieces, steps):
    (x1_hbm, c_hbm, g2_ref, b2_ref, bup_ref, bdown_ref), refs = refs[:6], refs[6:]
    source, refs = (refs[:12], refs[12:]) if pieces else (refs[:2], refs[2:])
    (out_hbm, dx1_hbm, da_hbm, gbup_ref, sums_ref, first_ref, second_ref), refs = refs[:7], refs[7:]
    x1_ref, c_ref, out_ref, da_ref, a2_ref, acc_ref, dh_ref, gr_ref, du_ref = refs[:9]
    wups, wdowns, gups, gdowns, load_sem, store_sem, in_sem, out_sem = refs[9:]
    step = pl.program_id(0)
    length, width = x1_ref.shape
    chunk = bup_ref.shape[1]
    blocks = length // block
    slot = lax.rem(step, 2)
    rows = width // (4 * Z_SIZE)

    def load(j, to):
        if pieces:
            own = at_rows((at[0] * 2 + at[1]) * 2 * rows, 2 * rows)
            src = source[0].at[:, at_columns(j * chunk, chunk)]
            pltpu.make_async_copy(src, wups.at[to, own], load_sem.at[0, to]).start()

            def put_up(piece, f, y, c):
                dst = wups.at[to, at_rows((f * 2 + c) * rows, rows), at_columns(y * COLUMNS, COLUMNS)]
                pltpu.make_async_copy(piece.at[at_rows(j * rows, rows)], dst, load_sem.at[0, to]).start()

            def put_down(piece, x, y, c):
                dst = wdowns.at[to, at_rows((x * 2 + c) * 4 * rows, 4 * rows), at_columns(y * COLUMNS, COLUMNS)]
                pltpu.make_async_copy(piece, dst, load_sem.at[1, to]).start()

            for dc in range(2):
                f, _, c = spot(at, 0, 1, 0, dc)
                for y in range(2):
                    put_up(source[2 + dc].at[y, 0, pl.ds(2 * rows, 4 * rows)], f, y, c)

            def one(dz, carry):
                for dx, dy, dc in EVERY:
                    put_up(far_piece(source[4:], 0, dz, dx, dy, dc), *spot(at, dz, dx, dy, dc))
                return carry

            lax.fori_loop(1, Z_SIZE, one, 0)

            @pl.when(j == at[0])
            def _():
                here = at_rows(at[1] * 8 * rows, 8 * rows)
                pltpu.make_async_copy(source[1], wdowns.at[to, here], load_sem.at[1, to]).start()
                for dc in range(2):
                    _, _, c = spot(at, 0, 1, 0, dc)
                    for y in range(2):
                        put_down(source[2 + dc].at[y, 1, pl.ds(2 * rows, 4 * rows)], 1 - at[1], y, c)

            @pl.when(j != at[0])
            def _():
                back = lax.rem(at[0] + (Z_SIZE - j), Z_SIZE)
                for dx, dy, dc in EVERY:
                    _, y, c = spot(at, back, dx, dy, dc)
                    put_down(far_piece(source[4:], 1, back, dx, dy, dc), lax.bitwise_xor(at[1], dx), y, c)

        else:
            part = source[0].at[:, at_columns(j * chunk, chunk)]
            pltpu.make_async_copy(part, wups.at[to], load_sem.at[0, to]).start()
            part = source[1].at[at_rows(j * chunk, chunk), :]
            pltpu.make_async_copy(part, wdowns.at[to], load_sem.at[1, to]).start()

    def store(j, to):
        if pieces:

            def one(dz, carry):
                for dx, dy, dc in EVERY:
                    f, y, c = spot(at, Z_SIZE - dz, dx, dy, dc)
                    src = gups.at[to, at_rows(f * 2 * rows + c * rows, rows), at_columns(y * COLUMNS, COLUMNS)]
                    dst = (first_ref, second_ref)[dc].at[piece_index(0, dz, dx, dy), at_rows(j * rows, rows)]
                    pltpu.make_async_copy(src, dst, store_sem.at[0, to]).start()
                return carry

            lax.fori_loop(0, Z_SIZE, one, 0)
            ahead = lax.rem(j + Z_SIZE - at[0], Z_SIZE)
            for dx, dy, dc in EVERY:
                f, y, c = spot(at, 0, dx, dy, dc)
                x = lax.bitwise_xor(at[1], dx)
                src = gdowns.at[to, at_rows((x * 2 + c) * 4 * rows, 4 * rows), at_columns(y * COLUMNS, COLUMNS)]
                dst = (first_ref, second_ref)[dc].at[piece_index(1, ahead, dx, dy)]
                pltpu.make_async_copy(src, dst, store_sem.at[1, to]).start()
        else:
            part = first_ref.at[:, at_columns(j * chunk, chunk)]
            pltpu.make_async_copy(gups.at[to], part, store_sem.at[0, to]).start()
            part = second_ref.at[at_rows(j * chunk, chunk), :]
            pltpu.make_async_copy(gdowns.at[to], part, store_sem.at[1, to]).start()

    def wait_load(to):
        pltpu.make_async_copy(wups.at[to], wups.at[to], load_sem.at[0, to]).wait()
        pltpu.make_async_copy(wdowns.at[to], wdowns.at[to], load_sem.at[1, to]).wait()

    def wait_store(to):
        pltpu.make_async_copy(gups.at[to], gups.at[to], store_sem.at[0, to]).wait()
        pltpu.make_async_copy(gdowns.at[to], gdowns.at[to], store_sem.at[1, to]).wait()

    def bring(i):
        here = at_rows(i * block, block)
        return [
            pltpu.make_async_copy(x1_hbm.at[here, :], x1_ref.at[here, :], in_sem.at[0, i]),
            pltpu.make_async_copy(c_hbm.at[here, :], c_ref.at[here, :], in_sem.at[1, i]),
        ]

    def give(i):
        here = at_rows(i * block, block)
        return [
            pltpu.make_async_copy(out_ref.at[here, :], out_hbm.at[here, :], out_sem.at[0, i]),
            pltpu.make_async_copy(x1_ref.at[here, :], dx1_hbm.at[here, :], out_sem.at[1, i]),
            pltpu.make_async_copy(da_ref.at[here, :], da_hbm.at[here, :], out_sem.at[2, i]),
        ]

    @pl.when(step == 0)
    def _():
        for i in range(blocks):
            bring(i)[0].start()
        load(0, 0)
        for i in range(blocks):
            bring(i)[1].start()

        def one(i, carry):
            here = pl.ds(i * block, block)
            bring(i)[0].wait()
            xhat, _ = normalize(x1_ref[here, :])
            a2_ref[here, :] = (xhat * g2_ref[...] + b2_ref[...]).astype(BF16)
            acc_ref[here, :] = jnp.zeros((block, width), F32)
            dh_ref[here, :] = jnp.zeros((block, width), F32)
            return carry

        lax.fori_loop(0, blocks, one, 0)
        for i in range(blocks):
            bring(i)[1].wait()

    wait_load(slot)

    @pl.when(step < steps - 1)
    def _():
        load(step + 1, 1 - slot)

    wup_ref, wdown_ref = wups.at[slot], wdowns.at[slot]

    def one(i, bias_sum):
        here = pl.ds(i * block, block)
        u = nn(a2_ref[here, :], wup_ref[...]) + bup_ref[...]
        phi = 0.5 + 0.5 * lax.erf(u * math.sqrt(0.5))
        slope = phi + u * (jnp.exp(-0.5 * u * u) * (1.0 / math.sqrt(2.0 * math.pi)))
        gr = (u * phi).astype(BF16)
        gr_ref[here, :] = gr
        du = (nt(c_ref[here, :], wdown_ref[...]) * slope).astype(BF16)
        du_ref[here, :] = du
        out = nn(gr, wdown_ref[...])
        dh = nt(du, wup_ref[...])

        acc_ref[here, :] += out
        dh_ref[here, :] += dh
        return bias_sum + jnp.sum(du.astype(F32), 0, keepdims=True)

    gbup_ref[...] = lax.fori_loop(0, blocks, one, jnp.zeros((1, chunk), F32))

    @pl.when(step >= 2)
    def _():
        wait_store(slot)

    gdowns[slot] = tn(gr_ref[...], c_ref[...]).astype(BF16)
    gups[slot] = tn(a2_ref[...], du_ref[...]).astype(BF16)
    store(step, slot)

    @pl.when(step == steps - 1)
    def _():
        def one(i, sums):
            here = pl.ds(i * block, block)
            x1 = x1_ref[here, :]
            xhat, scale = normalize(x1)
            out_ref[here, :] = (x1 + acc_ref[here, :] + bdown_ref[...]).astype(BF16)
            dh = dh_ref[here, :]
            c = c_ref[here, :].astype(F32)
            e = dh * g2_ref[...]
            dx1 = c + scale * (
                e - jnp.mean(e, -1, keepdims=True) - xhat * jnp.mean(e * xhat, -1, keepdims=True)
            )
            x1_ref[here, :] = dx1
            da = dx1.astype(BF16)
            da_ref[here, :] = da
            for copy in give(i):
                copy.start()
            new = (
                jnp.sum(dh * xhat, 0, keepdims=True),
                jnp.sum(dh, 0, keepdims=True),
                jnp.sum(c, 0, keepdims=True),
                jnp.sum(da.astype(F32), 0, keepdims=True),
            )
            return tuple(a + b for a, b in zip(sums, new))

        sums = lax.fori_loop(0, blocks, one, (jnp.zeros((1, width), F32),) * 4)
        for i in range(4):
            sums_ref[i : i + 1, :] = sums[i]
        for i in range(blocks):
            for copy in give(i):
                copy.wait()
        wait_store(1 - slot)
        wait_store(slot)


def feed(at, x1, c, g2, b2, bup, bdown, source):
    length, width = x1.shape
    hidden = bup.shape[1]
    steps = 4
    chunk = hidden // steps
    pieces = len(source) == 12
    if pieces:
        rows = width // Z_SIZE
        stored = [shape_of((PIECES, rows, COLUMNS), BF16)] * 2
    else:
        stored = [shape_of((width, hidden), BF16), shape_of((hidden, width), BF16)]
    return call(
        functools.partial(feed_kernel, block=length // 2, pieces=pieces, steps=steps),
        (steps,),
        [
            ANY,
            ANY,
            full((1, width)),
            full((1, width)),
            pl.BlockSpec((1, chunk), lambda j, *ids: (0, j)),
            full((1, width)),
        ]
        + [ANY] * len(source),
        [
            ANY,
            ANY,
            ANY,
            pl.BlockSpec((1, chunk), lambda j, *ids: (0, j)),
            full((8, width)),
            ANY,
            ANY,
        ],
        [
            shape_of((length, width), BF16),
            shape_of((length, width), F32),
            shape_of((length, width), BF16),
            shape_of((1, hidden), F32),
            shape_of((8, width), F32),
        ]
        + stored,
        [
            pltpu.VMEM((length, width), F32),
            pltpu.VMEM((length, width), BF16),
            pltpu.VMEM((length, width), BF16),
            pltpu.VMEM((length, width), BF16),
            pltpu.VMEM((length, width), BF16),
            pltpu.VMEM((length, width), F32),
            pltpu.VMEM((length, width), F32),
            pltpu.VMEM((length, chunk), BF16),
            pltpu.VMEM((length, chunk), BF16),
            pltpu.VMEM((2, width, chunk), BF16),
            pltpu.VMEM((2, chunk, width), BF16),
            pltpu.VMEM((2, width, chunk), BF16),
            pltpu.VMEM((2, chunk, width), BF16),
            pltpu.SemaphoreType.DMA((2, 2)),
            pltpu.SemaphoreType.DMA((2, 2)),
            pltpu.SemaphoreType.DMA((2, 4)),
            pltpu.SemaphoreType.DMA((3, 4)),
        ],
        name="feed",
        cost=(29e9, 40e6),
    )(at, x1, c, g2, b2, bup, bdown, *source)


def attend_back_kernel(
    plan, qkv_ref, da_ref, lse_ref, cos_ref, sin_ref, wout_ref, *refs, base, count,
):
    dqkv_ref, bias_ref, dout_ref, mask_ref = refs[-4:]
    gene = pl.program_id(0) + base
    span, width = da_ref.shape
    score_scale = 1.0 / math.sqrt(HEAD_DIM)
    dout_ref[...] = nt(da_ref[...], wout_ref[...]).astype(BF16)
    mask_ref[...] = jnp.where(allowed_pairs(plan, gene, span), 1.0, 0.0)
    cos, sin = cos_ref[...], sin_ref[...]
    masks = head_masks(span)

    def back(t):
        return (t * cos - swap_halves(t) * sin).astype(BF16)

    def pair(p, carry):
        part = lambda i: at_columns(i * width + p * LANES, LANES)
        q = qkv_ref[:, part(0)]
        k = qkv_ref[:, part(1)] * BF16(score_scale)
        v = qkv_ref[:, part(2)]
        dout = dout_ref[:, part(0)]
        kh = both(masks, k)
        s = nt(kh, q).reshape(2, span, span)
        s = jnp.where((mask_ref[...] > 0.5)[None], s, NEG_FILL)
        weights = jnp.exp(s - stack(lse_ref[pl.ds(2 * p + h, 1), :] for h in range(2)))
        dw = nt(both(masks, v), dout).reshape(2, span, span)
        dot = jnp.sum(weights * dw, 1, keepdims=True)
        ds = (weights * (dw - dot)).astype(BF16)
        weights = weights.astype(BF16)
        dv = nn(beside(weights), both(masks, dout))
        dk = nn(beside(ds), both(masks, q))
        dq = tn(ds.reshape(2 * span, span), kh)
        dqkv_ref[:, part(0)] = back(dq)
        dqkv_ref[:, part(1)] = back(dk * score_scale)
        dqkv_ref[:, part(2)] = dv.astype(BF16)
        return carry

    lax.fori_loop(0, width // LANES, pair, 0, unroll=2 if count == 1 else True)

    bqkv = jnp.sum(dqkv_ref[...].astype(F32), 0, keepdims=True)

    @pl.when(gene == base)
    def _():
        bias_ref[0:1, :] = bqkv

    @pl.when(gene > base)
    def _():
        bias_ref[0:1, :] += bqkv


def attend_back(plan, qkv, da, lse, cos, sin, wout, base, count, before=()):
    length, width = da.shape
    span = length // GENES
    rows = lambda shape: pl.BlockSpec(shape, lambda g, *ids: (g + base, 0))
    return call(
        functools.partial(attend_back_kernel, base=base, count=count),
        (count,),
        [
            rows((span, 3 * width)),
            rows((span, width)),
            pl.BlockSpec((16, span), lambda g, *ids: (0, g + base)),
            rows((span, LANES)),
            rows((span, LANES)),
            full((width, width)),
        ]
        + [ANY] * len(before),
        [rows((span, 3 * width)), full((8, 3 * width))],
        [shape_of((length, 3 * width), BF16), shape_of((8, 3 * width), F32)],
        [pltpu.VMEM((span, width), BF16), pltpu.VMEM((span, span), F32)],
        name="attend_back",
        cost=(4e9 * count, 6e6 * count),
        aliases={7 + i: i for i in range(len(before))},
    )(plan, qkv, da, lse, cos, sin, wout, *before)


def project_back_kernel(xp_ref, g1_ref, dx1_ref, dqkv_ref, wqkv_ref, dxp_ref, sums_ref):
    step = pl.program_id(0)
    dh = nt(dqkv_ref[...], wqkv_ref[...])
    xhat, scale = normalize(xp_ref[...].astype(F32))
    e = dh * g1_ref[...]
    dx = dx1_ref[...] + scale * (
        e - jnp.mean(e, -1, keepdims=True) - xhat * jnp.mean(e * xhat, -1, keepdims=True)
    )
    dxp_ref[...] = dx.astype(BF16)

    @pl.when(step == 0)
    def _():
        sums_ref[...] = jnp.zeros_like(sums_ref)

    sums_ref[0:1, :] += jnp.sum(dh * xhat, 0, keepdims=True)
    sums_ref[1:2, :] += jnp.sum(dh, 0, keepdims=True)


def project_back(xp, g1, dx1, dqkv, wqkv):
    length, width = xp.shape
    span = length // GENES
    return call(
        project_back_kernel,
        (GENES,),
        [
            rows_of((span, width)),
            full((1, width)),
            rows_of((span, width)),
            rows_of((span, 3 * width)),
            full((width, 3 * width)),
        ],
        [rows_of((span, width)), full((8, width))],
        [shape_of((length, width), BF16), shape_of((8, width), F32)],
        prefetch=0,
        name="project_back",
        cost=(0, 0),
    )(xp, g1, dx1, dqkv, wqkv)


def grads_kernel(at, *refs, pieces):
    (xp_hbm, o_hbm, da_hbm, dqkv_hbm, g1_ref, b1_ref), refs = refs[:6], refs[6:]
    sums, refs = (refs[:5], refs[5:]) if pieces else ((), refs)
    first_ref, second_ref, xp_ref, o_ref, da_ref, dqkv_ref, a1_ref, grad_ref, in_sem, sem, *rest = refs
    small_ref, small_sem = rest if pieces else (None, None)
    step = pl.program_id(0)
    width = xp_ref.shape[1]
    rows = width // (4 * Z_SIZE)
    slot = lax.rem(step, 2)

    def bring(j):
        part = dqkv_hbm.at[:, at_columns(j * width, width)]
        return pltpu.make_async_copy(part, dqkv_ref.at[lax.rem(j, 2)], in_sem.at[3 + lax.rem(j, 2)])

    whole = [
        pltpu.make_async_copy(src, dst, in_sem.at[i])
        for i, (src, dst) in enumerate(((o_hbm, o_ref), (da_hbm, da_ref), (xp_hbm, xp_ref)))
    ]

    def wait(to):
        pltpu.make_async_copy(grad_ref.at[to], grad_ref.at[to], sem.at[to]).wait()

    def store(half, base, to):
        def one(dz, carry):
            for dx, dy, dc in EVERY:
                f, y, c = spot(at, Z_SIZE - dz, dx, dy, dc)
                src = grad_ref.at[to, at_rows(f * 2 * rows + c * rows, rows), at_columns(y * COLUMNS, COLUMNS)]
                dst = (first_ref, second_ref)[dc].at[
                    jnp.where(half == 0, piece_index(0, dz, dx, dy), piece_index(1, dz, dx, dy)),
                    at_rows(base * rows, rows),
                ]
                pltpu.make_async_copy(src, dst, sem.at[to]).start()
            return carry

        lax.fori_loop(0, Z_SIZE, one, 0)

    def pack():
        sums1, low_ref, high_ref, sums2, gbup = sums
        line = lambda ref, i: ref[i : i + 1, :]
        vectors = [
            line(sums1, 0), line(sums1, 1), line(low_ref, 0) + line(high_ref, 0), line(sums2, 3),
            line(sums2, 0), line(sums2, 1), gbup[...], line(sums2, 2),
        ]
        shards = 2 * Z_SIZE
        columns = []
        for value in vectors:
            size = value.shape[1] // shards
            spread_out = jnp.broadcast_to(value, (shards, value.shape[1]))
            mask = iota(spread_out.shape, 1) // size == iota(spread_out.shape, 0)
            own = jnp.where(mask, spread_out, 0.0).astype(BF16)
            columns.append(nt(own, spread(size, value.shape[1])).astype(BF16))
        packed = jnp.concatenate(columns, 1).astype(F32)
        for f in range(shards):
            for i in range(4):
                part = packed[f : f + 1, i * COLUMNS : (i + 1) * COLUMNS]
                small_ref[f, i // 2, i % 2] = jnp.broadcast_to(part, (8, COLUMNS)).astype(BF16)

    def smalls(act):
        def one(dz, carry):
            for dx, dy, dc in EVERY:
                f, y, c = spot(at, Z_SIZE - dz, dx, dy, dc)
                for half in range(2):
                    src = small_ref.at[f, y, c]
                    dst = (first_ref, second_ref)[dc].at[piece_index(half, dz, dx, dy), pl.ds(2 * rows, 8)]
                    act(pltpu.make_async_copy(src, dst, small_sem))
            return carry

        lax.fori_loop(0, Z_SIZE, one, 0)

    @pl.when(step == 0)
    def _():
        for copy in whole:
            copy.start()
        bring(step).start()
        if pieces:
            pack()
            smalls(lambda copy: copy.start())
        whole[0].wait()
        whole[1].wait()
        grad_ref[0] = tn(o_ref[...], da_ref[...]).astype(BF16)
        if pieces:
            store(1, 1, 0)
        else:
            pltpu.make_async_copy(grad_ref.at[0], second_ref, sem.at[0]).start()
        whole[2].wait()
        xhat, _ = normalize(xp_ref[...].astype(F32))
        a1_ref[...] = (xhat * g1_ref[...] + b1_ref[...]).astype(BF16)

    @pl.when(step > 0)
    def _():
        bring(step - 1).wait()

        @pl.when(step < 3)
        def _():
            bring(step).start()

        @pl.when(step >= 2)
        def _():
            wait(slot)

        grad_ref[slot] = tn(a1_ref[...], dqkv_ref[lax.rem(step - 1, 2)]).astype(BF16)
        if pieces:
            store(lax.div(step - 1, 2), lax.rem(step - 1, 2), slot)
        else:
            dst = first_ref.at[:, at_columns((step - 1) * width, width)]
            pltpu.make_async_copy(grad_ref.at[slot], dst, sem.at[slot]).start()

    @pl.when(step == 3)
    def _():
        wait(0)
        wait(1)
        if pieces:
            smalls(lambda copy: copy.wait())


def grads(at, xp, g1, b1, o, da, dqkv, sums):
    pieces = bool(sums)
    length, width = xp.shape
    if pieces:
        rows = width // (2 * Z_SIZE) + 8
        stored = [shape_of((PIECES, rows, COLUMNS), BF16)] * 2
    else:
        stored = [shape_of((width, 3 * width), BF16), shape_of((width, width), BF16)]
    return call(
        functools.partial(grads_kernel, pieces=pieces),
        (4,),
        [ANY] * 4 + [full((1, width))] * 2 + [full(v.shape) for v in sums],
        [ANY, ANY],
        stored,
        [pltpu.VMEM((length, width), BF16)] * 3
        + [
            pltpu.VMEM((2, length, width), BF16),
            pltpu.VMEM((length, width), BF16),
            pltpu.VMEM((2, width, width), BF16),
            pltpu.SemaphoreType.DMA((5,)),
            pltpu.SemaphoreType.DMA((2,)),
        ]
        + ([pltpu.VMEM((2 * Z_SIZE, 2, 2, 8, COLUMNS), BF16), pltpu.SemaphoreType.DMA] if pieces else []),
        name="grads",
        cost=(5e9, 12e6),
    )(at, xp, o, da, dqkv, g1, b1, *sums)


def restore_kernel(plan, outp_ref, dxp_ref, out_ref, dx_ref):
    span, width = out_ref.shape
    slots = iota((1, span), 1)
    source = jnp.concatenate([source_of_slots(plan, g, slots) for g in range(GENES)], 1)
    codon = iota((span, outp_ref.shape[0]), 0) + pl.program_id(0) * span
    pick = jnp.where(codon == source, 1.0, 0.0).astype(BF16)
    out_ref[...] = nn(pick, outp_ref[...]).astype(BF16)
    dx_ref[...] = nn(pick, dxp_ref[...]).astype(BF16)


def restore(plan, outp, dxp):
    length, width = outp.shape
    span = length // GENES
    return call(
        restore_kernel,
        (GENES,),
        [full((length, width)), full((length, width))],
        [rows_of((span, width))] * 2,
        [shape_of((length, width), BF16)] * 2,
        name="restore",
        cost=(3.3e9, 8e6),
    )(plan, outp, dxp)


def deliver_first_kernel(at, mine, other, wqkv, wout, *rest):
    vectors, row_ref = rest[:8], rest[8]
    width = wout.shape[1]
    rows = wout.shape[0] // 2
    for dc, one in enumerate((mine, other)):
        c = lax.bitwise_xor(at[3], dc)
        here = pl.ds(pl.multiple_of(c * rows, 8), rows)
        for y in range(2):
            for b in range(4):
                ref, base = (wqkv, b * width) if b < 3 else (wout, 0)
                start = base + y * COLUMNS
                piece = one[y, b // 2, (b % 2) * rows : (b % 2 + 1) * rows, :]
                ref[here, start : start + COLUMNS] = piece.astype(F32)
            start = at_columns((y * 2 + c) * COLUMNS, COLUMNS)
            row_ref[:, start] = one[y, 0, 2 * rows : 2 * rows + 8, :].astype(F32)
    for ref, start in zip(vectors, SLOTS):
        ref[...] = row_ref[0:1, start : start + ref.shape[0]].reshape(ref.shape[0])


def deliver_first(at, mine, other, sizes):
    rows = (mine.shape[2] - 8) // 2
    width = 2 * COLUMNS
    shapes = [(2 * rows, 3 * width), (2 * rows, width)] + [(n,) for n in sizes]
    return call(
        deliver_first_kernel,
        (1,),
        [pl.BlockSpec(memory_space=pltpu.VMEM)] * 2,
        [full(s) for s in shapes],
        [shape_of(s, F32) for s in shapes],
        [pltpu.VMEM((8, PACKED), F32)],
        name="deliver_first",
        cost=(0, 2e6),
    )(at, mine, other)


def deliver_second_kernel(at, mine, other, wup, wdown):
    width = wdown.shape[1]
    rows = wup.shape[0] // 2
    for dc, two in enumerate((mine, other)):
        c = lax.bitwise_xor(at[3], dc)
        here = pl.ds(pl.multiple_of(c * rows, 8), rows)
        down = pl.ds(pl.multiple_of(c * 4 * rows, 8), 4 * rows)
        for y in range(2):
            for b in range(4):
                start = b * width + y * COLUMNS
                wup[here, start : start + COLUMNS] = two[y, 0, b * rows : (b + 1) * rows, :].astype(F32)
            wdown[down, y * COLUMNS : (y + 1) * COLUMNS] = two[y, 1].astype(F32)


def deliver_second(at, mine, other):
    rows = mine.shape[2] // 4
    width = 2 * COLUMNS
    shapes = [(2 * rows, 4 * width), (8 * rows, width)]
    return call(
        deliver_second_kernel,
        (1,),
        [pl.BlockSpec(memory_space=pltpu.VMEM)] * 2,
        [full(s) for s in shapes],
        [shape_of(s, F32) for s in shapes],
        name="deliver_second",
        cost=(0, 4e6),
    )(at, mine, other)


def gather(shard):
    return lax.all_gather(shard, "fsdp", axis=0, tiled=True)


def reduce_rows(grad):
    part = lax.psum_scatter(grad, "fsdp", scatter_dimension=0, tiled=True)
    return lax.psum(part.astype(BF16), "replica").astype(F32)


def low(value):
    return value.astype(BF16)


def add(*values):
    total = values[0].astype(F32)
    for v in values[1:]:
        total = total + v.astype(F32)
    return total


def to_z(arrays):
    arrays = arrays if isinstance(arrays, list) else [arrays] * 3
    return [move(v, ALONG_Z[d]) for d, v in zip((1, 2, 3), arrays)]


def over_x(array):
    return move(array, ACROSS_X)


def over_y(array):
    return move(array, ACROSS_Y)


def over_core(array):
    return move(array, ACROSS_CORE)


def stack(arrays):
    return jnp.stack(list(arrays))


class Sum:
    def __init__(self, kept, got):
        self.kept, self.got = kept, got

    def plane_one(self):
        return self.part(8, 16), self.part(24, 32)

    def part(self, start, stop, *more):
        return low(add(self.kept[start:stop], self.got[start:stop], *more))

    def plane_two(self, by_x, by_y):
        self.by_x, self.by_y = by_x, by_y
        return self.part(4, 8, by_x[Z_SIZE:]), self.part(20, 24, by_y[Z_SIZE:])

    def along_z(self, by_y, by_x):
        def at_z(d, rounded):
            first = add(self.kept[d], self.got[d], self.by_x[d], by_y[d])
            second = add(self.kept[16 + d], self.got[16 + d], self.by_y[d], by_x[d])
            return low(stack([first, second])) if rounded else stack([first, second])

        self.own = at_z(0, False)
        return [at_z(d, True) for d in range(1, Z_SIZE)]

    def total(self, by_z):
        return low(add(self.own, *by_z))


def settle(bit, mine, other):
    return jnp.where(bit == 0, stack([mine, other]), stack([other, mine]))


def body(
    layer_input, cotangent, segment_ids, pad_mask, ln1_gain, ln1_bias, w_qkv, b_qkv, w_out, b_out,
    ln2_gain, ln2_bias, w_up, b_up, w_down, b_down, *, tuned,
):
    vectors = (ln1_gain, ln1_bias, b_qkv, b_out, ln2_gain, ln2_bias, b_up, b_down)
    sizes = [v.shape[0] for v in vectors]
    x, c = layer_input[0], cotangent[0]
    if tuned:
        at = place()
        near1, near2, side = quarters(at, w_qkv, w_out, w_up, w_down, vectors)
        near1, near2, side, x = tie((near1, near2, side, x))
        z1 = to_z(near1)
        far_side = over_x(side)
        z2_one = move(near2, ALONG_Z[1])
        prepared = prepare(segment_ids, x, c)
        z1, z2_one, prepared = tie((z1, z2_one, prepared))
        plan, xp, cp, cos, sin = prepared

        count = near1.shape[1] - 8
        first1, second1 = stack(q[0, :count] for q in z1), stack(q[1] for q in z1)
        rows = stack(q[0, count:] for q in [near1] + z1)
        first1, second1, near2 = tie((first1, second1, near2))
        first_y, second_x = over_y(first1), over_x(second1)
        z2_three = move(near2, ALONG_Z[3])
        first_y, second_x, z2_three, near2, far_side = tie((first_y, second_x, z2_three, near2, far_side))

        near1 = stack([stack([first1, first_y]), stack([second1, second_x])[:, :, :count]])
        far_rows = jnp.concatenate([far_side[0, :1, 3 * count :], second_x[:, count:]])
        early = [stack(q[h] for q in (z2_one, z2_three)) for h in range(2)]
        unit = lambda v: v.reshape(-1, count // 2, COLUMNS)
        to_x, to_y = (jnp.concatenate([unit(near1[h]), unit(early[1 - h])]) for h in range(2))
        near1, to_x, to_y, rows, far_rows, near2, far_side, early = tie(
            (near1, to_x, to_y, rows, far_rows, near2, far_side, early)
        )
        by_x, by_y = over_x(to_x), over_y(to_y)
        near_core1, core_side = over_core(near1), over_core(far_side)
        z2_two = move(near2, ALONG_Z[2])
        params = unpack(at, rows, far_rows, sizes)
        by_x, by_y, near_core1, core_side, params, z2_two = tie(
            (by_x, by_y, near_core1, core_side, params, z2_two)
        )

        late = [z2_two[h : h + 1] for h in range(2)]
        units = unit(near1[0]).shape[0]
        far1 = stack([v[:units].reshape(near1.shape[1:]) for v in (by_x, by_y)])
        far1, late = tie((far1, late))
        far_core1 = over_core(far1)
        late_far = [over_y(late[0]), over_x(late[1])]
        late_far, far_core1 = tie((late_far, far_core1))

        attention = (w_qkv, w_out, far_side, core_side) + (near1, far1) * 2 + (near_core1, far_core1) * 2
        early_far = [v[units:].reshape(early[0].shape) for v in (by_y, by_x)]
        order = lambda e, l: jnp.concatenate([e[:1], l, e[1:]])
        first2, second2 = (
            stack([order(early[h], late[h]), order(early_far[h], late_far[h])]) for h in range(2)
        )
        first2, second2, attention, params, plan = tie((first2, second2, attention, params, plan))
        far_first2, far_second2 = over_x(first2), over_y(second2)
        core2 = [over_core(v) for v in (first2, second2)]
    else:
        at = jnp.zeros((4,), jnp.int32)
        plan, xp, cp, cos, sin = prepare(segment_ids, x, c)
        params = [gather(v[None]).reshape(1, -1).astype(F32) for v in vectors]
        attention = gather(w_qkv), gather(w_out)
        forward = gather(w_up), gather(w_down)
    g1, b1, bqkv, bout, g2, b2, bup, bdown = params
    (qkv, o, lse, x1), (wqkv, wout) = attend(plan, at, xp, cos, sin, g1, b1, bqkv, bout, attention)
    if tuned:
        far_first2, far_second2, core2, x1 = tie((far_first2, far_second2, core2, x1))
        far_core2 = over_core(far_first2), over_core(far_second2)
        forward = (
            w_up, w_down, far_side, core_side, first2, far_first2, second2, far_second2,
            core2[0], far_core2[0], core2[1], far_core2[1],
        )
    outp, dx1, da, gbup, sums2, *parts2 = feed(at, x1, cp, g2, b2, bup, bdown, forward)
    back = functools.partial(attend_back, plan, qkv, da, lse, cos, sin, wout)
    split = 1
    if tuned:
        kept2, sent2 = parts2
        got2 = over_core(sent2)
        dqkv, bias_low = back(0, split)
        got2, dqkv = tie((got2, dqkv))
        group2 = Sum(kept2, got2)
        to_x, to_y, dqkv = tie(group2.plane_one() + (dqkv,))
        by_x, by_y = over_x(to_x), over_y(to_y)
    else:
        dqkv, bias_low = back(0, split)
    dqkv, bias_high = back(split, GENES - split, (dqkv,))
    dxp, sums1 = project_back(xp, g1, dx1, dqkv, wqkv)
    sums = [sums1, bias_low, bias_high, sums2, gbup]
    if tuned:
        by_x, by_y, sums, dxp, dqkv = tie((by_x, by_y, sums, dxp, dqkv))
        to_y, to_x = group2.plane_two(by_x, by_y)
        to_y, to_x, dqkv = tie((to_y, to_x, dqkv))
        by_y, by_x = over_y(to_y), over_x(to_x)
        kept1, sent1 = grads(at, xp, g1, b1, o, da, dqkv, sums)
        by_y, by_x, kept1, sent1 = tie((by_y, by_x, kept1, sent1))
        got1 = over_core(sent1)
        got1, *to_z2 = tie([got1] + group2.along_z(by_y, by_x))
        group1 = Sum(kept1, got1)
        to_x, to_y, *to_z2 = tie([*group1.plane_one(), *to_z2])
        two = move(to_z2[1], ALONG_Z[2])
        by_x, by_y, two, *to_z2 = tie((over_x(to_x), over_y(to_y), two, to_z2[0], to_z2[2]))
        to_y, to_x, *to_z2 = tie([*group1.plane_two(by_x, by_y), *to_z2])
        one, three = move(to_z2[0], ALONG_Z[1]), move(to_z2[1], ALONG_Z[3])
        by_y, by_x, one, three = tie((over_y(to_y), over_x(to_x), one, three))
        z2 = one, two, three
        to_z1 = group1.along_z(by_y, by_x)
        total2 = group2.total(z2)
        to_z1, total2, outp, dxp = tie((to_z1, total2, outp, dxp))
        z1 = to_z(to_z1)
        by_y = over_y(total2)
        layer_out, input_grad = restore(plan, outp, dxp)
        z1, by_y, layer_out, input_grad = tie((z1, by_y, layer_out, input_grad))
        total1 = group1.total(z1)
        final2 = settle(at[2], total2, by_y)
        total1, final2 = tie((total1, final2))
        by_y, other2 = over_y(total1), over_core(final2)
        wup, wdown = deliver_second(at, final2, other2)
        by_y, wup, wdown = tie((by_y, wup, wdown))
        final1 = settle(at[2], total1, by_y)
        other1 = over_core(final1)
        wqkv, wout, *small = deliver_first(at, final1, other1, sizes)
    else:
        parts1 = grads(at, xp, g1, b1, o, da, dqkv, ())
        layer_out, input_grad = restore(plan, outp, dxp)
        wqkv, wout = map(reduce_rows, parts1)
        wup, wdown = map(reduce_rows, parts2)
        bias = bias_low + bias_high
        small = [sums1[0], sums1[1], bias[0], sums2[3], sums2[0], sums2[1], gbup[0], sums2[2]]
        small = [reduce_rows(v) for v in small]
    dg1, db1, dbqkv, dbout, dg2, db2, dbup, dbdown = small
    return (
        layer_out[None], input_grad[None], dg1, db1, wqkv, dbqkv, wout, dbout, dg2, db2,
        wup, dbup, wdown, dbdown,
    )


def solution(mesh):
    rows = ("fsdp", "replica")
    by_row = P(rows, None, None)
    vector, matrix = P("fsdp"), P("fsdp", None)
    params = (
        vector, vector, matrix, vector, matrix, vector, vector, vector, matrix, vector, matrix, vector,
    )
    in_specs = (by_row, by_row, P(rows, None), P(rows, None)) + params
    out_specs = (by_row, by_row) + params
    return jax.shard_map(
        functools.partial(body, tuned=tuned_mesh(mesh)),
        mesh=mesh, in_specs=in_specs, out_specs=out_specs, check_vma=False,
    )
```

```python
import functools
import math

import jax
import jax.numpy as jnp
import numpy as np
from jax import lax
from jax.experimental import pallas as pl
from jax.experimental.pallas import tpu as pltpu
from jax.sharding import PartitionSpec as P

HEADS = 12
HEAD_DIM = 64
GENES = 4
LANES = 128
EPSILON = 1e-05
NEG_FILL = -1000000000.0
F32 = jnp.float32
BF16 = jnp.bfloat16
MIB = 1 << 20


def nn(left, right):
    return lax.dot_general(left, right, (((1,), (0,)), ((), ())), preferred_element_type=F32)


def nt(left, right):
    return lax.dot_general(left, right, (((1,), (1,)), ((), ())), preferred_element_type=F32)


def tn(left, right):
    return lax.dot_general(left, right, (((0,), (0,)), ((), ())), preferred_element_type=F32)


def iota(shape, axis):
    return lax.broadcasted_iota(jnp.int32, shape, axis)


def full(shape):
    return pl.BlockSpec(shape, lambda *ids: (0,) * len(shape))


def rows_of(shape):
    return pl.BlockSpec(shape, lambda g, *ids: (g,) + (0,) * (len(shape) - 1))


def call(kernel, grid, in_specs, out_specs, out_shape, scratch=(), vmem=60, prefetch=1, name=None, cost=None, aliases=None):
    return pl.pallas_call(
        kernel,
        grid_spec=pltpu.PrefetchScalarGridSpec(
            num_scalar_prefetch=prefetch,
            grid=grid,
            in_specs=in_specs,
            out_specs=out_specs,
            scratch_shapes=list(scratch),
        ),
        out_shape=out_shape,
        input_output_aliases=aliases or {},
        compiler_params=pltpu.CompilerParams(
            dimension_semantics=("arbitrary",) * len(grid), vmem_limit_bytes=vmem * MIB
        ),
        name=name,
        cost_estimate=cost and pl.CostEstimate(flops=int(cost[0]), bytes_accessed=int(cost[1]), transcendentals=0),
    )


def shape_of(shape, dtype):
    return jax.ShapeDtypeStruct(shape, dtype)


def normalize(x):
    mean = jnp.mean(x, -1, keepdims=True)
    centered = x - mean
    scale = lax.rsqrt(jnp.mean(centered * centered, -1, keepdims=True) + EPSILON)
    return centered * scale, scale


def swap_halves(t):
    low = (iota(t.shape, 1) % HEAD_DIM) < HEAD_DIM // 2
    return jnp.where(
        low, pltpu.roll(t, LANES - HEAD_DIM // 2, 1), pltpu.roll(t, HEAD_DIM // 2, 1)
    )


def head_masks(rows):
    lane = iota((rows, LANES), 1)
    return [(lane < HEAD_DIM), (lane >= HEAD_DIM)]


def both(masks, value):
    return jnp.concatenate([keep(mask, value) for mask in masks], 0)


def beside(value):
    return jnp.concatenate([value[0], value[1]], 1)


def allowed_pairs(plan, gene, span):
    length = plan[gene]
    i, j = iota((span, span), 0), iota((span, span), 1)
    return ((i < length) & (j < length)) | (i == j)


def keep(mask, value):
    return jnp.where(mask, value, jnp.zeros_like(value))


Z_SIZE = 4
COLUMNS = 384
AXES = ("fsdp", "replica")
ANY = pl.BlockSpec(memory_space=pl.ANY)
PIECES = 32
EVERY = [(dx, dy, dc) for dx in range(2) for dy in range(2) for dc in range(2)]
SLOTS = (0, 128, 256, 640, 768, 896, 1024, 1408)
PACKED = 1536


def tuned_mesh(mesh):
    return mesh.shape["fsdp"] == 2 * Z_SIZE and mesh.shape["replica"] == 4


def pairs(step):
    out = []
    for z in range(Z_SIZE):
        for x in range(2):
            for y in range(2):
                for c in range(2):
                    tz, tx, ty, tc = step(z, x, y, c)
                    out.append((((z * 2 + x) * 2 + y) * 2 + c, (((tz % Z_SIZE) * 2 + tx) * 2 + ty) * 2 + tc))
    return out


ACROSS_X = pairs(lambda z, x, y, c: (z, 1 - x, y, c))
ACROSS_Y = pairs(lambda z, x, y, c: (z, x, 1 - y, c))
ACROSS_CORE = pairs(lambda z, x, y, c: (z, x, y, 1 - c))
ALONG_Z = [pairs(functools.partial(lambda d, z, x, y, c: (z + d, x, y, c), d)) for d in range(Z_SIZE)]
tie = lax.optimization_barrier


def move(array, table):
    return lax.ppermute(array, AXES, table)


def place():
    f, r = lax.axis_index("fsdp"), lax.axis_index("replica")
    return jnp.stack([f // 2, f % 2, r // 2, r % 2]).astype(jnp.int32)


def spot(at, dz, dx, dy, dc):
    z = lax.rem(at[0] + (Z_SIZE - dz), Z_SIZE)
    return z * 2 + lax.bitwise_xor(at[1], dx), lax.bitwise_xor(at[2], dy), lax.bitwise_xor(at[3], dc)


def piece_index(half, dz, dx, dy):
    return (16 + dy * 8 + dx * 4 if half else dx * 8 + dy * 4) + dz


def at_rows(start, size):
    return pl.ds(pl.multiple_of(start, 16), size)


def at_columns(start, size):
    return pl.ds(pl.multiple_of(start, LANES), size)


def quarters_kernel(at, *refs):
    wqkv, wout, wup, wdown = refs[:4]
    vectors, (near1, near2, near, side, packed) = refs[4:12], refs[12:]
    width = wout.shape[1]
    rows = wout.shape[0] // 2
    packed[...] = jnp.zeros_like(packed)
    for ref, start in zip(vectors, SLOTS):
        packed[:, start : start + ref.shape[0]] = ref[...].reshape(1, -1)
    tail = jnp.zeros((8, COLUMNS), BF16)
    for i in range(4):
        part = jnp.broadcast_to(packed[:, i * COLUMNS : (i + 1) * COLUMNS], (8, COLUMNS))
        tail = jnp.where(iota((8, COLUMNS), 0) == i, part, tail)
    mine = at_rows(at[3] * rows, rows)
    for y in range(2):
        for b in range(4):
            ref, base = (wqkv, b * width) if b < 3 else (wout, 0)
            start = base + y * COLUMNS
            side[y, b // 2, (b % 2) * rows : (b % 2 + 1) * rows, :] = ref[mine, start : start + COLUMNS]
            start = b * width + y * COLUMNS
            side[y, 0, (2 + b) * rows : (3 + b) * rows, :] = wup[mine, start : start + COLUMNS]
        here = slice(y * COLUMNS, (y + 1) * COLUMNS)
        side[y, 1, 2 * rows : 6 * rows, :] = wdown[at_rows(at[3] * 4 * rows, 4 * rows), here]
        for h in range(2):
            side[y, h, 6 * rows : 6 * rows + 8, :] = tail
    near1[:, 0 : 2 * rows, :] = side[at[2], :, 0 : 2 * rows, :]
    near2[...] = side[at[2], :, 2 * rows : 6 * rows, :]
    for h in range(2):
        near1[h, 2 * rows : 2 * rows + 8, :] = tail
    near[:, 0 : 2 * rows + 8, :] = near1[...]
    near[:, 2 * rows + 8 : 6 * rows + 8, :] = near2[...]


def quarters(at, wqkv, wout, wup, wdown, vectors):
    rows = wqkv.shape[0] // 2
    shapes = [
        (2, 2 * rows + 8, COLUMNS),
        (2, 4 * rows, COLUMNS),
        (2, 6 * rows + 8, COLUMNS),
        (2, 2, 6 * rows + 8, COLUMNS),
    ]
    matrices = (wqkv, wout, wup, wdown)
    return call(
        quarters_kernel,
        (1,),
        [full(v.shape) for v in matrices + tuple(vectors)],
        [full(s) for s in shapes],
        [shape_of(s, BF16) for s in shapes],
        [pltpu.VMEM((1, PACKED), BF16)],
        name="quarters",
        cost=(0, 6e6),
    )(at, *matrices, *vectors)


def rel_mask(at, columns, size):
    row = iota((2 * Z_SIZE, columns), 0)
    z = (at[0] + Z_SIZE - row % Z_SIZE) % Z_SIZE
    shard = z * 2 + jnp.where(row < Z_SIZE, at[1], 1 - at[1])
    return iota((2 * Z_SIZE, columns), 1) // size == shard


def spread(size, columns):
    lanes = -(-size // LANES) * LANES
    lane, column = iota((lanes, columns), 0), iota((lanes, columns), 1)
    return jnp.where(column % size == lane, 1.0, 0.0).astype(BF16)


def unpack_kernel(at, near_ref, far_ref, *refs):
    out, row_ref = refs[:8], refs[8]
    for x_bit, rows in enumerate((near_ref, far_ref)):
        for d in range(Z_SIZE):
            here = x_bit * Z_SIZE + d
            for i in range(4):
                row_ref[here : here + 1, i * COLUMNS : (i + 1) * COLUMNS] = rows[d, i : i + 1, :].astype(F32)
    for ref, start in zip(out, SLOTS):
        columns = ref.shape[1]
        size = columns // (2 * Z_SIZE)
        table = spread(size, columns)
        got = nn(row_ref[:, start : start + table.shape[0]].astype(BF16), table)
        ref[...] = jnp.sum(jnp.where(rel_mask(at, columns, size), got, 0.0), 0, keepdims=True)


def unpack(at, near, far, sizes):
    shapes = [(1, n * 2 * Z_SIZE) for n in sizes]
    return call(
        unpack_kernel,
        (1,),
        [full(near.shape)] * 2,
        [full(s) for s in shapes],
        [shape_of(s, F32) for s in shapes],
        [pltpu.VMEM((2 * Z_SIZE, PACKED), F32)],
        name="unpack",
        cost=(1e8, 1e5),
    )(at, near, far)


def plan_of(segments):
    lengths = [jnp.sum(jnp.where(segments == g, 1.0, 0.0)).astype(jnp.int32) for g in range(GENES)]
    span = segments.size // GENES
    starts, before, start, free = [], [], 0, 0
    for g in range(GENES):
        starts.append(start)
        before.append(free)
        start = start + lengths[g]
        free = free + span - lengths[g]
    return [jnp.asarray(v, jnp.int32) for v in lengths + starts + before + [start]]


def source_of_slots(plan, gene, slots):
    length = plan[gene]
    return jnp.where(
        slots < length,
        plan[GENES + gene] + slots,
        plan[3 * GENES] + plan[2 * GENES + gene] + slots - length,
    )


def prepare_kernel(seg_ref, x_ref, c_ref, freq_ref, plan_ref, xp_ref, cp_ref, cos_ref, sin_ref):
    gene = pl.program_id(0)
    span = xp_ref.shape[0]
    length = x_ref.shape[0]

    @pl.when(gene == 0)
    def _():
        for i, v in enumerate(plan_of(seg_ref[...])):
            plan_ref[i] = v

    slots = iota((span, 1), 0)
    source = source_of_slots(plan_ref, gene, slots)
    pick = jnp.where(iota((span, length), 1) == source, 1.0, 0.0).astype(BF16)
    xp_ref[...] = nn(pick, x_ref[...]).astype(BF16)
    cp_ref[...] = nn(pick, c_ref[...]).astype(BF16)
    start = jnp.where(slots < plan_ref[gene], plan_ref[GENES + gene], plan_ref[3 * GENES])
    angle = (source - start).astype(F32) * freq_ref[...]
    low = iota((span, LANES), 1) % HEAD_DIM < HEAD_DIM // 2
    cos_ref[...] = jnp.cos(angle)
    sine = jnp.sin(angle)
    sin_ref[...] = jnp.where(low, -sine, sine)


def prepare(segments, x, c):
    length, width = x.shape
    span = length // GENES
    frequency = np.power(10000.0, np.arange(HEAD_DIM // 2) * (-2.0 / HEAD_DIM))
    frequency = jnp.asarray(np.tile(frequency, LANES // (HEAD_DIM // 2))[None], F32)
    return call(
        prepare_kernel,
        (GENES,),
        [full((1, length)), full((length, width)), full((length, width)), full((1, LANES))],
        [
            pl.BlockSpec(memory_space=pltpu.SMEM),
            rows_of((span, width)),
            rows_of((span, width)),
            rows_of((span, LANES)),
            rows_of((span, LANES)),
        ],
        [
            shape_of((16,), jnp.int32),
            shape_of((length, width), BF16),
            shape_of((length, width), BF16),
            shape_of((length, LANES), F32),
            shape_of((length, LANES), F32),
        ],
        prefetch=0,
        name="prepare",
        cost=(3.3e9, 8e6),
    )(segments, x, c, frequency)


def far_piece(refs, half, dz, dx, dy, dc):
    refs = refs[4 * dc : 4 * dc + 4]
    ref, at = (refs[dx], (dy, dz - 1)) if half == 0 else (refs[2 + dy], (dx, dz - 1))
    return ref.at[(half,) + at] if len(ref.shape) == 5 else ref.at[at]


def load_matrices(at, source, wqkv_ref, wout_ref, sem):
    width = wout_ref.shape[0]
    rows = width // (4 * Z_SIZE)
    own = at_rows((at[0] * 2 + at[1]) * 2 * rows, 2 * rows)
    pltpu.make_async_copy(source[0], wqkv_ref.at[own], sem.at[0]).start()
    pltpu.make_async_copy(source[1], wout_ref.at[own], sem.at[1]).start()

    def put(piece, f, y, c):
        down = at_rows((f * 2 + c) * rows, rows)
        for b in range(4):
            src = piece(b // 2).at[pl.ds((b % 2) * rows, rows)]
            across = at_columns((b % 3) * width + y * COLUMNS, COLUMNS)
            dst = wqkv_ref if b < 3 else wout_ref
            pltpu.make_async_copy(src, dst.at[down, across], sem.at[b // 3]).start()

    for dc in range(2):
        f, _, c = spot(at, 0, 1, 0, dc)
        for y in range(2):
            put(lambda half: source[2 + dc].at[y, half, pl.ds(0, 2 * rows)], f, y, c)

    def one(dz, carry):
        for dx, dy, dc in EVERY:
            put(lambda half: far_piece(source[4:], half, dz, dx, dy, dc), *spot(at, dz, dx, dy, dc))
        return carry

    lax.fori_loop(1, Z_SIZE, one, 0)


def attend_kernel(plan, at, *refs, pieces):
    (xp_ref, cos_ref, sin_ref, g1_ref, b1_ref, bqkv_ref, bout_ref), refs = refs[:7], refs[7:]
    source, refs = (refs[:12], refs[12:]) if pieces else (refs[:2], refs[2:])
    (qkv_ref, o_ref, lse_ref, x1_ref), refs = refs[:4], refs[4:]
    if pieces:
        whole, refs = refs[:2], refs[2:]
    wqkv_ref, wout_ref, mask_ref, a1_ref, sem = refs
    step = pl.program_id(0)
    gene = jnp.maximum(step - 1, 0)
    span = cos_ref.shape[0]
    width = xp_ref.shape[1]

    def wait_both():
        pltpu.make_async_copy(wqkv_ref, wqkv_ref, sem.at[0]).wait()
        pltpu.make_async_copy(wout_ref, wout_ref, sem.at[1]).wait()

    @pl.when(step == 0)
    def _():
        if pieces:
            load_matrices(at, source, wqkv_ref, wout_ref, sem)
        else:
            pltpu.make_async_copy(source[0], wqkv_ref, sem.at[0]).start()
            pltpu.make_async_copy(source[1], wout_ref, sem.at[1]).start()

        def norm(i, carry):
            here = pl.ds(i * span, span)
            xhat, _ = normalize(xp_ref[here, :].astype(F32))
            a1_ref[here, :] = (xhat * g1_ref[...] + b1_ref[...]).astype(BF16)
            return carry

        lax.fori_loop(0, GENES, norm, 0)
        wait_both()
        if pieces:
            pltpu.make_async_copy(wqkv_ref, whole[0], sem.at[0]).start()
            pltpu.make_async_copy(wout_ref, whole[1], sem.at[1]).start()

    @pl.when(step > 0)
    def _():
        attend_gene(
            plan, gene, xp_ref, a1_ref, cos_ref, sin_ref, bqkv_ref, bout_ref, wqkv_ref, wout_ref, mask_ref,
            qkv_ref, o_ref, lse_ref, x1_ref,
        )

    if pieces:

        @pl.when(step == pl.num_programs(0) - 1)
        def _():
            wait_both()


def attend_gene(
    plan, gene, xp_ref, a1_ref, cos_ref, sin_ref, bqkv_ref, bout_ref, wqkv_ref, wout_ref, mask_ref,
    qkv_ref, o_ref, lse_ref, x1_ref,
):
    span, width = o_ref.shape
    here = pl.ds(gene * span, span)
    x = xp_ref[here, :].astype(F32)
    a1 = a1_ref[here, :]
    cos, sin = cos_ref[...], sin_ref[...]
    for part in range(3):
        base = part * width
        t = nn(a1, wqkv_ref[:, base : base + width]) + bqkv_ref[:, base : base + width]
        for p in range(width // LANES):
            piece = t[:, p * LANES : (p + 1) * LANES]
            if part < 2:
                piece = piece * cos + swap_halves(piece) * sin
            qkv_ref[:, base + p * LANES : base + (p + 1) * LANES] = piece.astype(BF16)
    mask_ref[...] = jnp.where(allowed_pairs(plan, gene, span), 1.0, 0.0)
    masks = head_masks(span)
    def pair(p, carry):
        part = lambda i: at_columns(i * width + p * LANES, LANES)
        q = qkv_ref[:, part(0)]
        k = qkv_ref[:, part(1)] * BF16(1.0 / math.sqrt(HEAD_DIM))
        v = qkv_ref[:, part(2)]
        s = nt(both(masks, k), q).reshape(2, span, span)
        s = jnp.where((mask_ref[...] > 0.5)[None], s, NEG_FILL)
        peak = jnp.max(s, 1, keepdims=True)
        e = jnp.exp(s - peak)
        total = jnp.sum(e, 1, keepdims=True)
        weights = (e * (1.0 / total)).astype(BF16).reshape(2 * span, span)
        lse = peak + jnp.log(total)
        for h in range(2):
            lse_ref[pl.ds(2 * p + h, 1), :] = lse[h]
        o_ref[:, part(0)] = tn(weights, both(masks, v)).astype(BF16)
        return carry

    lax.fori_loop(0, width // LANES, pair, 0, unroll=True)
    x1_ref[...] = x + nn(o_ref[...], wout_ref[...]) + bout_ref[...]


def attend(plan, at, xp, cos, sin, g1, b1, bqkv, bout, source):
    length, width = xp.shape
    span = length // GENES
    pieces = len(source) == 12
    behind = lambda shape: pl.BlockSpec(shape, lambda g, *ids: (jnp.maximum(g - 1, 0), 0))
    weights = [shape_of((width, 3 * width), BF16), shape_of((width, width), BF16)]
    got = call(
        functools.partial(attend_kernel, pieces=pieces),
        (GENES + 1,),
        [
            full((length, width)),
            behind((span, LANES)),
            behind((span, LANES)),
            full((1, width)),
            full((1, width)),
            full((1, 3 * width)),
            full((1, width)),
        ]
        + [ANY] * len(source),
        [
            behind((span, 3 * width)),
            behind((span, width)),
            pl.BlockSpec((16, span), lambda g, *ids: (0, jnp.maximum(g - 1, 0))),
            behind((span, width)),
        ]
        + [ANY] * (2 if pieces else 0),
        [
            shape_of((length, 3 * width), BF16),
            shape_of((length, width), BF16),
            shape_of((16, length), F32),
            shape_of((length, width), F32),
        ]
        + (weights if pieces else []),
        [
            pltpu.VMEM((width, 3 * width), BF16),
            pltpu.VMEM((width, width), BF16),
            pltpu.VMEM((span, span), F32),
            pltpu.VMEM((length, width), BF16),
            pltpu.SemaphoreType.DMA((2,)),
        ],
        prefetch=2,
        name="attend",
        cost=(11e9, 20e6),
    )(plan, at, xp, cos, sin, g1, b1, bqkv, bout, *source)
    return got[:4], (got[4:] if pieces else source)


def feed_kernel(at, *refs, block, pieces, steps):
    (x1_hbm, c_hbm, g2_ref, b2_ref, bup_ref, bdown_ref), refs = refs[:6], refs[6:]
    source, refs = (refs[:12], refs[12:]) if pieces else (refs[:2], refs[2:])
    (out_hbm, dx1_hbm, da_hbm, gbup_ref, sums_ref, first_ref, second_ref), refs = refs[:7], refs[7:]
    x1_ref, c_ref, out_ref, da_ref, a2_ref, acc_ref, dh_ref, gr_ref, du_ref = refs[:9]
    wups, wdowns, gups, gdowns, load_sem, store_sem, in_sem, out_sem = refs[9:]
    step = pl.program_id(0)
    length, width = x1_ref.shape
    chunk = bup_ref.shape[1]
    blocks = length // block
    slot = lax.rem(step, 2)
    rows = width // (4 * Z_SIZE)

    def load(j, to):
        if pieces:
            own = at_rows((at[0] * 2 + at[1]) * 2 * rows, 2 * rows)
            src = source[0].at[:, at_columns(j * chunk, chunk)]
            pltpu.make_async_copy(src, wups.at[to, own], load_sem.at[0, to]).start()

            def put_up(piece, f, y, c):
                dst = wups.at[to, at_rows((f * 2 + c) * rows, rows), at_columns(y * COLUMNS, COLUMNS)]
                pltpu.make_async_copy(piece.at[at_rows(j * rows, rows)], dst, load_sem.at[0, to]).start()

            def put_down(piece, x, y, c):
                dst = wdowns.at[to, at_rows((x * 2 + c) * 4 * rows, 4 * rows), at_columns(y * COLUMNS, COLUMNS)]
                pltpu.make_async_copy(piece, dst, load_sem.at[1, to]).start()

            for dc in range(2):
                f, _, c = spot(at, 0, 1, 0, dc)
                for y in range(2):
                    put_up(source[2 + dc].at[y, 0, pl.ds(2 * rows, 4 * rows)], f, y, c)

            def one(dz, carry):
                for dx, dy, dc in EVERY:
                    put_up(far_piece(source[4:], 0, dz, dx, dy, dc), *spot(at, dz, dx, dy, dc))
                return carry

            lax.fori_loop(1, Z_SIZE, one, 0)

            @pl.when(j == at[0])
            def _():
                here = at_rows(at[1] * 8 * rows, 8 * rows)
                pltpu.make_async_copy(source[1], wdowns.at[to, here], load_sem.at[1, to]).start()
                for dc in range(2):
                    _, _, c = spot(at, 0, 1, 0, dc)
                    for y in range(2):
                        put_down(source[2 + dc].at[y, 1, pl.ds(2 * rows, 4 * rows)], 1 - at[1], y, c)

            @pl.when(j != at[0])
            def _():
                back = lax.rem(at[0] + (Z_SIZE - j), Z_SIZE)
                for dx, dy, dc in EVERY:
                    _, y, c = spot(at, back, dx, dy, dc)
                    put_down(far_piece(source[4:], 1, back, dx, dy, dc), lax.bitwise_xor(at[1], dx), y, c)

        else:
            part = source[0].at[:, at_columns(j * chunk, chunk)]
            pltpu.make_async_copy(part, wups.at[to], load_sem.at[0, to]).start()
            part = source[1].at[at_rows(j * chunk, chunk), :]
            pltpu.make_async_copy(part, wdowns.at[to], load_sem.at[1, to]).start()

    def store(j, to):
        if pieces:

            def one(dz, carry):
                for dx, dy, dc in EVERY:
                    f, y, c = spot(at, Z_SIZE - dz, dx, dy, dc)
                    src = gups.at[to, at_rows(f * 2 * rows + c * rows, rows), at_columns(y * COLUMNS, COLUMNS)]
                    dst = (first_ref, second_ref)[dc].at[piece_index(0, dz, dx, dy), at_rows(j * rows, rows)]
                    pltpu.make_async_copy(src, dst, store_sem.at[0, to]).start()
                return carry

            lax.fori_loop(0, Z_SIZE, one, 0)
            ahead = lax.rem(j + Z_SIZE - at[0], Z_SIZE)
            for dx, dy, dc in EVERY:
                f, y, c = spot(at, 0, dx, dy, dc)
                x = lax.bitwise_xor(at[1], dx)
                src = gdowns.at[to, at_rows((x * 2 + c) * 4 * rows, 4 * rows), at_columns(y * COLUMNS, COLUMNS)]
                dst = (first_ref, second_ref)[dc].at[piece_index(1, ahead, dx, dy)]
                pltpu.make_async_copy(src, dst, store_sem.at[1, to]).start()
        else:
            part = first_ref.at[:, at_columns(j * chunk, chunk)]
            pltpu.make_async_copy(gups.at[to], part, store_sem.at[0, to]).start()
            part = second_ref.at[at_rows(j * chunk, chunk), :]
            pltpu.make_async_copy(gdowns.at[to], part, store_sem.at[1, to]).start()

    def wait_load(to):
        pltpu.make_async_copy(wups.at[to], wups.at[to], load_sem.at[0, to]).wait()
        pltpu.make_async_copy(wdowns.at[to], wdowns.at[to], load_sem.at[1, to]).wait()

    def wait_store(to):
        pltpu.make_async_copy(gups.at[to], gups.at[to], store_sem.at[0, to]).wait()
        pltpu.make_async_copy(gdowns.at[to], gdowns.at[to], store_sem.at[1, to]).wait()

    def bring(i):
        here = at_rows(i * block, block)
        return [
            pltpu.make_async_copy(x1_hbm.at[here, :], x1_ref.at[here, :], in_sem.at[0, i]),
            pltpu.make_async_copy(c_hbm.at[here, :], c_ref.at[here, :], in_sem.at[1, i]),
        ]

    def give(i):
        here = at_rows(i * block, block)
        return [
            pltpu.make_async_copy(out_ref.at[here, :], out_hbm.at[here, :], out_sem.at[0, i]),
            pltpu.make_async_copy(x1_ref.at[here, :], dx1_hbm.at[here, :], out_sem.at[1, i]),
            pltpu.make_async_copy(da_ref.at[here, :], da_hbm.at[here, :], out_sem.at[2, i]),
        ]

    @pl.when(step == 0)
    def _():
        for i in range(blocks):
            bring(i)[0].start()
        load(0, 0)
        for i in range(blocks):
            bring(i)[1].start()

        def one(i, carry):
            here = pl.ds(i * block, block)
            bring(i)[0].wait()
            xhat, _ = normalize(x1_ref[here, :])
            a2_ref[here, :] = (xhat * g2_ref[...] + b2_ref[...]).astype(BF16)
            acc_ref[here, :] = jnp.zeros((block, width), F32)
            dh_ref[here, :] = jnp.zeros((block, width), F32)
            return carry

        lax.fori_loop(0, blocks, one, 0)
        for i in range(blocks):
            bring(i)[1].wait()

    wait_load(slot)

    @pl.when(step < steps - 1)
    def _():
        load(step + 1, 1 - slot)

    wup_ref, wdown_ref = wups.at[slot], wdowns.at[slot]

    def one(i, bias_sum):
        here = pl.ds(i * block, block)
        u = nn(a2_ref[here, :], wup_ref[...]) + bup_ref[...]
        phi = 0.5 + 0.5 * lax.erf(u * math.sqrt(0.5))
        slope = phi + u * (jnp.exp(-0.5 * u * u) * (1.0 / math.sqrt(2.0 * math.pi)))
        gr = (u * phi).astype(BF16)
        gr_ref[here, :] = gr
        du = (nt(c_ref[here, :], wdown_ref[...]) * slope).astype(BF16)
        du_ref[here, :] = du
        out = nn(gr, wdown_ref[...])
        dh = nt(du, wup_ref[...])

        acc_ref[here, :] += out
        dh_ref[here, :] += dh
        return bias_sum + jnp.sum(du.astype(F32), 0, keepdims=True)

    gbup_ref[...] = lax.fori_loop(0, blocks, one, jnp.zeros((1, chunk), F32))

    @pl.when(step >= 2)
    def _():
        wait_store(slot)

    gdowns[slot] = tn(gr_ref[...], c_ref[...]).astype(BF16)
    gups[slot] = tn(a2_ref[...], du_ref[...]).astype(BF16)
    store(step, slot)

    @pl.when(step == steps - 1)
    def _():
        def one(i, sums):
            here = pl.ds(i * block, block)
            x1 = x1_ref[here, :]
            xhat, scale = normalize(x1)
            out_ref[here, :] = (x1 + acc_ref[here, :] + bdown_ref[...]).astype(BF16)
            dh = dh_ref[here, :]
            c = c_ref[here, :].astype(F32)
            e = dh * g2_ref[...]
            dx1 = c + scale * (
                e - jnp.mean(e, -1, keepdims=True) - xhat * jnp.mean(e * xhat, -1, keepdims=True)
            )
            x1_ref[here, :] = dx1
            da = dx1.astype(BF16)
            da_ref[here, :] = da
            for copy in give(i):
                copy.start()
            new = (
                jnp.sum(dh * xhat, 0, keepdims=True),
                jnp.sum(dh, 0, keepdims=True),
                jnp.sum(c, 0, keepdims=True),
                jnp.sum(da.astype(F32), 0, keepdims=True),
            )
            return tuple(a + b for a, b in zip(sums, new))

        sums = lax.fori_loop(0, blocks, one, (jnp.zeros((1, width), F32),) * 4)
        for i in range(4):
            sums_ref[i : i + 1, :] = sums[i]
        for i in range(blocks):
            for copy in give(i):
                copy.wait()
        wait_store(1 - slot)
        wait_store(slot)


def feed(at, x1, c, g2, b2, bup, bdown, source):
    length, width = x1.shape
    hidden = bup.shape[1]
    steps = 4
    chunk = hidden // steps
    pieces = len(source) == 12
    if pieces:
        rows = width // Z_SIZE
        stored = [shape_of((PIECES, rows, COLUMNS), BF16)] * 2
    else:
        stored = [shape_of((width, hidden), BF16), shape_of((hidden, width), BF16)]
    return call(
        functools.partial(feed_kernel, block=length // 2, pieces=pieces, steps=steps),
        (steps,),
        [
            ANY,
            ANY,
            full((1, width)),
            full((1, width)),
            pl.BlockSpec((1, chunk), lambda j, *ids: (0, j)),
            full((1, width)),
        ]
        + [ANY] * len(source),
        [
            ANY,
            ANY,
            ANY,
            pl.BlockSpec((1, chunk), lambda j, *ids: (0, j)),
            full((8, width)),
            ANY,
            ANY,
        ],
        [
            shape_of((length, width), BF16),
            shape_of((length, width), F32),
            shape_of((length, width), BF16),
            shape_of((1, hidden), F32),
            shape_of((8, width), F32),
        ]
        + stored,
        [
            pltpu.VMEM((length, width), F32),
            pltpu.VMEM((length, width), BF16),
            pltpu.VMEM((length, width), BF16),
            pltpu.VMEM((length, width), BF16),
            pltpu.VMEM((length, width), BF16),
            pltpu.VMEM((length, width), F32),
            pltpu.VMEM((length, width), F32),
            pltpu.VMEM((length, chunk), BF16),
            pltpu.VMEM((length, chunk), BF16),
            pltpu.VMEM((2, width, chunk), BF16),
            pltpu.VMEM((2, chunk, width), BF16),
            pltpu.VMEM((2, width, chunk), BF16),
            pltpu.VMEM((2, chunk, width), BF16),
            pltpu.SemaphoreType.DMA((2, 2)),
            pltpu.SemaphoreType.DMA((2, 2)),
            pltpu.SemaphoreType.DMA((2, 4)),
            pltpu.SemaphoreType.DMA((3, 4)),
        ],
        name="feed",
        cost=(29e9, 40e6),
    )(at, x1, c, g2, b2, bup, bdown, *source)


def attend_back_kernel(
    plan, qkv_ref, da_ref, lse_ref, cos_ref, sin_ref, wout_ref, *refs, base, count,
):
    dqkv_ref, bias_ref, dout_ref, mask_ref = refs[-4:]
    gene = pl.program_id(0) + base
    span, width = da_ref.shape
    score_scale = 1.0 / math.sqrt(HEAD_DIM)
    dout_ref[...] = nt(da_ref[...], wout_ref[...]).astype(BF16)
    mask_ref[...] = jnp.where(allowed_pairs(plan, gene, span), 1.0, 0.0)
    cos, sin = cos_ref[...], sin_ref[...]
    masks = head_masks(span)

    def back(t):
        return (t * cos - swap_halves(t) * sin).astype(BF16)

    def pair(p, carry):
        part = lambda i: at_columns(i * width + p * LANES, LANES)
        q = qkv_ref[:, part(0)]
        k = qkv_ref[:, part(1)] * BF16(score_scale)
        v = qkv_ref[:, part(2)]
        dout = dout_ref[:, part(0)]
        kh = both(masks, k)
        s = nt(kh, q).reshape(2, span, span)
        s = jnp.where((mask_ref[...] > 0.5)[None], s, NEG_FILL)
        weights = jnp.exp(s - stack(lse_ref[pl.ds(2 * p + h, 1), :] for h in range(2)))
        dw = nt(both(masks, v), dout).reshape(2, span, span)
        dot = jnp.sum(weights * dw, 1, keepdims=True)
        ds = (weights * (dw - dot)).astype(BF16)
        weights = weights.astype(BF16)
        dv = nn(beside(weights), both(masks, dout))
        dk = nn(beside(ds), both(masks, q))
        dq = tn(ds.reshape(2 * span, span), kh)
        dqkv_ref[:, part(0)] = back(dq)
        dqkv_ref[:, part(1)] = back(dk * score_scale)
        dqkv_ref[:, part(2)] = dv.astype(BF16)
        return carry

    lax.fori_loop(0, width // LANES, pair, 0, unroll=2 if count == 1 else True)

    bqkv = jnp.sum(dqkv_ref[...].astype(F32), 0, keepdims=True)

    @pl.when(gene == base)
    def _():
        bias_ref[0:1, :] = bqkv

    @pl.when(gene > base)
    def _():
        bias_ref[0:1, :] += bqkv


def attend_back(plan, qkv, da, lse, cos, sin, wout, base, count, before=()):
    length, width = da.shape
    span = length // GENES
    rows = lambda shape: pl.BlockSpec(shape, lambda g, *ids: (g + base, 0))
    return call(
        functools.partial(attend_back_kernel, base=base, count=count),
        (count,),
        [
            rows((span, 3 * width)),
            rows((span, width)),
            pl.BlockSpec((16, span), lambda g, *ids: (0, g + base)),
            rows((span, LANES)),
            rows((span, LANES)),
            full((width, width)),
        ]
        + [ANY] * len(before),
        [rows((span, 3 * width)), full((8, 3 * width))],
        [shape_of((length, 3 * width), BF16), shape_of((8, 3 * width), F32)],
        [pltpu.VMEM((span, width), BF16), pltpu.VMEM((span, span), F32)],
        name="attend_back",
        cost=(4e9 * count, 6e6 * count),
        aliases={7 + i: i for i in range(len(before))},
    )(plan, qkv, da, lse, cos, sin, wout, *before)


def project_back_kernel(xp_ref, g1_ref, dx1_ref, dqkv_ref, wqkv_ref, dxp_ref, sums_ref):
    step = pl.program_id(0)
    dh = nt(dqkv_ref[...], wqkv_ref[...])
    xhat, scale = normalize(xp_ref[...].astype(F32))
    e = dh * g1_ref[...]
    dx = dx1_ref[...] + scale * (
        e - jnp.mean(e, -1, keepdims=True) - xhat * jnp.mean(e * xhat, -1, keepdims=True)
    )
    dxp_ref[...] = dx.astype(BF16)

    @pl.when(step == 0)
    def _():
        sums_ref[...] = jnp.zeros_like(sums_ref)

    sums_ref[0:1, :] += jnp.sum(dh * xhat, 0, keepdims=True)
    sums_ref[1:2, :] += jnp.sum(dh, 0, keepdims=True)


def project_back(xp, g1, dx1, dqkv, wqkv):
    length, width = xp.shape
    span = length // GENES
    return call(
        project_back_kernel,
        (GENES,),
        [
            rows_of((span, width)),
            full((1, width)),
            rows_of((span, width)),
            rows_of((span, 3 * width)),
            full((width, 3 * width)),
        ],
        [rows_of((span, width)), full((8, width))],
        [shape_of((length, width), BF16), shape_of((8, width), F32)],
        prefetch=0,
        name="project_back",
        cost=(0, 0),
    )(xp, g1, dx1, dqkv, wqkv)


def grads_kernel(at, *refs, pieces):
    (xp_hbm, o_hbm, da_hbm, dqkv_hbm, g1_ref, b1_ref), refs = refs[:6], refs[6:]
    sums, refs = (refs[:5], refs[5:]) if pieces else ((), refs)
    first_ref, second_ref, xp_ref, o_ref, da_ref, dqkv_ref, a1_ref, grad_ref, in_sem, sem, *rest = refs
    small_ref, small_sem = rest if pieces else (None, None)
    step = pl.program_id(0)
    width = xp_ref.shape[1]
    rows = width // (4 * Z_SIZE)
    slot = lax.rem(step, 2)

    def bring(j):
        part = dqkv_hbm.at[:, at_columns(j * width, width)]
        return pltpu.make_async_copy(part, dqkv_ref.at[lax.rem(j, 2)], in_sem.at[3 + lax.rem(j, 2)])

    whole = [
        pltpu.make_async_copy(src, dst, in_sem.at[i])
        for i, (src, dst) in enumerate(((o_hbm, o_ref), (da_hbm, da_ref), (xp_hbm, xp_ref)))
    ]

    def wait(to):
        pltpu.make_async_copy(grad_ref.at[to], grad_ref.at[to], sem.at[to]).wait()

    def store(half, base, to):
        def one(dz, carry):
            for dx, dy, dc in EVERY:
                f, y, c = spot(at, Z_SIZE - dz, dx, dy, dc)
                src = grad_ref.at[to, at_rows(f * 2 * rows + c * rows, rows), at_columns(y * COLUMNS, COLUMNS)]
                dst = (first_ref, second_ref)[dc].at[
                    jnp.where(half == 0, piece_index(0, dz, dx, dy), piece_index(1, dz, dx, dy)),
                    at_rows(base * rows, rows),
                ]
                pltpu.make_async_copy(src, dst, sem.at[to]).start()
            return carry

        lax.fori_loop(0, Z_SIZE, one, 0)

    def pack():
        sums1, low_ref, high_ref, sums2, gbup = sums
        line = lambda ref, i: ref[i : i + 1, :]
        vectors = [
            line(sums1, 0), line(sums1, 1), line(low_ref, 0) + line(high_ref, 0), line(sums2, 3),
            line(sums2, 0), line(sums2, 1), gbup[...], line(sums2, 2),
        ]
        shards = 2 * Z_SIZE
        columns = []
        for value in vectors:
            size = value.shape[1] // shards
            spread_out = jnp.broadcast_to(value, (shards, value.shape[1]))
            mask = iota(spread_out.shape, 1) // size == iota(spread_out.shape, 0)
            own = jnp.where(mask, spread_out, 0.0).astype(BF16)
            columns.append(nt(own, spread(size, value.shape[1])).astype(BF16))
        packed = jnp.concatenate(columns, 1).astype(F32)
        for f in range(shards):
            for i in range(4):
                part = packed[f : f + 1, i * COLUMNS : (i + 1) * COLUMNS]
                small_ref[f, i // 2, i % 2] = jnp.broadcast_to(part, (8, COLUMNS)).astype(BF16)

    def smalls(act):
        def one(dz, carry):
            for dx, dy, dc in EVERY:
                f, y, c = spot(at, Z_SIZE - dz, dx, dy, dc)
                for half in range(2):
                    src = small_ref.at[f, y, c]
                    dst = (first_ref, second_ref)[dc].at[piece_index(half, dz, dx, dy), pl.ds(2 * rows, 8)]
                    act(pltpu.make_async_copy(src, dst, small_sem))
            return carry

        lax.fori_loop(0, Z_SIZE, one, 0)

    @pl.when(step == 0)
    def _():
        for copy in whole:
            copy.start()
        bring(step).start()
        if pieces:
            pack()
            smalls(lambda copy: copy.start())
        whole[0].wait()
        whole[1].wait()
        grad_ref[0] = tn(o_ref[...], da_ref[...]).astype(BF16)
        if pieces:
            store(1, 1, 0)
        else:
            pltpu.make_async_copy(grad_ref.at[0], second_ref, sem.at[0]).start()
        whole[2].wait()
        xhat, _ = normalize(xp_ref[...].astype(F32))
        a1_ref[...] = (xhat * g1_ref[...] + b1_ref[...]).astype(BF16)

    @pl.when(step > 0)
    def _():
        bring(step - 1).wait()

        @pl.when(step < 3)
        def _():
            bring(step).start()

        @pl.when(step >= 2)
        def _():
            wait(slot)

        grad_ref[slot] = tn(a1_ref[...], dqkv_ref[lax.rem(step - 1, 2)]).astype(BF16)
        if pieces:
            store(lax.div(step - 1, 2), lax.rem(step - 1, 2), slot)
        else:
            dst = first_ref.at[:, at_columns((step - 1) * width, width)]
            pltpu.make_async_copy(grad_ref.at[slot], dst, sem.at[slot]).start()

    @pl.when(step == 3)
    def _():
        wait(0)
        wait(1)
        if pieces:
            smalls(lambda copy: copy.wait())


def grads(at, xp, g1, b1, o, da, dqkv, sums):
    pieces = bool(sums)
    length, width = xp.shape
    if pieces:
        rows = width // (2 * Z_SIZE) + 8
        stored = [shape_of((PIECES, rows, COLUMNS), BF16)] * 2
    else:
        stored = [shape_of((width, 3 * width), BF16), shape_of((width, width), BF16)]
    return call(
        functools.partial(grads_kernel, pieces=pieces),
        (4,),
        [ANY] * 4 + [full((1, width))] * 2 + [full(v.shape) for v in sums],
        [ANY, ANY],
        stored,
        [pltpu.VMEM((length, width), BF16)] * 3
        + [
            pltpu.VMEM((2, length, width), BF16),
            pltpu.VMEM((length, width), BF16),
            pltpu.VMEM((2, width, width), BF16),
            pltpu.SemaphoreType.DMA((5,)),
            pltpu.SemaphoreType.DMA((2,)),
        ]
        + ([pltpu.VMEM((2 * Z_SIZE, 2, 2, 8, COLUMNS), BF16), pltpu.SemaphoreType.DMA] if pieces else []),
        name="grads",
        cost=(5e9, 12e6),
    )(at, xp, o, da, dqkv, g1, b1, *sums)


def restore_kernel(plan, outp_ref, dxp_ref, out_ref, dx_ref):
    span, width = out_ref.shape
    slots = iota((1, span), 1)
    source = jnp.concatenate([source_of_slots(plan, g, slots) for g in range(GENES)], 1)
    codon = iota((span, outp_ref.shape[0]), 0) + pl.program_id(0) * span
    pick = jnp.where(codon == source, 1.0, 0.0).astype(BF16)
    out_ref[...] = nn(pick, outp_ref[...]).astype(BF16)
    dx_ref[...] = nn(pick, dxp_ref[...]).astype(BF16)


def restore(plan, outp, dxp):
    length, width = outp.shape
    span = length // GENES
    return call(
        restore_kernel,
        (GENES,),
        [full((length, width)), full((length, width))],
        [rows_of((span, width))] * 2,
        [shape_of((length, width), BF16)] * 2,
        name="restore",
        cost=(3.3e9, 8e6),
    )(plan, outp, dxp)


def deliver_first_kernel(at, mine, other, wqkv, wout, *rest):
    vectors, row_ref = rest[:8], rest[8]
    width = wout.shape[1]
    rows = wout.shape[0] // 2
    for dc, one in enumerate((mine, other)):
        c = lax.bitwise_xor(at[3], dc)
        here = pl.ds(pl.multiple_of(c * rows, 8), rows)
        for y in range(2):
            for b in range(4):
                ref, base = (wqkv, b * width) if b < 3 else (wout, 0)
                start = base + y * COLUMNS
                piece = one[y, b // 2, (b % 2) * rows : (b % 2 + 1) * rows, :]
                ref[here, start : start + COLUMNS] = piece.astype(F32)
            start = at_columns((y * 2 + c) * COLUMNS, COLUMNS)
            row_ref[:, start] = one[y, 0, 2 * rows : 2 * rows + 8, :].astype(F32)
    for ref, start in zip(vectors, SLOTS):
        ref[...] = row_ref[0:1, start : start + ref.shape[0]].reshape(ref.shape[0])


def deliver_first(at, mine, other, sizes):
    rows = (mine.shape[2] - 8) // 2
    width = 2 * COLUMNS
    shapes = [(2 * rows, 3 * width), (2 * rows, width)] + [(n,) for n in sizes]
    return call(
        deliver_first_kernel,
        (1,),
        [pl.BlockSpec(memory_space=pltpu.VMEM)] * 2,
        [full(s) for s in shapes],
        [shape_of(s, F32) for s in shapes],
        [pltpu.VMEM((8, PACKED), F32)],
        name="deliver_first",
        cost=(0, 2e6),
    )(at, mine, other)


def deliver_second_kernel(at, mine, other, wup, wdown):
    width = wdown.shape[1]
    rows = wup.shape[0] // 2
    for dc, two in enumerate((mine, other)):
        c = lax.bitwise_xor(at[3], dc)
        here = pl.ds(pl.multiple_of(c * rows, 8), rows)
        down = pl.ds(pl.multiple_of(c * 4 * rows, 8), 4 * rows)
        for y in range(2):
            for b in range(4):
                start = b * width + y * COLUMNS
                wup[here, start : start + COLUMNS] = two[y, 0, b * rows : (b + 1) * rows, :].astype(F32)
            wdown[down, y * COLUMNS : (y + 1) * COLUMNS] = two[y, 1].astype(F32)


def deliver_second(at, mine, other):
    rows = mine.shape[2] // 4
    width = 2 * COLUMNS
    shapes = [(2 * rows, 4 * width), (8 * rows, width)]
    return call(
        deliver_second_kernel,
        (1,),
        [pl.BlockSpec(memory_space=pltpu.VMEM)] * 2,
        [full(s) for s in shapes],
        [shape_of(s, F32) for s in shapes],
        name="deliver_second",
        cost=(0, 4e6),
    )(at, mine, other)


def gather(shard):
    return lax.all_gather(shard, "fsdp", axis=0, tiled=True)


def reduce_rows(grad):
    part = lax.psum_scatter(grad, "fsdp", scatter_dimension=0, tiled=True)
    return lax.psum(part.astype(BF16), "replica").astype(F32)


def low(value):
    return value.astype(BF16)


def add(*values):
    total = values[0].astype(F32)
    for v in values[1:]:
        total = total + v.astype(F32)
    return total


def to_z(arrays):
    arrays = arrays if isinstance(arrays, list) else [arrays] * 3
    return [move(v, ALONG_Z[d]) for d, v in zip((1, 2, 3), arrays)]


def over_x(array):
    return move(array, ACROSS_X)


def over_y(array):
    return move(array, ACROSS_Y)


def over_core(array):
    return move(array, ACROSS_CORE)


def stack(arrays):
    return jnp.stack(list(arrays))


class Sum:
    def __init__(self, kept, got):
        self.kept, self.got = kept, got

    def plane_one(self):
        return self.part(8, 16), self.part(24, 32)

    def part(self, start, stop, *more):
        return low(add(self.kept[start:stop], self.got[start:stop], *more))

    def plane_two(self, by_x, by_y):
        self.by_x, self.by_y = by_x, by_y
        return self.part(4, 8, by_x[Z_SIZE:]), self.part(20, 24, by_y[Z_SIZE:])

    def along_z(self, by_y, by_x):
        def at_z(d, rounded):
            first = add(self.kept[d], self.got[d], self.by_x[d], by_y[d])
            second = add(self.kept[16 + d], self.got[16 + d], self.by_y[d], by_x[d])
            return low(stack([first, second])) if rounded else stack([first, second])

        self.own = at_z(0, False)
        return [at_z(d, True) for d in range(1, Z_SIZE)]

    def total(self, by_z):
        return low(add(self.own, *by_z))


def settle(bit, mine, other):
    return jnp.where(bit == 0, stack([mine, other]), stack([other, mine]))


def body(
    layer_input, cotangent, segment_ids, pad_mask, ln1_gain, ln1_bias, w_qkv, b_qkv, w_out, b_out,
    ln2_gain, ln2_bias, w_up, b_up, w_down, b_down, *, tuned,
):
    vectors = (ln1_gain, ln1_bias, b_qkv, b_out, ln2_gain, ln2_bias, b_up, b_down)
    sizes = [v.shape[0] for v in vectors]
    x, c = layer_input[0], cotangent[0]
    if tuned:
        at = place()
        near1, near2, near, side = quarters(at, w_qkv, w_out, w_up, w_down, vectors)
        near1, near2, near, side, x = tie((near1, near2, near, side, x))
        z_one, z1_two, z1_three = move(near, ALONG_Z[1]), move(near1, ALONG_Z[2]), move(near1, ALONG_Z[3])
        far_side = over_x(side)
        prepared = prepare(segment_ids, x, c)
        z_one, z1_two, z1_three, prepared = tie((z_one, z1_two, z1_three, prepared))
        split = near1.shape[1]
        z1, z2_one = [z_one[:, :split], z1_two, z1_three], z_one[:, split:]
        plan, xp, cp, cos, sin = prepared

        count = near1.shape[1] - 8
        first1, second1 = stack(q[0, :count] for q in z1), stack(q[1] for q in z1)
        rows = stack(q[0, count:] for q in [near1] + z1)
        first1, second1, near2 = tie((first1, second1, near2))
        first_y, second_x = over_y(first1), over_x(second1)
        z2_three = move(near2, ALONG_Z[3])
        first_y, second_x, z2_three, near2, far_side = tie((first_y, second_x, z2_three, near2, far_side))

        near1 = stack([stack([first1, first_y]), stack([second1, second_x])[:, :, :count]])
        far_rows = jnp.concatenate([far_side[0, :1, 3 * count :], second_x[:, count:]])
        early = [stack(q[h] for q in (z2_one, z2_three)) for h in range(2)]
        unit = lambda v: v.reshape(-1, count // 2, COLUMNS)
        to_x, to_y = (jnp.concatenate([unit(near1[h]), unit(early[1 - h])]) for h in range(2))
        near1, to_x, to_y, rows, far_rows, near2, far_side, early = tie(
            (near1, to_x, to_y, rows, far_rows, near2, far_side, early)
        )
        by_x, by_y = over_x(to_x), over_y(to_y)
        near_core1, core_side = over_core(near1), over_core(far_side)
        z2_two = move(near2, ALONG_Z[2])
        params = unpack(at, rows, far_rows, sizes)
        by_x, by_y, near_core1, core_side, params, z2_two = tie(
            (by_x, by_y, near_core1, core_side, params, z2_two)
        )

        late = [z2_two[h : h + 1] for h in range(2)]
        units = unit(near1[0]).shape[0]
        far1 = stack([v[:units].reshape(near1.shape[1:]) for v in (by_x, by_y)])
        far1, late = tie((far1, late))
        far_core1 = over_core(far1)
        late_far = [over_y(late[0]), over_x(late[1])]
        late_far, far_core1 = tie((late_far, far_core1))

        attention = (w_qkv, w_out, far_side, core_side) + (near1, far1) * 2 + (near_core1, far_core1) * 2
        early_far = [v[units:].reshape(early[0].shape) for v in (by_y, by_x)]
        order = lambda e, l: jnp.concatenate([e[:1], l, e[1:]])
        first2, second2 = (
            stack([order(early[h], late[h]), order(early_far[h], late_far[h])]) for h in range(2)
        )
        first2, second2, attention, params, plan = tie((first2, second2, attention, params, plan))
        far_first2, far_second2 = over_x(first2), over_y(second2)
        core2 = [over_core(v) for v in (first2, second2)]
    else:
        at = jnp.zeros((4,), jnp.int32)
        plan, xp, cp, cos, sin = prepare(segment_ids, x, c)
        params = [gather(v[None]).reshape(1, -1).astype(F32) for v in vectors]
        attention = gather(w_qkv), gather(w_out)
        forward = gather(w_up), gather(w_down)
    g1, b1, bqkv, bout, g2, b2, bup, bdown = params
    (qkv, o, lse, x1), (wqkv, wout) = attend(plan, at, xp, cos, sin, g1, b1, bqkv, bout, attention)
    if tuned:
        far_first2, far_second2, core2, x1 = tie((far_first2, far_second2, core2, x1))
        far_core2 = over_core(far_first2), over_core(far_second2)
        forward = (
            w_up, w_down, far_side, core_side, first2, far_first2, second2, far_second2,
            core2[0], far_core2[0], core2[1], far_core2[1],
        )
    outp, dx1, da, gbup, sums2, *parts2 = feed(at, x1, cp, g2, b2, bup, bdown, forward)
    back = functools.partial(attend_back, plan, qkv, da, lse, cos, sin, wout)
    split = 1
    if tuned:
        kept2, sent2 = parts2
        got2 = over_core(sent2)
        dqkv, bias_low = back(0, split)
        got2, dqkv = tie((got2, dqkv))
        group2 = Sum(kept2, got2)
        to_x, to_y, dqkv = tie(group2.plane_one() + (dqkv,))
        by_x, by_y = over_x(to_x), over_y(to_y)
    else:
        dqkv, bias_low = back(0, split)
    dqkv, bias_high = back(split, GENES - split, (dqkv,))
    dxp, sums1 = project_back(xp, g1, dx1, dqkv, wqkv)
    sums = [sums1, bias_low, bias_high, sums2, gbup]
    if tuned:
        by_x, by_y, sums, dxp, dqkv = tie((by_x, by_y, sums, dxp, dqkv))
        to_y, to_x = group2.plane_two(by_x, by_y)
        to_y, to_x, dqkv = tie((to_y, to_x, dqkv))
        by_y, by_x = over_y(to_y), over_x(to_x)
        kept1, sent1 = grads(at, xp, g1, b1, o, da, dqkv, sums)
        by_y, by_x, kept1, sent1 = tie((by_y, by_x, kept1, sent1))
        got1 = over_core(sent1)
        got1, *to_z2 = tie([got1] + group2.along_z(by_y, by_x))
        group1 = Sum(kept1, got1)
        to_x, to_y, *to_z2 = tie([*group1.plane_one(), *to_z2])
        two = move(to_z2[1], ALONG_Z[2])
        parts = [add(kept1[i : i + Z_SIZE], got1[i : i + Z_SIZE]) for i in (0, 4, 16, 20)]
        by_x, by_y, two, parts, *to_z2 = tie((over_x(to_x), over_y(to_y), two, parts, to_z2[0], to_z2[2]))
        to_y, to_x = low(parts[1] + by_x[Z_SIZE:]), low(parts[3] + by_y[Z_SIZE:])
        to_y, to_x, *to_z2 = tie([to_y, to_x, *to_z2])
        one, three = move(to_z2[0], ALONG_Z[1]), move(to_z2[1], ALONG_Z[3])
        parts = parts[0] + by_x[:Z_SIZE], parts[2] + by_y[:Z_SIZE]
        by_y, by_x, one, three, parts = tie((over_y(to_y), over_x(to_x), one, three, parts))
        z2 = one, two, three
        at_z = lambda d: stack([parts[0][d] + by_y[d], parts[1][d] + by_x[d]])
        to_z1 = [low(at_z(d)) for d in range(1, Z_SIZE)]
        group1.own = at_z(0)
        total2 = group2.total(z2)
        to_z1, total2, outp, dxp = tie((to_z1, total2, outp, dxp))
        z1 = to_z(to_z1)
        by_y = over_y(total2)
        layer_out, input_grad = restore(plan, outp, dxp)
        z1, by_y, layer_out, input_grad = tie((z1, by_y, layer_out, input_grad))
        total1 = group1.total(z1)
        final2 = settle(at[2], total2, by_y)
        total1, final2 = tie((total1, final2))
        by_y, other2 = over_y(total1), over_core(final2)
        wup, wdown = deliver_second(at, final2, other2)
        by_y, wup, wdown = tie((by_y, wup, wdown))
        final1 = settle(at[2], total1, by_y)
        other1 = over_core(final1)
        wqkv, wout, *small = deliver_first(at, final1, other1, sizes)
    else:
        parts1 = grads(at, xp, g1, b1, o, da, dqkv, ())
        layer_out, input_grad = restore(plan, outp, dxp)
        wqkv, wout = map(reduce_rows, parts1)
        wup, wdown = map(reduce_rows, parts2)
        bias = bias_low + bias_high
        small = [sums1[0], sums1[1], bias[0], sums2[3], sums2[0], sums2[1], gbup[0], sums2[2]]
        small = [reduce_rows(v) for v in small]
    dg1, db1, dbqkv, dbout, dg2, db2, dbup, dbdown = small
    return (
        layer_out[None], input_grad[None], dg1, db1, wqkv, dbqkv, wout, dbout, dg2, db2,
        wup, dbup, wdown, dbdown,
    )


def solution(mesh):
    rows = ("fsdp", "replica")
    by_row = P(rows, None, None)
    vector, matrix = P("fsdp"), P("fsdp", None)
    params = (
        vector, vector, matrix, vector, matrix, vector, vector, vector, matrix, vector, matrix, vector,
    )
    in_specs = (by_row, by_row, P(rows, None), P(rows, None)) + params
    out_specs = (by_row, by_row) + params
    return jax.shard_map(
        functools.partial(body, tuned=tuned_mesh(mesh)),
        mesh=mesh, in_specs=in_specs, out_specs=out_specs, check_vma=False,
    )
```

```python
import functools
import math

import jax
import jax.numpy as jnp
import numpy as np
from jax import lax
from jax.experimental import pallas as pl
from jax.experimental.pallas import tpu as pltpu
from jax.sharding import PartitionSpec as P

HEADS = 12
HEAD_DIM = 64
GENES = 4
LANES = 128
EPSILON = 1e-05
NEG_FILL = -1000000000.0
F32 = jnp.float32
BF16 = jnp.bfloat16
MIB = 1 << 20


def nn(left, right):
    return lax.dot_general(left, right, (((1,), (0,)), ((), ())), preferred_element_type=F32)


def nt(left, right):
    return lax.dot_general(left, right, (((1,), (1,)), ((), ())), preferred_element_type=F32)


def tn(left, right):
    return lax.dot_general(left, right, (((0,), (0,)), ((), ())), preferred_element_type=F32)


def iota(shape, axis):
    return lax.broadcasted_iota(jnp.int32, shape, axis)


def full(shape):
    return pl.BlockSpec(shape, lambda *ids: (0,) * len(shape))


def rows_of(shape):
    return pl.BlockSpec(shape, lambda g, *ids: (g,) + (0,) * (len(shape) - 1))


def call(kernel, grid, in_specs, out_specs, out_shape, scratch=(), vmem=60, prefetch=1, name=None, cost=None, aliases=None):
    return pl.pallas_call(
        kernel,
        grid_spec=pltpu.PrefetchScalarGridSpec(
            num_scalar_prefetch=prefetch,
            grid=grid,
            in_specs=in_specs,
            out_specs=out_specs,
            scratch_shapes=list(scratch),
        ),
        out_shape=out_shape,
        input_output_aliases=aliases or {},
        compiler_params=pltpu.CompilerParams(
            dimension_semantics=("arbitrary",) * len(grid), vmem_limit_bytes=vmem * MIB
        ),
        name=name,
        cost_estimate=cost and pl.CostEstimate(flops=int(cost[0]), bytes_accessed=int(cost[1]), transcendentals=0),
    )


def shape_of(shape, dtype):
    return jax.ShapeDtypeStruct(shape, dtype)


def normalize(x):
    mean = jnp.mean(x, -1, keepdims=True)
    centered = x - mean
    scale = lax.rsqrt(jnp.mean(centered * centered, -1, keepdims=True) + EPSILON)
    return centered * scale, scale


def swap_halves(t):
    low = (iota(t.shape, 1) % HEAD_DIM) < HEAD_DIM // 2
    return jnp.where(
        low, pltpu.roll(t, LANES - HEAD_DIM // 2, 1), pltpu.roll(t, HEAD_DIM // 2, 1)
    )


def head_masks(rows):
    lane = iota((rows, LANES), 1)
    return [(lane < HEAD_DIM), (lane >= HEAD_DIM)]


def both(masks, value):
    return jnp.concatenate([keep(mask, value) for mask in masks], 0)


def beside(value):
    return jnp.concatenate([value[0], value[1]], 1)


def allowed_pairs(plan, gene, span):
    length = plan[gene]
    i, j = iota((span, span), 0), iota((span, span), 1)
    return ((i < length) & (j < length)) | (i == j)


def keep(mask, value):
    return jnp.where(mask, value, jnp.zeros_like(value))


Z_SIZE = 4
COLUMNS = 384
AXES = ("fsdp", "replica")
ANY = pl.BlockSpec(memory_space=pl.ANY)
PIECES = 32
EVERY = [(dx, dy, dc) for dx in range(2) for dy in range(2) for dc in range(2)]
SLOTS = (0, 128, 256, 640, 768, 896, 1024, 1408)
PACKED = 1536


def tuned_mesh(mesh):
    return mesh.shape["fsdp"] == 2 * Z_SIZE and mesh.shape["replica"] == 4


def pairs(step):
    out = []
    for z in range(Z_SIZE):
        for x in range(2):
            for y in range(2):
                for c in range(2):
                    tz, tx, ty, tc = step(z, x, y, c)
                    out.append((((z * 2 + x) * 2 + y) * 2 + c, (((tz % Z_SIZE) * 2 + tx) * 2 + ty) * 2 + tc))
    return out


ACROSS_X = pairs(lambda z, x, y, c: (z, 1 - x, y, c))
ACROSS_Y = pairs(lambda z, x, y, c: (z, x, 1 - y, c))
ACROSS_CORE = pairs(lambda z, x, y, c: (z, x, y, 1 - c))
ALONG_Z = [pairs(functools.partial(lambda d, z, x, y, c: (z + d, x, y, c), d)) for d in range(Z_SIZE)]
tie = lax.optimization_barrier


def move(array, table):
    return lax.ppermute(array, AXES, table)


def place():
    f, r = lax.axis_index("fsdp"), lax.axis_index("replica")
    return jnp.stack([f // 2, f % 2, r // 2, r % 2]).astype(jnp.int32)


def spot(at, dz, dx, dy, dc):
    z = lax.rem(at[0] + (Z_SIZE - dz), Z_SIZE)
    return z * 2 + lax.bitwise_xor(at[1], dx), lax.bitwise_xor(at[2], dy), lax.bitwise_xor(at[3], dc)


def piece_index(half, dz, dx, dy):
    return (16 + dy * 8 + dx * 4 if half else dx * 8 + dy * 4) + dz


def at_rows(start, size):
    return pl.ds(pl.multiple_of(start, 16), size)


def at_columns(start, size):
    return pl.ds(pl.multiple_of(start, LANES), size)


def quarters_kernel(at, *refs):
    wqkv, wout, wup, wdown = refs[:4]
    vectors, (near1, near2, near, side, packed) = refs[4:12], refs[12:]
    width = wout.shape[1]
    rows = wout.shape[0]
    packed[...] = jnp.zeros_like(packed)
    for ref, start in zip(vectors, SLOTS):
        packed[:, start : start + ref.shape[0]] = ref[...].reshape(1, -1)
    tail = jnp.zeros((8, COLUMNS), BF16)
    for i in range(4):
        part = jnp.broadcast_to(packed[:, i * COLUMNS : (i + 1) * COLUMNS], (8, COLUMNS))
        tail = jnp.where(iota((8, COLUMNS), 0) == i, part, tail)
    for y in range(2):
        for b in range(4):
            ref, base = (wqkv, b * width) if b < 3 else (wout, 0)
            start = base + y * COLUMNS
            side[y, b // 2, (b % 2) * rows : (b % 2 + 1) * rows, :] = ref[:, start : start + COLUMNS]
            start = b * width + y * COLUMNS
            side[y, 0, (2 + b) * rows : (3 + b) * rows, :] = wup[:, start : start + COLUMNS]
        here = slice(y * COLUMNS, (y + 1) * COLUMNS)
        side[y, 1, 2 * rows : 6 * rows, :] = wdown[:, here]
        for h in range(2):
            side[y, h, 6 * rows : 6 * rows + 8, :] = tail
    near1[:, 0 : 2 * rows, :] = side[at[2], :, 0 : 2 * rows, :]
    near2[...] = side[at[2], :, 2 * rows : 6 * rows, :]
    for h in range(2):
        near1[h, 2 * rows : 2 * rows + 8, :] = tail
    near[:, 0 : 2 * rows + 8, :] = near1[...]
    near[:, 2 * rows + 8 : 6 * rows + 8, :] = near2[...]


def quarters(at, wqkv, wout, wup, wdown, vectors):
    rows = wqkv.shape[0] // 2
    shapes = [
        (2, 2 * rows + 8, COLUMNS),
        (2, 4 * rows, COLUMNS),
        (2, 6 * rows + 8, COLUMNS),
        (2, 2, 6 * rows + 8, COLUMNS),
    ]
    matrices = (wqkv, wout, wup, wdown)
    mine = lambda v: pl.BlockSpec((v.shape[0] // 2, v.shape[1]), lambda i, at: (at[3], 0))
    return call(
        quarters_kernel,
        (1,),
        [mine(v) for v in matrices] + [full(v.shape) for v in vectors],
        [full(s) for s in shapes],
        [shape_of(s, BF16) for s in shapes],
        [pltpu.VMEM((1, PACKED), BF16)],
        name="quarters",
        cost=(0, 6e6),
    )(at, *matrices, *vectors)


def rel_mask(at, columns, size):
    row = iota((2 * Z_SIZE, columns), 0)
    z = (at[0] + Z_SIZE - row % Z_SIZE) % Z_SIZE
    shard = z * 2 + jnp.where(row < Z_SIZE, at[1], 1 - at[1])
    return iota((2 * Z_SIZE, columns), 1) // size == shard


def spread(size, columns):
    lanes = -(-size // LANES) * LANES
    lane, column = iota((lanes, columns), 0), iota((lanes, columns), 1)
    return jnp.where(column % size == lane, 1.0, 0.0).astype(BF16)


def unpack_kernel(at, near_ref, far_ref, *refs):
    out, row_ref = refs[:8], refs[8]
    for x_bit, rows in enumerate((near_ref, far_ref)):
        for d in range(Z_SIZE):
            here = x_bit * Z_SIZE + d
            for i in range(4):
                row_ref[here : here + 1, i * COLUMNS : (i + 1) * COLUMNS] = rows[d, i : i + 1, :].astype(F32)
    for ref, start in zip(out, SLOTS):
        columns = ref.shape[1]
        size = columns // (2 * Z_SIZE)
        table = spread(size, columns)
        got = nn(row_ref[:, start : start + table.shape[0]].astype(BF16), table)
        ref[...] = jnp.sum(jnp.where(rel_mask(at, columns, size), got, 0.0), 0, keepdims=True)


def unpack(at, near, far, sizes):
    shapes = [(1, n * 2 * Z_SIZE) for n in sizes]
    return call(
        unpack_kernel,
        (1,),
        [full(near.shape)] * 2,
        [full(s) for s in shapes],
        [shape_of(s, F32) for s in shapes],
        [pltpu.VMEM((2 * Z_SIZE, PACKED), F32)],
        name="unpack",
        cost=(1e8, 1e5),
    )(at, near, far)


def plan_of(segments):
    lengths = [jnp.sum(jnp.where(segments == g, 1.0, 0.0)).astype(jnp.int32) for g in range(GENES)]
    span = segments.size // GENES
    starts, before, start, free = [], [], 0, 0
    for g in range(GENES):
        starts.append(start)
        before.append(free)
        start = start + lengths[g]
        free = free + span - lengths[g]
    return [jnp.asarray(v, jnp.int32) for v in lengths + starts + before + [start]]


def source_of_slots(plan, gene, slots):
    length = plan[gene]
    return jnp.where(
        slots < length,
        plan[GENES + gene] + slots,
        plan[3 * GENES] + plan[2 * GENES + gene] + slots - length,
    )


def prepare_kernel(seg_ref, x_ref, c_ref, freq_ref, plan_ref, xp_ref, cp_ref, cos_ref, sin_ref):
    gene = pl.program_id(0)
    span = xp_ref.shape[0]
    length = x_ref.shape[0]

    @pl.when(gene == 0)
    def _():
        for i, v in enumerate(plan_of(seg_ref[...])):
            plan_ref[i] = v

    slots = iota((span, 1), 0)
    source = source_of_slots(plan_ref, gene, slots)
    pick = jnp.where(iota((span, length), 1) == source, 1.0, 0.0).astype(BF16)
    xp_ref[...] = nn(pick, x_ref[...]).astype(BF16)
    cp_ref[...] = nn(pick, c_ref[...]).astype(BF16)
    start = jnp.where(slots < plan_ref[gene], plan_ref[GENES + gene], plan_ref[3 * GENES])
    angle = (source - start).astype(F32) * freq_ref[...]
    low = iota((span, LANES), 1) % HEAD_DIM < HEAD_DIM // 2
    cos_ref[...] = jnp.cos(angle)
    sine = jnp.sin(angle)
    sin_ref[...] = jnp.where(low, -sine, sine)


def prepare(segments, x, c):
    length, width = x.shape
    span = length // GENES
    frequency = np.power(10000.0, np.arange(HEAD_DIM // 2) * (-2.0 / HEAD_DIM))
    frequency = jnp.asarray(np.tile(frequency, LANES // (HEAD_DIM // 2))[None], F32)
    return call(
        prepare_kernel,
        (GENES,),
        [full((1, length)), full((length, width)), full((length, width)), full((1, LANES))],
        [
            pl.BlockSpec(memory_space=pltpu.SMEM),
            rows_of((span, width)),
            rows_of((span, width)),
            rows_of((span, LANES)),
            rows_of((span, LANES)),
        ],
        [
            shape_of((16,), jnp.int32),
            shape_of((length, width), BF16),
            shape_of((length, width), BF16),
            shape_of((length, LANES), F32),
            shape_of((length, LANES), F32),
        ],
        prefetch=0,
        name="prepare",
        cost=(3.3e9, 8e6),
    )(segments, x, c, frequency)


def far_piece(refs, half, dz, dx, dy, dc):
    refs = refs[4 * dc : 4 * dc + 4]
    ref, at = (refs[dx], (dy, dz - 1)) if half == 0 else (refs[2 + dy], (dx, dz - 1))
    return ref.at[(half,) + at] if len(ref.shape) == 5 else ref.at[at]


def load_matrices(at, source, wqkv_ref, wout_ref, sem):
    width = wout_ref.shape[0]
    rows = width // (4 * Z_SIZE)
    own = at_rows((at[0] * 2 + at[1]) * 2 * rows, 2 * rows)
    pltpu.make_async_copy(source[0], wqkv_ref.at[own], sem.at[0]).start()
    pltpu.make_async_copy(source[1], wout_ref.at[own], sem.at[1]).start()

    def put(piece, f, y, c):
        down = at_rows((f * 2 + c) * rows, rows)
        for b in range(4):
            src = piece(b // 2).at[pl.ds((b % 2) * rows, rows)]
            across = at_columns((b % 3) * width + y * COLUMNS, COLUMNS)
            dst = wqkv_ref if b < 3 else wout_ref
            pltpu.make_async_copy(src, dst.at[down, across], sem.at[b // 3]).start()

    for dc in range(2):
        f, _, c = spot(at, 0, 1, 0, dc)
        for y in range(2):
            put(lambda half: source[2 + dc].at[y, half, pl.ds(0, 2 * rows)], f, y, c)

    def one(dz, carry):
        for dx, dy, dc in EVERY:
            put(lambda half: far_piece(source[4:], half, dz, dx, dy, dc), *spot(at, dz, dx, dy, dc))
        return carry

    lax.fori_loop(1, Z_SIZE, one, 0)


def attend_kernel(plan, at, *refs, pieces):
    (xp_ref, cos_ref, sin_ref, g1_ref, b1_ref, bqkv_ref, bout_ref), refs = refs[:7], refs[7:]
    source, refs = (refs[:12], refs[12:]) if pieces else (refs[:2], refs[2:])
    (qkv_ref, o_ref, lse_ref, x1_ref), refs = refs[:4], refs[4:]
    if pieces:
        whole, refs = refs[:2], refs[2:]
    wqkv_ref, wout_ref, mask_ref, a1_ref, sem = refs
    step = pl.program_id(0)
    gene = jnp.maximum(step - 1, 0)
    span = cos_ref.shape[0]
    width = xp_ref.shape[1]

    def wait_both():
        pltpu.make_async_copy(wqkv_ref, wqkv_ref, sem.at[0]).wait()
        pltpu.make_async_copy(wout_ref, wout_ref, sem.at[1]).wait()

    @pl.when(step == 0)
    def _():
        if pieces:
            load_matrices(at, source, wqkv_ref, wout_ref, sem)
        else:
            pltpu.make_async_copy(source[0], wqkv_ref, sem.at[0]).start()
            pltpu.make_async_copy(source[1], wout_ref, sem.at[1]).start()

        def norm(i, carry):
            here = pl.ds(i * span, span)
            xhat, _ = normalize(xp_ref[here, :].astype(F32))
            a1_ref[here, :] = (xhat * g1_ref[...] + b1_ref[...]).astype(BF16)
            return carry

        lax.fori_loop(0, GENES, norm, 0)
        wait_both()
        if pieces:
            pltpu.make_async_copy(wqkv_ref, whole[0], sem.at[0]).start()
            pltpu.make_async_copy(wout_ref, whole[1], sem.at[1]).start()

    @pl.when(step > 0)
    def _():
        attend_gene(
            plan, gene, xp_ref, a1_ref, cos_ref, sin_ref, bqkv_ref, bout_ref, wqkv_ref, wout_ref, mask_ref,
            qkv_ref, o_ref, lse_ref, x1_ref,
        )

    if pieces:

        @pl.when(step == pl.num_programs(0) - 1)
        def _():
            wait_both()


def attend_gene(
    plan, gene, xp_ref, a1_ref, cos_ref, sin_ref, bqkv_ref, bout_ref, wqkv_ref, wout_ref, mask_ref,
    qkv_ref, o_ref, lse_ref, x1_ref,
):
    span, width = o_ref.shape
    here = pl.ds(gene * span, span)
    x = xp_ref[here, :].astype(F32)
    a1 = a1_ref[here, :]
    cos, sin = cos_ref[...], sin_ref[...]
    for part in range(3):
        base = part * width
        t = nn(a1, wqkv_ref[:, base : base + width]) + bqkv_ref[:, base : base + width]
        for p in range(width // LANES):
            piece = t[:, p * LANES : (p + 1) * LANES]
            if part < 2:
                piece = piece * cos + swap_halves(piece) * sin
            qkv_ref[:, base + p * LANES : base + (p + 1) * LANES] = piece.astype(BF16)
    mask_ref[...] = jnp.where(allowed_pairs(plan, gene, span), 1.0, 0.0)
    masks = head_masks(span)
    def pair(p, carry):
        part = lambda i: at_columns(i * width + p * LANES, LANES)
        q = qkv_ref[:, part(0)]
        k = qkv_ref[:, part(1)] * BF16(1.0 / math.sqrt(HEAD_DIM))
        v = qkv_ref[:, part(2)]
        s = nt(both(masks, k), q).reshape(2, span, span)
        s = jnp.where((mask_ref[...] > 0.5)[None], s, NEG_FILL)
        peak = jnp.max(s, 1, keepdims=True)
        e = jnp.exp(s - peak)
        total = jnp.sum(e, 1, keepdims=True)
        weights = (e * (1.0 / total)).astype(BF16).reshape(2 * span, span)
        lse = peak + jnp.log(total)
        for h in range(2):
            lse_ref[pl.ds(2 * p + h, 1), :] = lse[h]
        o_ref[:, part(0)] = tn(weights, both(masks, v)).astype(BF16)
        return carry

    lax.fori_loop(0, width // LANES, pair, 0, unroll=True)
    x1_ref[...] = x + nn(o_ref[...], wout_ref[...]) + bout_ref[...]


def attend(plan, at, xp, cos, sin, g1, b1, bqkv, bout, source):
    length, width = xp.shape
    span = length // GENES
    pieces = len(source) == 12
    behind = lambda shape: pl.BlockSpec(shape, lambda g, *ids: (jnp.maximum(g - 1, 0), 0))
    weights = [shape_of((width, 3 * width), BF16), shape_of((width, width), BF16)]
    got = call(
        functools.partial(attend_kernel, pieces=pieces),
        (GENES + 1,),
        [
            full((length, width)),
            behind((span, LANES)),
            behind((span, LANES)),
            full((1, width)),
            full((1, width)),
            full((1, 3 * width)),
            full((1, width)),
        ]
        + [ANY] * len(source),
        [
            behind((span, 3 * width)),
            behind((span, width)),
            pl.BlockSpec((16, span), lambda g, *ids: (0, jnp.maximum(g - 1, 0))),
            behind((span, width)),
        ]
        + [ANY] * (2 if pieces else 0),
        [
            shape_of((length, 3 * width), BF16),
            shape_of((length, width), BF16),
            shape_of((16, length), F32),
            shape_of((length, width), F32),
        ]
        + (weights if pieces else []),
        [
            pltpu.VMEM((width, 3 * width), BF16),
            pltpu.VMEM((width, width), BF16),
            pltpu.VMEM((span, span), F32),
            pltpu.VMEM((length, width), BF16),
            pltpu.SemaphoreType.DMA((2,)),
        ],
        prefetch=2,
        name="attend",
        cost=(11e9, 20e6),
    )(plan, at, xp, cos, sin, g1, b1, bqkv, bout, *source)
    return got[:4], (got[4:] if pieces else source)


def feed_kernel(at, *refs, block, pieces, steps):
    (x1_hbm, c_hbm, g2_ref, b2_ref, bup_ref, bdown_ref), refs = refs[:6], refs[6:]
    source, refs = (refs[:12], refs[12:]) if pieces else (refs[:2], refs[2:])
    (out_hbm, dx1_hbm, da_hbm, gbup_ref, sums_ref, first_ref, second_ref), refs = refs[:7], refs[7:]
    x1_ref, c_ref, out_ref, da_ref, a2_ref, acc_ref, dh_ref, gr_ref, du_ref = refs[:9]
    wups, wdowns, gups, gdowns, load_sem, store_sem, in_sem, out_sem = refs[9:]
    step = pl.program_id(0)
    length, width = x1_ref.shape
    chunk = bup_ref.shape[1]
    blocks = length // block
    slot = lax.rem(step, 2)
    rows = width // (4 * Z_SIZE)

    def load(j, to):
        if pieces:
            own = at_rows((at[0] * 2 + at[1]) * 2 * rows, 2 * rows)
            src = source[0].at[:, at_columns(j * chunk, chunk)]
            pltpu.make_async_copy(src, wups.at[to, own], load_sem.at[0, to]).start()

            def put_up(piece, f, y, c):
                dst = wups.at[to, at_rows((f * 2 + c) * rows, rows), at_columns(y * COLUMNS, COLUMNS)]
                pltpu.make_async_copy(piece.at[at_rows(j * rows, rows)], dst, load_sem.at[0, to]).start()

            def put_down(piece, x, y, c):
                dst = wdowns.at[to, at_rows((x * 2 + c) * 4 * rows, 4 * rows), at_columns(y * COLUMNS, COLUMNS)]
                pltpu.make_async_copy(piece, dst, load_sem.at[1, to]).start()

            for dc in range(2):
                f, _, c = spot(at, 0, 1, 0, dc)
                for y in range(2):
                    put_up(source[2 + dc].at[y, 0, pl.ds(2 * rows, 4 * rows)], f, y, c)

            def one(dz, carry):
                for dx, dy, dc in EVERY:
                    put_up(far_piece(source[4:], 0, dz, dx, dy, dc), *spot(at, dz, dx, dy, dc))
                return carry

            lax.fori_loop(1, Z_SIZE, one, 0)

            @pl.when(j == at[0])
            def _():
                here = at_rows(at[1] * 8 * rows, 8 * rows)
                pltpu.make_async_copy(source[1], wdowns.at[to, here], load_sem.at[1, to]).start()
                for dc in range(2):
                    _, _, c = spot(at, 0, 1, 0, dc)
                    for y in range(2):
                        put_down(source[2 + dc].at[y, 1, pl.ds(2 * rows, 4 * rows)], 1 - at[1], y, c)

            @pl.when(j != at[0])
            def _():
                back = lax.rem(at[0] + (Z_SIZE - j), Z_SIZE)
                for dx, dy, dc in EVERY:
                    _, y, c = spot(at, back, dx, dy, dc)
                    put_down(far_piece(source[4:], 1, back, dx, dy, dc), lax.bitwise_xor(at[1], dx), y, c)

        else:
            part = source[0].at[:, at_columns(j * chunk, chunk)]
            pltpu.make_async_copy(part, wups.at[to], load_sem.at[0, to]).start()
            part = source[1].at[at_rows(j * chunk, chunk), :]
            pltpu.make_async_copy(part, wdowns.at[to], load_sem.at[1, to]).start()

    def store(j, to):
        if pieces:

            def one(dz, carry):
                for dx, dy, dc in EVERY:
                    f, y, c = spot(at, Z_SIZE - dz, dx, dy, dc)
                    src = gups.at[to, at_rows(f * 2 * rows + c * rows, rows), at_columns(y * COLUMNS, COLUMNS)]
                    dst = (first_ref, second_ref)[dc].at[piece_index(0, dz, dx, dy), at_rows(j * rows, rows)]
                    pltpu.make_async_copy(src, dst, store_sem.at[0, to]).start()
                return carry

            lax.fori_loop(0, Z_SIZE, one, 0)
            ahead = lax.rem(j + Z_SIZE - at[0], Z_SIZE)
            for dx, dy, dc in EVERY:
                f, y, c = spot(at, 0, dx, dy, dc)
                x = lax.bitwise_xor(at[1], dx)
                src = gdowns.at[to, at_rows((x * 2 + c) * 4 * rows, 4 * rows), at_columns(y * COLUMNS, COLUMNS)]
                dst = (first_ref, second_ref)[dc].at[piece_index(1, ahead, dx, dy)]
                pltpu.make_async_copy(src, dst, store_sem.at[1, to]).start()
        else:
            part = first_ref.at[:, at_columns(j * chunk, chunk)]
            pltpu.make_async_copy(gups.at[to], part, store_sem.at[0, to]).start()
            part = second_ref.at[at_rows(j * chunk, chunk), :]
            pltpu.make_async_copy(gdowns.at[to], part, store_sem.at[1, to]).start()

    def wait_load(to):
        pltpu.make_async_copy(wups.at[to], wups.at[to], load_sem.at[0, to]).wait()
        pltpu.make_async_copy(wdowns.at[to], wdowns.at[to], load_sem.at[1, to]).wait()

    def wait_store(to):
        pltpu.make_async_copy(gups.at[to], gups.at[to], store_sem.at[0, to]).wait()
        pltpu.make_async_copy(gdowns.at[to], gdowns.at[to], store_sem.at[1, to]).wait()

    def bring(i):
        here = at_rows(i * block, block)
        return [
            pltpu.make_async_copy(x1_hbm.at[here, :], x1_ref.at[here, :], in_sem.at[0, i]),
            pltpu.make_async_copy(c_hbm.at[here, :], c_ref.at[here, :], in_sem.at[1, i]),
        ]

    def give(i):
        here = at_rows(i * block, block)
        return [
            pltpu.make_async_copy(out_ref.at[here, :], out_hbm.at[here, :], out_sem.at[0, i]),
            pltpu.make_async_copy(x1_ref.at[here, :], dx1_hbm.at[here, :], out_sem.at[1, i]),
            pltpu.make_async_copy(da_ref.at[here, :], da_hbm.at[here, :], out_sem.at[2, i]),
        ]

    @pl.when(step == 0)
    def _():
        for i in range(blocks):
            bring(i)[0].start()
        load(0, 0)
        for i in range(blocks):
            bring(i)[1].start()

        def one(i, carry):
            here = pl.ds(i * block, block)
            bring(i)[0].wait()
            xhat, _ = normalize(x1_ref[here, :])
            a2_ref[here, :] = (xhat * g2_ref[...] + b2_ref[...]).astype(BF16)
            acc_ref[here, :] = jnp.zeros((block, width), F32)
            dh_ref[here, :] = jnp.zeros((block, width), F32)
            return carry

        lax.fori_loop(0, blocks, one, 0)
        for i in range(blocks):
            bring(i)[1].wait()

    wait_load(slot)

    @pl.when(step < steps - 1)
    def _():
        load(step + 1, 1 - slot)

    wup_ref, wdown_ref = wups.at[slot], wdowns.at[slot]

    def one(i, bias_sum):
        here = pl.ds(i * block, block)
        u = nn(a2_ref[here, :], wup_ref[...]) + bup_ref[...]
        phi = 0.5 + 0.5 * lax.erf(u * math.sqrt(0.5))
        slope = phi + u * (jnp.exp(-0.5 * u * u) * (1.0 / math.sqrt(2.0 * math.pi)))
        gr = (u * phi).astype(BF16)
        gr_ref[here, :] = gr
        du = (nt(c_ref[here, :], wdown_ref[...]) * slope).astype(BF16)
        du_ref[here, :] = du
        out = nn(gr, wdown_ref[...])
        dh = nt(du, wup_ref[...])

        acc_ref[here, :] += out
        dh_ref[here, :] += dh
        return bias_sum + jnp.sum(du.astype(F32), 0, keepdims=True)

    gbup_ref[...] = lax.fori_loop(0, blocks, one, jnp.zeros((1, chunk), F32))

    @pl.when(step >= 2)
    def _():
        wait_store(slot)

    gdowns[slot] = tn(gr_ref[...], c_ref[...]).astype(BF16)
    gups[slot] = tn(a2_ref[...], du_ref[...]).astype(BF16)
    store(step, slot)

    @pl.when(step == steps - 1)
    def _():
        def one(i, sums):
            here = pl.ds(i * block, block)
            x1 = x1_ref[here, :]
            xhat, scale = normalize(x1)
            out_ref[here, :] = (x1 + acc_ref[here, :] + bdown_ref[...]).astype(BF16)
            dh = dh_ref[here, :]
            c = c_ref[here, :].astype(F32)
            e = dh * g2_ref[...]
            dx1 = c + scale * (
                e - jnp.mean(e, -1, keepdims=True) - xhat * jnp.mean(e * xhat, -1, keepdims=True)
            )
            x1_ref[here, :] = dx1
            da = dx1.astype(BF16)
            da_ref[here, :] = da
            for copy in give(i):
                copy.start()
            new = (
                jnp.sum(dh * xhat, 0, keepdims=True),
                jnp.sum(dh, 0, keepdims=True),
                jnp.sum(c, 0, keepdims=True),
                jnp.sum(da.astype(F32), 0, keepdims=True),
            )
            return tuple(a + b for a, b in zip(sums, new))

        sums = lax.fori_loop(0, blocks, one, (jnp.zeros((1, width), F32),) * 4)
        for i in range(4):
            sums_ref[i : i + 1, :] = sums[i]
        for i in range(blocks):
            for copy in give(i):
                copy.wait()
        wait_store(1 - slot)
        wait_store(slot)


def feed(at, x1, c, g2, b2, bup, bdown, source):
    length, width = x1.shape
    hidden = bup.shape[1]
    steps = 4
    chunk = hidden // steps
    pieces = len(source) == 12
    if pieces:
        rows = width // Z_SIZE
        stored = [shape_of((PIECES, rows, COLUMNS), BF16)] * 2
    else:
        stored = [shape_of((width, hidden), BF16), shape_of((hidden, width), BF16)]
    return call(
        functools.partial(feed_kernel, block=length // 2, pieces=pieces, steps=steps),
        (steps,),
        [
            ANY,
            ANY,
            full((1, width)),
            full((1, width)),
            pl.BlockSpec((1, chunk), lambda j, *ids: (0, j)),
            full((1, width)),
        ]
        + [ANY] * len(source),
        [
            ANY,
            ANY,
            ANY,
            pl.BlockSpec((1, chunk), lambda j, *ids: (0, j)),
            full((8, width)),
            ANY,
            ANY,
        ],
        [
            shape_of((length, width), BF16),
            shape_of((length, width), F32),
            shape_of((length, width), BF16),
            shape_of((1, hidden), F32),
            shape_of((8, width), F32),
        ]
        + stored,
        [
            pltpu.VMEM((length, width), F32),
            pltpu.VMEM((length, width), BF16),
            pltpu.VMEM((length, width), BF16),
            pltpu.VMEM((length, width), BF16),
            pltpu.VMEM((length, width), BF16),
            pltpu.VMEM((length, width), F32),
            pltpu.VMEM((length, width), F32),
            pltpu.VMEM((length, chunk), BF16),
            pltpu.VMEM((length, chunk), BF16),
            pltpu.VMEM((2, width, chunk), BF16),
            pltpu.VMEM((2, chunk, width), BF16),
            pltpu.VMEM((2, width, chunk), BF16),
            pltpu.VMEM((2, chunk, width), BF16),
            pltpu.SemaphoreType.DMA((2, 2)),
            pltpu.SemaphoreType.DMA((2, 2)),
            pltpu.SemaphoreType.DMA((2, 4)),
            pltpu.SemaphoreType.DMA((3, 4)),
        ],
        name="feed",
        cost=(29e9, 40e6),
    )(at, x1, c, g2, b2, bup, bdown, *source)


def attend_back_kernel(
    plan, qkv_ref, da_ref, lse_ref, cos_ref, sin_ref, wout_ref, *refs, base, count,
):
    dqkv_ref, bias_ref, dout_ref, mask_ref = refs[-4:]
    gene = pl.program_id(0) + base
    span, width = da_ref.shape
    score_scale = 1.0 / math.sqrt(HEAD_DIM)
    dout_ref[...] = nt(da_ref[...], wout_ref[...]).astype(BF16)
    mask_ref[...] = jnp.where(allowed_pairs(plan, gene, span), 1.0, 0.0)
    cos, sin = cos_ref[...], sin_ref[...]
    masks = head_masks(span)

    def back(t):
        return (t * cos - swap_halves(t) * sin).astype(BF16)

    def pair(p, carry):
        part = lambda i: at_columns(i * width + p * LANES, LANES)
        q = qkv_ref[:, part(0)]
        k = qkv_ref[:, part(1)] * BF16(score_scale)
        v = qkv_ref[:, part(2)]
        dout = dout_ref[:, part(0)]
        kh = both(masks, k)
        s = nt(kh, q).reshape(2, span, span)
        s = jnp.where((mask_ref[...] > 0.5)[None], s, NEG_FILL)
        weights = jnp.exp(s - stack(lse_ref[pl.ds(2 * p + h, 1), :] for h in range(2)))
        dw = nt(both(masks, v), dout).reshape(2, span, span)
        dot = jnp.sum(weights * dw, 1, keepdims=True)
        ds = (weights * (dw - dot)).astype(BF16)
        weights = weights.astype(BF16)
        dv = nn(beside(weights), both(masks, dout))
        dk = nn(beside(ds), both(masks, q))
        dq = tn(ds.reshape(2 * span, span), kh)
        dqkv_ref[:, part(0)] = back(dq)
        dqkv_ref[:, part(1)] = back(dk * score_scale)
        dqkv_ref[:, part(2)] = dv.astype(BF16)
        return carry

    lax.fori_loop(0, width // LANES, pair, 0, unroll=2 if count == 1 else True)

    bqkv = jnp.sum(dqkv_ref[...].astype(F32), 0, keepdims=True)

    @pl.when(gene == base)
    def _():
        bias_ref[0:1, :] = bqkv

    @pl.when(gene > base)
    def _():
        bias_ref[0:1, :] += bqkv


def attend_back(plan, qkv, da, lse, cos, sin, wout, base, count, before=()):
    length, width = da.shape
    span = length // GENES
    rows = lambda shape: pl.BlockSpec(shape, lambda g, *ids: (g + base, 0))
    return call(
        functools.partial(attend_back_kernel, base=base, count=count),
        (count,),
        [
            rows((span, 3 * width)),
            rows((span, width)),
            pl.BlockSpec((16, span), lambda g, *ids: (0, g + base)),
            rows((span, LANES)),
            rows((span, LANES)),
            full((width, width)),
        ]
        + [ANY] * len(before),
        [rows((span, 3 * width)), full((8, 3 * width))],
        [shape_of((length, 3 * width), BF16), shape_of((8, 3 * width), F32)],
        [pltpu.VMEM((span, width), BF16), pltpu.VMEM((span, span), F32)],
        name="attend_back",
        cost=(4e9 * count, 6e6 * count),
        aliases={7 + i: i for i in range(len(before))},
    )(plan, qkv, da, lse, cos, sin, wout, *before)


def project_back_kernel(xp_ref, g1_ref, dx1_ref, dqkv_ref, wqkv_ref, dxp_ref, sums_ref):
    step = pl.program_id(0)
    dh = nt(dqkv_ref[...], wqkv_ref[...])
    xhat, scale = normalize(xp_ref[...].astype(F32))
    e = dh * g1_ref[...]
    dx = dx1_ref[...] + scale * (
        e - jnp.mean(e, -1, keepdims=True) - xhat * jnp.mean(e * xhat, -1, keepdims=True)
    )
    dxp_ref[...] = dx.astype(BF16)

    @pl.when(step == 0)
    def _():
        sums_ref[...] = jnp.zeros_like(sums_ref)

    sums_ref[0:1, :] += jnp.sum(dh * xhat, 0, keepdims=True)
    sums_ref[1:2, :] += jnp.sum(dh, 0, keepdims=True)


def project_back(xp, g1, dx1, dqkv, wqkv):
    length, width = xp.shape
    span = length // GENES
    return call(
        project_back_kernel,
        (GENES,),
        [
            rows_of((span, width)),
            full((1, width)),
            rows_of((span, width)),
            rows_of((span, 3 * width)),
            full((width, 3 * width)),
        ],
        [rows_of((span, width)), full((8, width))],
        [shape_of((length, width), BF16), shape_of((8, width), F32)],
        prefetch=0,
        name="project_back",
        cost=(0, 0),
    )(xp, g1, dx1, dqkv, wqkv)


def grads_kernel(at, *refs, pieces):
    (xp_hbm, o_hbm, da_hbm, dqkv_hbm, g1_ref, b1_ref), refs = refs[:6], refs[6:]
    sums, refs = (refs[:5], refs[5:]) if pieces else ((), refs)
    first_ref, second_ref, xp_ref, o_ref, da_ref, dqkv_ref, a1_ref, grad_ref, in_sem, sem, *rest = refs
    small_ref, small_sem = rest if pieces else (None, None)
    step = pl.program_id(0)
    width = xp_ref.shape[1]
    rows = width // (4 * Z_SIZE)
    slot = lax.rem(step, 2)

    def bring(j):
        part = dqkv_hbm.at[:, at_columns(j * width, width)]
        return pltpu.make_async_copy(part, dqkv_ref.at[lax.rem(j, 2)], in_sem.at[3 + lax.rem(j, 2)])

    whole = [
        pltpu.make_async_copy(src, dst, in_sem.at[i])
        for i, (src, dst) in enumerate(((o_hbm, o_ref), (da_hbm, da_ref), (xp_hbm, xp_ref)))
    ]

    def wait(to):
        pltpu.make_async_copy(grad_ref.at[to], grad_ref.at[to], sem.at[to]).wait()

    def store(half, base, to):
        def one(dz, carry):
            for dx, dy, dc in EVERY:
                f, y, c = spot(at, Z_SIZE - dz, dx, dy, dc)
                src = grad_ref.at[to, at_rows(f * 2 * rows + c * rows, rows), at_columns(y * COLUMNS, COLUMNS)]
                dst = (first_ref, second_ref)[dc].at[
                    jnp.where(half == 0, piece_index(0, dz, dx, dy), piece_index(1, dz, dx, dy)),
                    at_rows(base * rows, rows),
                ]
                pltpu.make_async_copy(src, dst, sem.at[to]).start()
            return carry

        lax.fori_loop(0, Z_SIZE, one, 0)

    def pack():
        sums1, low_ref, high_ref, sums2, gbup = sums
        line = lambda ref, i: ref[i : i + 1, :]
        vectors = [
            line(sums1, 0), line(sums1, 1), line(low_ref, 0) + line(high_ref, 0), line(sums2, 3),
            line(sums2, 0), line(sums2, 1), gbup[...], line(sums2, 2),
        ]
        shards = 2 * Z_SIZE
        columns = []
        for value in vectors:
            size = value.shape[1] // shards
            spread_out = jnp.broadcast_to(value, (shards, value.shape[1]))
            mask = iota(spread_out.shape, 1) // size == iota(spread_out.shape, 0)
            own = jnp.where(mask, spread_out, 0.0).astype(BF16)
            columns.append(nt(own, spread(size, value.shape[1])).astype(BF16))
        packed = jnp.concatenate(columns, 1).astype(F32)
        for f in range(shards):
            for i in range(4):
                part = packed[f : f + 1, i * COLUMNS : (i + 1) * COLUMNS]
                small_ref[f, i // 2, i % 2] = jnp.broadcast_to(part, (8, COLUMNS)).astype(BF16)

    def smalls(act):
        def one(dz, carry):
            for dx, dy, dc in EVERY:
                f, y, c = spot(at, Z_SIZE - dz, dx, dy, dc)
                for half in range(2):
                    src = small_ref.at[f, y, c]
                    dst = (first_ref, second_ref)[dc].at[piece_index(half, dz, dx, dy), pl.ds(2 * rows, 8)]
                    act(pltpu.make_async_copy(src, dst, small_sem))
            return carry

        lax.fori_loop(0, Z_SIZE, one, 0)

    @pl.when(step == 0)
    def _():
        for copy in whole:
            copy.start()
        bring(step).start()
        if pieces:
            pack()
            smalls(lambda copy: copy.start())
        whole[0].wait()
        whole[1].wait()
        grad_ref[0] = tn(o_ref[...], da_ref[...]).astype(BF16)
        if pieces:
            store(1, 1, 0)
        else:
            pltpu.make_async_copy(grad_ref.at[0], second_ref, sem.at[0]).start()
        whole[2].wait()
        xhat, _ = normalize(xp_ref[...].astype(F32))
        a1_ref[...] = (xhat * g1_ref[...] + b1_ref[...]).astype(BF16)

    @pl.when(step > 0)
    def _():
        bring(step - 1).wait()

        @pl.when(step < 3)
        def _():
            bring(step).start()

        @pl.when(step >= 2)
        def _():
            wait(slot)

        grad_ref[slot] = tn(a1_ref[...], dqkv_ref[lax.rem(step - 1, 2)]).astype(BF16)
        if pieces:
            store(lax.div(step - 1, 2), lax.rem(step - 1, 2), slot)
        else:
            dst = first_ref.at[:, at_columns((step - 1) * width, width)]
            pltpu.make_async_copy(grad_ref.at[slot], dst, sem.at[slot]).start()

    @pl.when(step == 3)
    def _():
        wait(0)
        wait(1)
        if pieces:
            smalls(lambda copy: copy.wait())


def grads(at, xp, g1, b1, o, da, dqkv, sums):
    pieces = bool(sums)
    length, width = xp.shape
    if pieces:
        rows = width // (2 * Z_SIZE) + 8
        stored = [shape_of((PIECES, rows, COLUMNS), BF16)] * 2
    else:
        stored = [shape_of((width, 3 * width), BF16), shape_of((width, width), BF16)]
    return call(
        functools.partial(grads_kernel, pieces=pieces),
        (4,),
        [ANY] * 4 + [full((1, width))] * 2 + [full(v.shape) for v in sums],
        [ANY, ANY],
        stored,
        [pltpu.VMEM((length, width), BF16)] * 3
        + [
            pltpu.VMEM((2, length, width), BF16),
            pltpu.VMEM((length, width), BF16),
            pltpu.VMEM((2, width, width), BF16),
            pltpu.SemaphoreType.DMA((5,)),
            pltpu.SemaphoreType.DMA((2,)),
        ]
        + ([pltpu.VMEM((2 * Z_SIZE, 2, 2, 8, COLUMNS), BF16), pltpu.SemaphoreType.DMA] if pieces else []),
        name="grads",
        cost=(5e9, 12e6),
    )(at, xp, o, da, dqkv, g1, b1, *sums)


def restore_kernel(plan, outp_ref, dxp_ref, out_ref, dx_ref):
    span, width = out_ref.shape
    slots = iota((1, span), 1)
    source = jnp.concatenate([source_of_slots(plan, g, slots) for g in range(GENES)], 1)
    codon = iota((span, outp_ref.shape[0]), 0) + pl.program_id(0) * span
    pick = jnp.where(codon == source, 1.0, 0.0).astype(BF16)
    out_ref[...] = nn(pick, outp_ref[...]).astype(BF16)
    dx_ref[...] = nn(pick, dxp_ref[...]).astype(BF16)


def restore(plan, outp, dxp):
    length, width = outp.shape
    span = length // GENES
    return call(
        restore_kernel,
        (GENES,),
        [full((length, width)), full((length, width))],
        [rows_of((span, width))] * 2,
        [shape_of((length, width), BF16)] * 2,
        name="restore",
        cost=(3.3e9, 8e6),
    )(plan, outp, dxp)


def deliver_first_kernel(at, mine, other, wqkv, wout, *rest):
    vectors, row_ref = rest[:8], rest[8]
    width = wout.shape[1]
    rows = wout.shape[0] // 2
    for dc, one in enumerate((mine, other)):
        c = lax.bitwise_xor(at[3], dc)
        here = pl.ds(pl.multiple_of(c * rows, 8), rows)
        for y in range(2):
            for b in range(4):
                ref, base = (wqkv, b * width) if b < 3 else (wout, 0)
                start = base + y * COLUMNS
                piece = one[y, b // 2, (b % 2) * rows : (b % 2 + 1) * rows, :]
                ref[here, start : start + COLUMNS] = piece.astype(F32)
            start = at_columns((y * 2 + c) * COLUMNS, COLUMNS)
            row_ref[:, start] = one[y, 0, 2 * rows : 2 * rows + 8, :].astype(F32)
    for ref, start in zip(vectors, SLOTS):
        ref[...] = row_ref[0:1, start : start + ref.shape[0]].reshape(ref.shape[0])


def deliver_first(at, mine, other, sizes):
    rows = (mine.shape[2] - 8) // 2
    width = 2 * COLUMNS
    shapes = [(2 * rows, 3 * width), (2 * rows, width)] + [(n,) for n in sizes]
    return call(
        deliver_first_kernel,
        (1,),
        [pl.BlockSpec(memory_space=pltpu.VMEM)] * 2,
        [full(s) for s in shapes],
        [shape_of(s, F32) for s in shapes],
        [pltpu.VMEM((8, PACKED), F32)],
        name="deliver_first",
        cost=(0, 2e6),
    )(at, mine, other)


def deliver_second_kernel(at, mine, other, wup, wdown):
    width = wdown.shape[1]
    rows = wup.shape[0] // 2
    for dc, two in enumerate((mine, other)):
        c = lax.bitwise_xor(at[3], dc)
        here = pl.ds(pl.multiple_of(c * rows, 8), rows)
        down = pl.ds(pl.multiple_of(c * 4 * rows, 8), 4 * rows)
        for y in range(2):
            for b in range(4):
                start = b * width + y * COLUMNS
                wup[here, start : start + COLUMNS] = two[y, 0, b * rows : (b + 1) * rows, :].astype(F32)
            wdown[down, y * COLUMNS : (y + 1) * COLUMNS] = two[y, 1].astype(F32)


def deliver_second(at, mine, other):
    rows = mine.shape[2] // 4
    width = 2 * COLUMNS
    shapes = [(2 * rows, 4 * width), (8 * rows, width)]
    return call(
        deliver_second_kernel,
        (1,),
        [pl.BlockSpec(memory_space=pltpu.VMEM)] * 2,
        [full(s) for s in shapes],
        [shape_of(s, F32) for s in shapes],
        name="deliver_second",
        cost=(0, 4e6),
    )(at, mine, other)


def gather(shard):
    return lax.all_gather(shard, "fsdp", axis=0, tiled=True)


def reduce_rows(grad):
    part = lax.psum_scatter(grad, "fsdp", scatter_dimension=0, tiled=True)
    return lax.psum(part.astype(BF16), "replica").astype(F32)


def low(value):
    return value.astype(BF16)


def add(*values):
    total = values[0].astype(F32)
    for v in values[1:]:
        total = total + v.astype(F32)
    return total


def to_z(arrays):
    arrays = arrays if isinstance(arrays, list) else [arrays] * 3
    return [move(v, ALONG_Z[d]) for d, v in zip((1, 2, 3), arrays)]


def over_x(array):
    return move(array, ACROSS_X)


def over_y(array):
    return move(array, ACROSS_Y)


def over_core(array):
    return move(array, ACROSS_CORE)


def stack(arrays):
    return jnp.stack(list(arrays))


class Sum:
    def __init__(self, kept, got):
        self.kept, self.got = kept, got

    def plane_one(self):
        return self.part(8, 16), self.part(24, 32)

    def part(self, start, stop, *more):
        return low(add(self.kept[start:stop], self.got[start:stop], *more))

    def plane_two(self, by_x, by_y):
        self.by_x, self.by_y = by_x, by_y
        return self.part(4, 8, by_x[Z_SIZE:]), self.part(20, 24, by_y[Z_SIZE:])

    def along_z(self, by_y, by_x):
        def at_z(d, rounded):
            first = add(self.kept[d], self.got[d], self.by_x[d], by_y[d])
            second = add(self.kept[16 + d], self.got[16 + d], self.by_y[d], by_x[d])
            return low(stack([first, second])) if rounded else stack([first, second])

        self.own = at_z(0, False)
        return [at_z(d, True) for d in range(1, Z_SIZE)]

    def total(self, by_z):
        return low(add(self.own, *by_z))


def settle(bit, mine, other):
    return jnp.where(bit == 0, stack([mine, other]), stack([other, mine]))


def body(
    layer_input, cotangent, segment_ids, pad_mask, ln1_gain, ln1_bias, w_qkv, b_qkv, w_out, b_out,
    ln2_gain, ln2_bias, w_up, b_up, w_down, b_down, *, tuned,
):
    vectors = (ln1_gain, ln1_bias, b_qkv, b_out, ln2_gain, ln2_bias, b_up, b_down)
    sizes = [v.shape[0] for v in vectors]
    x, c = layer_input[0], cotangent[0]
    if tuned:
        at = place()
        near1, near2, near, side = quarters(at, w_qkv, w_out, w_up, w_down, vectors)
        near1, near2, near, side, x = tie((near1, near2, near, side, x))
        z_one, z1_two, z1_three = move(near, ALONG_Z[1]), move(near1, ALONG_Z[2]), move(near1, ALONG_Z[3])
        far_side = over_x(side)
        prepared = prepare(segment_ids, x, c)
        z_one, z1_two, z1_three, prepared = tie((z_one, z1_two, z1_three, prepared))
        split = near1.shape[1]
        z1, z2_one = [z_one[:, :split], z1_two, z1_three], z_one[:, split:]
        plan, xp, cp, cos, sin = prepared

        count = near1.shape[1] - 8
        first1, second1 = stack(q[0, :count] for q in z1), stack(q[1] for q in z1)
        rows = stack(q[0, count:] for q in [near1] + z1)
        first1, second1, near2 = tie((first1, second1, near2))
        first_y, second_x = over_y(first1), over_x(second1)
        z2_three = move(near2, ALONG_Z[3])
        first_y, second_x, z2_three, near2, far_side = tie((first_y, second_x, z2_three, near2, far_side))

        near1 = stack([stack([first1, first_y]), stack([second1, second_x])[:, :, :count]])
        far_rows = jnp.concatenate([far_side[0, :1, 3 * count :], second_x[:, count:]])
        early = [stack(q[h] for q in (z2_one, z2_three)) for h in range(2)]
        unit = lambda v: v.reshape(-1, count // 2, COLUMNS)
        to_x, to_y = (jnp.concatenate([unit(near1[h]), unit(early[1 - h])]) for h in range(2))
        to_x, to_y, near2, far_side = tie((to_x, to_y, near2, far_side))
        by_x, by_y = over_x(to_x), over_y(to_y)
        near_core1, core_side = over_core(near1), over_core(far_side)
        z2_two = move(near2, ALONG_Z[2])
        params = unpack(at, rows, far_rows, sizes)
        by_x, by_y, near_core1, core_side, params, z2_two = tie(
            (by_x, by_y, near_core1, core_side, params, z2_two)
        )

        late = [z2_two[h : h + 1] for h in range(2)]
        units = unit(near1[0]).shape[0]
        far1 = stack([v[:units].reshape(near1.shape[1:]) for v in (by_x, by_y)])
        far1, late = tie((far1, late))
        far_core1 = over_core(far1)
        late_far = [over_y(late[0]), over_x(late[1])]
        late_far, far_core1 = tie((late_far, far_core1))

        attention = (w_qkv, w_out, far_side, core_side) + (near1, far1) * 2 + (near_core1, far_core1) * 2
        early_far = [v[units:].reshape(early[0].shape) for v in (by_y, by_x)]
        order = lambda e, l: jnp.concatenate([e[:1], l, e[1:]])
        first2, second2 = (
            stack([order(early[h], late[h]), order(early_far[h], late_far[h])]) for h in range(2)
        )
        first2, second2, attention, params, plan = tie((first2, second2, attention, params, plan))
        far_first2, far_second2 = over_x(first2), over_y(second2)
        core2 = [over_core(v) for v in (first2, second2)]
    else:
        at = jnp.zeros((4,), jnp.int32)
        plan, xp, cp, cos, sin = prepare(segment_ids, x, c)
        params = [gather(v[None]).reshape(1, -1).astype(F32) for v in vectors]
        attention = gather(w_qkv), gather(w_out)
        forward = gather(w_up), gather(w_down)
    g1, b1, bqkv, bout, g2, b2, bup, bdown = params
    (qkv, o, lse, x1), (wqkv, wout) = attend(plan, at, xp, cos, sin, g1, b1, bqkv, bout, attention)
    if tuned:
        far_first2, far_second2, core2, x1 = tie((far_first2, far_second2, core2, x1))
        far_core2 = over_core(far_first2), over_core(far_second2)
        forward = (
            w_up, w_down, far_side, core_side, first2, far_first2, second2, far_second2,
            core2[0], far_core2[0], core2[1], far_core2[1],
        )
    outp, dx1, da, gbup, sums2, *parts2 = feed(at, x1, cp, g2, b2, bup, bdown, forward)
    back = functools.partial(attend_back, plan, qkv, da, lse, cos, sin, wout)
    split = 1
    if tuned:
        kept2, sent2 = parts2
        got2 = over_core(sent2)
        dqkv, bias_low = back(0, split)
        got2, dqkv = tie((got2, dqkv))
        group2 = Sum(kept2, got2)
        to_x, to_y, dqkv = tie(group2.plane_one() + (dqkv,))
        by_x, by_y = over_x(to_x), over_y(to_y)
    else:
        dqkv, bias_low = back(0, split)
    dqkv, bias_high = back(split, GENES - split, (dqkv,))
    dxp, sums1 = project_back(xp, g1, dx1, dqkv, wqkv)
    sums = [sums1, bias_low, bias_high, sums2, gbup]
    if tuned:
        by_x, by_y, sums, dxp, dqkv = tie((by_x, by_y, sums, dxp, dqkv))
        to_y, to_x = group2.plane_two(by_x, by_y)
        to_y, to_x, dqkv = tie((to_y, to_x, dqkv))
        by_y, by_x = over_y(to_y), over_x(to_x)
        kept1, sent1 = grads(at, xp, g1, b1, o, da, dqkv, sums)
        by_y, by_x, kept1, sent1 = tie((by_y, by_x, kept1, sent1))
        got1 = over_core(sent1)
        got1, *to_z2 = tie([got1] + group2.along_z(by_y, by_x))
        group1 = Sum(kept1, got1)
        to_x, to_y, *to_z2 = tie([*group1.plane_one(), *to_z2])
        two = move(to_z2[1], ALONG_Z[2])
        parts = [add(kept1[i : i + Z_SIZE], got1[i : i + Z_SIZE]) for i in (0, 4, 16, 20)]
        by_x, by_y, two, parts, *to_z2 = tie((over_x(to_x), over_y(to_y), two, parts, to_z2[0], to_z2[2]))
        to_y, to_x = low(parts[1] + by_x[Z_SIZE:]), low(parts[3] + by_y[Z_SIZE:])
        to_y, to_x, *to_z2 = tie([to_y, to_x, *to_z2])
        one, three = move(to_z2[0], ALONG_Z[1]), move(to_z2[1], ALONG_Z[3])
        parts = parts[0] + by_x[:Z_SIZE], parts[2] + by_y[:Z_SIZE]
        by_y, by_x, one, three, parts = tie((over_y(to_y), over_x(to_x), one, three, parts))
        z2 = one, two, three
        at_z = lambda d: stack([parts[0][d] + by_y[d], parts[1][d] + by_x[d]])
        to_z1 = [low(at_z(d)) for d in range(1, Z_SIZE)]
        group1.own = at_z(0)
        to_z1, z2, outp, dxp = tie((to_z1, z2, outp, dxp))
        total2 = group2.total(z2)
        z1 = to_z(to_z1)
        by_y = over_y(total2)
        layer_out, input_grad = restore(plan, outp, dxp)
        z1, by_y, layer_out, input_grad = tie((z1, by_y, layer_out, input_grad))
        total1 = group1.total(z1)
        final2 = settle(at[2], total2, by_y)
        total1, final2 = tie((total1, final2))
        by_y, other2 = over_y(total1), over_core(final2)
        wup, wdown = deliver_second(at, final2, other2)
        by_y, wup, wdown = tie((by_y, wup, wdown))
        final1 = settle(at[2], total1, by_y)
        other1 = over_core(final1)
        wqkv, wout, *small = deliver_first(at, final1, other1, sizes)
    else:
        parts1 = grads(at, xp, g1, b1, o, da, dqkv, ())
        layer_out, input_grad = restore(plan, outp, dxp)
        wqkv, wout = map(reduce_rows, parts1)
        wup, wdown = map(reduce_rows, parts2)
        bias = bias_low + bias_high
        small = [sums1[0], sums1[1], bias[0], sums2[3], sums2[0], sums2[1], gbup[0], sums2[2]]
        small = [reduce_rows(v) for v in small]
    dg1, db1, dbqkv, dbout, dg2, db2, dbup, dbdown = small
    return (
        layer_out[None], input_grad[None], dg1, db1, wqkv, dbqkv, wout, dbout, dg2, db2,
        wup, dbup, wdown, dbdown,
    )


def solution(mesh):
    rows = ("fsdp", "replica")
    by_row = P(rows, None, None)
    vector, matrix = P("fsdp"), P("fsdp", None)
    params = (
        vector, vector, matrix, vector, matrix, vector, vector, vector, matrix, vector, matrix, vector,
    )
    in_specs = (by_row, by_row, P(rows, None), P(rows, None)) + params
    out_specs = (by_row, by_row) + params
    return jax.shard_map(
        functools.partial(body, tuned=tuned_mesh(mesh)),
        mesh=mesh, in_specs=in_specs, out_specs=out_specs, check_vma=False,
    )
```
